32 devices in a mesh: dp: 8 (over y, x, core), mp: 4 (over z).
Axes of the slice: x: 2, y: 2, z: 4, core: 2. Of those that a mesh axis runs over, the one named last changes fastest.
Arguments:
- tokens: bfloat16 [20480, 1024], P(('dp', 'mp')), may hold values from -6 to 6
- context: int32 [40], P('dp'), may hold values from 0 to 475, as said below
- timestep: int32 [40], P('dp'), may hold values from 1 to 5000
- time_weight: float32 [1024], replicated, may hold values from -6 to 6
- time_bias: float32 [1024], replicated, may hold values from -3 to 3
- qkv_weight: bfloat16 [3, 1024, 1024], P(None, 'dp', 'mp'), may hold values from -0.1875 to 0.1875
- qv_bias: bfloat16 [16, 128], P('mp', 'dp'), may hold values from -3 to 3
- out_weight: bfloat16 [1024, 1024], P('mp', 'dp'), may hold values from -1 to 1
- out_bias: float32 [1024], replicated, may hold values from -3 to 3
- gain_one: float32 [1024], replicated, may hold values from 0.5 to 1.5
- shift_one: float32 [1024], replicated, may hold values from -3 to 3
- up_weight: bfloat16 [4096, 1024], P('mp', 'dp'), may hold values from -0.1875 to 0.1875
- up_bias: bfloat16 [32, 128], P('mp', 'dp'), may hold values from -3 to 3
- down_weight: bfloat16 [4096, 1024], P('mp', 'dp'), may hold values from -0.09375 to 0.09375
- down_bias: float32 [1024], replicated, may hold values from -3 to 3
- gain_two: float32 [1024], replicated, may hold values from 0.5 to 1.5
- shift_two: float32 [1024], replicated, may hold values from -3 to 3
- cotangent: bfloat16 [20480, 1024], P(('dp', 'mp')), may hold values from -6 to 6
Outputs:
- layer_out: bfloat16 [20480, 1024], P(('dp', 'mp'))
- grad_tokens: float32 [20480, 1024], P(('dp', 'mp'))
- grad_time_weight: float32 [1024], P(('dp', 'mp'))
- grad_time_bias: float32 [1024], P(('dp', 'mp'))
- grad_qkv_weight: float32 [3, 1024, 1024], P(None, 'dp', 'mp')
- grad_qv_bias: float32 [16, 128], P('mp', 'dp')
- grad_out_weight: float32 [1024, 1024], P('mp', 'dp')
- grad_out_bias: float32 [1024], P(('dp', 'mp'))
- grad_gain_one: float32 [1024], P(('dp', 'mp'))
- grad_shift_one: float32 [1024], P(('dp', 'mp'))
- grad_up_weight: float32 [4096, 1024], P('mp', 'dp')
- grad_up_bias: float32 [32, 128], P('mp', 'dp')
- grad_down_weight: float32 [4096, 1024], P('mp', 'dp')
- grad_down_bias: float32 [1024], P(('dp', 'mp'))
- grad_gain_two: float32 [1024], P(('dp', 'mp'))
- grad_shift_two: float32 [1024], P(('dp', 'mp'))
The draws below stay inside these ranges and needn't reach their ends.
Inputs may be any that keep to these rules, and one draw needn't show every extreme that they name: Sequence b holds context[b] context tokens followed by 25 block tokens; its remaining positions are padding and are never attended to.
All inputs are finite; a program needn't handle non-finite values.
Results may differ from the reference program's by a relative error of at most 0.019.
Values may be sent and summed in bfloat16 or wider, within the bound.
A program may use at most 128 MiB of HBM per device.

```python
import math
import jax
import jax.numpy as jnp
from jax import lax

D = 1024
H = 16
HD = 64
FF = 4096
LEN = 512
BLOCK = 25
TSTEPS = 5000
SEQ_DEV = 5
CTX_MAX = 475
SEQS = 40
TOKENS = 20480
N_DP = 8


def draw_context(key, part):
    first_key, second_key = jax.random.split(jax.random.fold_in(key, 11))
    lengths = jax.random.randint(first_key, (SEQS,), 0, CTX_MAX + 1)
    chosen = jax.random.randint(second_key, (), 0, SEQS)
    lengths = lengths.at[chosen].set(CTX_MAX)
    lengths = lengths.at[(chosen + 1) % SEQS].set(0)
    return lengths.astype(jnp.int32)


def place_ends(result, stream_key, smallest, top_value):
    longest = result.shape.index(max(result.shape))
    spots = []
    for shift in (0, 1):
        where = [jax.random.randint(jax.random.fold_in(stream_key, axis), (), 0, length) for axis, length in enumerate(result.shape)]
        where[longest] = (where[longest] + shift) % result.shape[longest]
        spots.append(tuple(where))
    return result.at[spots[0]].set(smallest).at[spots[1]].set(top_value)


def steps_of(stream_key, dims, cuts, smallest, high):
    level, own = 1.0, jax.random.fold_in(stream_key, 6)
    for dim, parts in cuts:
        draws = jnp.exp(jax.random.uniform(jax.random.fold_in(own, dim), (parts,), jnp.float32, smallest / len(cuts), high / len(cuts)))
        level = level * jnp.repeat(draws, dims[dim] // parts).reshape([-1 if axis == dim else 1 for axis in range(len(dims))])
    return level


def normal_values(key, extent, width, bound, cuts=(), held_as=jnp.bfloat16):
    entries = jax.random.normal(key, extent, jnp.float32) * width
    if len(cuts) > 0:
        entries = steps_of(key, extent, cuts, -0.22, 0.18) * entries
    return jnp.clip(entries, min=-bound, max=bound).astype(held_as)


def setup_inputs(seed: int = 0) -> dict:
    splits = jax.random.split(jax.random.key(seed), 19)
    return {
        "tokens": normal_values(splits[0], (TOKENS, D), 1.0, 6.0, ((0, 32),)),
        "context": draw_context(jax.random.fold_in(splits[18], 71), 0),
        "timestep": place_ends(jax.random.randint(splits[2], (SEQS,), 1, TSTEPS + 1), jax.random.fold_in(splits[2], 1), 1, TSTEPS).astype(jnp.int32),
        "time_weight": normal_values(splits[3], (D,), 1.0, 6.0, (), jnp.float32),
        "time_bias": normal_values(splits[4], (D,), 0.5, 3.0, (), jnp.float32),
        "qkv_weight": normal_values(splits[5], (3, D, D), D ** -0.5, 0.1875, ((1, 8), (2, 4))),
        "qv_bias": normal_values(splits[6], (H, 2 * HD), 0.5, 3.0, ((0, 4), (1, 8))),
        "out_weight": normal_values(splits[7], (D, D), (D // 32) ** -0.5, 1.0, ((0, 4), (1, 8))),
        "out_bias": normal_values(splits[8], (D,), 0.5, 3.0, (), jnp.float32),
        "gain_one": jnp.clip(1.0 + 0.1 * jax.random.normal(splits[9], (D,), jnp.float32), 0.5, 1.5),
        "shift_one": normal_values(splits[10], (D,), 0.5, 3.0, (), jnp.float32),
        "up_weight": normal_values(splits[11], (FF, D), D ** -0.5, 0.1875, ((0, 4), (1, 8))),
        "up_bias": normal_values(splits[12], (FF // 128, 128), 0.5, 3.0, ((0, 4), (1, 8))),
        "down_weight": normal_values(splits[13], (FF, D), FF ** -0.5, 0.09375, ((0, 4), (1, 8))),
        "down_bias": normal_values(splits[14], (D,), 0.5, 3.0, (), jnp.float32),
        "gain_two": jnp.clip(1.0 + 0.1 * jax.random.normal(splits[15], (D,), jnp.float32), 0.5, 1.5),
        "shift_two": normal_values(splits[16], (D,), 0.5, 3.0, (), jnp.float32),
        "cotangent": normal_values(splits[17], (TOKENS, D), 1.0, 6.0, ((0, 32),)),
    }


LN_EPS = 1e-05
MASKED = -1e+30

@jax.custom_vjp
def low(v):
    return lax.optimization_barrier(v.astype(jnp.bfloat16)).astype(jnp.float32)

@jax.custom_vjp
def low_back(v):
    return v

def low_keep(v):
    return (low(v), None)

def low_pass(kept, grad):
    return (grad,)

def back_keep(v):
    return (v, None)

def back_low(kept, grad):
    return (low(grad),)
low.defvjp(low_keep, low_pass)
low_back.defvjp(back_keep, back_low)

def product_hi(left, right):
    return jnp.dot(left, right, precision=lax.Precision.HIGHEST)

def layer_norm(values_in, gain, shift):
    average = lax.optimization_barrier(jnp.mean(values_in, axis=-1, keepdims=True))
    centred = values_in - average
    variance = lax.optimization_barrier(jnp.mean(centred * centred, axis=-1, keepdims=True))
    return centred * lax.rsqrt(variance + LN_EPS) * gain + shift

def attend(queries, key_rows, values, live_len):
    scores = jnp.einsum('qhd,khd->hqk', queries, key_rows, precision=lax.Precision.HIGHEST)
    scores = low_back(scores * (1.0 / math.sqrt(HD)))
    usable = jnp.arange(key_rows.shape[0]) < live_len
    scores = jnp.where(usable[None, None, :], scores, MASKED)
    row_max = lax.optimization_barrier(jnp.max(scores, axis=-1, keepdims=True))
    expo_vals = jnp.exp(scores - row_max)
    probs = low(expo_vals / lax.optimization_barrier(jnp.sum(expo_vals, axis=-1, keepdims=True)))
    return jnp.einsum('hqk,khd->qhd', probs, values, precision=lax.Precision.HIGHEST)

def forward(token_rows, fraction, live_len, time_weight, time_bias, qkv_weight, qv_bias, out_weight, out_bias, gain_one, shift_one, up_weight, up_bias, down_weight, down_bias, gain_two, shift_two):
    h_zero = token_rows + fraction[:, None] * time_weight + time_bias
    h_low = low(h_zero)
    q_bias = qv_bias[:, :HD].reshape(D)
    v_bias = qv_bias[:, HD:].reshape(D)
    queries = low(low_back(product_hi(h_low, qkv_weight[0]) + q_bias))
    key_rows = low(low_back(product_hi(h_low, qkv_weight[1])))
    values = low(low_back(product_hi(h_low, qkv_weight[2]) + v_bias))

    def shaped(array):
        return array.reshape(SEQ_DEV, LEN, H, HD)
    mixed_heads = lax.map(jax.checkpoint(lambda record: attend(*record)), (shaped(queries), shaped(key_rows), shaped(values), live_len))
    mixed_heads = low(low_back(mixed_heads.reshape(SEQ_DEV * LEN, D)))
    branch_a = low_back(product_hi(mixed_heads, out_weight) + out_bias)
    y_one = layer_norm(h_zero + branch_a, gain_one, shift_one)
    pre_act = low_back(product_hi(low(y_one), up_weight.T) + up_bias.reshape(FF))
    hidden = low(jax.nn.gelu(pre_act, approximate=False))
    branch_f = low_back(product_hi(hidden, down_weight) + down_bias)
    return layer_norm(y_one + branch_f, gain_two, shift_two)

def reference(tokens, context, timestep, time_weight, time_bias, qkv_weight, qv_bias, out_weight, out_bias, gain_one, shift_one, up_weight, up_bias, down_weight, down_bias, gain_two, shift_two, cotangent):
    params = tuple((tensor.astype(jnp.float32) for tensor in (time_weight, time_bias, qkv_weight, qv_bias, out_weight, out_bias, gain_one, shift_one, up_weight, up_bias, down_weight, down_bias, gain_two, shift_two)))
    fraction = jnp.repeat(timestep.astype(jnp.float32) / TSTEPS, LEN).reshape(N_DP, SEQ_DEV * LEN)
    live_all = (context + BLOCK).astype(jnp.int32).reshape(N_DP, SEQ_DEV)
    token_groups = tokens.astype(jnp.float32).reshape(N_DP, SEQ_DEV * LEN, D)
    cot_groups = cotangent.astype(jnp.float32).reshape(N_DP, SEQ_DEV * LEN, D)

    def one_group(running, record):
        token_rows, frac_rows, live_len, cot_rows = record

        def local(rows_in, *weights):
            return forward(rows_in, frac_rows, live_len, *weights)
        out_rows, pullback = jax.vjp(local, token_rows, *params)
        gradients = pullback(cot_rows)
        running = tuple((kept + fresh for kept, fresh in zip(running, gradients[1:])))
        return (running, (out_rows, gradients[0]))
    initial = tuple((jnp.zeros(tensor.shape, jnp.float32) for tensor in params))
    totals, (out_groups, grad_groups) = lax.scan(one_group, initial, (token_groups, fraction, live_all, cot_groups))
    layer_out = out_groups.reshape(TOKENS, D).astype(jnp.bfloat16)
    grad_tokens = grad_groups.reshape(TOKENS, D)
    return (layer_out, grad_tokens, totals[0], totals[1], totals[2], totals[3], totals[4], totals[5], totals[6], totals[7], totals[8], totals[9], totals[10], totals[11], totals[12], totals[13])
```

```python
import functools
import math

import jax
import jax.numpy as jnp
from jax import lax
from jax.experimental import pallas as pl
from jax.experimental.pallas import tpu as pltpu
from jax.sharding import PartitionSpec as P

BLOCK = 25
TSTEPS = 5000
LN_EPS = 1e-05
MASKED = -1e30
MESH = pl.DeviceIdType.MESH
BF = jnp.bfloat16
F32 = jnp.float32
PIECES = 12
LANES = 4
VMEM_LIMIT = 62 * 2**20


def dot_nn(left, right):
    return lax.dot_general(left, right, (((1,), (0,)), ((), ())), preferred_element_type=F32)


def dot_nt(left, right):
    return lax.dot_general(left, right, (((1,), (1,)), ((), ())), preferred_element_type=F32)


def dot_tn(left, right):
    return lax.dot_general(left, right, (((0,), (0,)), ((), ())), preferred_element_type=F32)


class Place:
    def __init__(self, outer):
        dp = lax.axis_index("dp")
        self.z = lax.axis_index("mp")
        self.outer = outer
        self.own = lax.div(dp, outer)
        self.rest = lax.rem(dp, outer)
        self.core = lax.rem(self.own, 2)
        self.chip = lax.div(self.own, 2)
        col, row = lax.rem(self.chip, 2), lax.div(self.chip, 2)
        self.side = row * 2 + (1 - col)
        self.over = (1 - row) * 2 + col
        self.diag = (1 - row) * 2 + (1 - col)

    def dev(self, chip, core, z):
        return ((chip * 2 + core) * self.outer + self.rest, z)

    def partner(self):
        return self.dev(self.chip, 1 - self.core, self.z)

    def beside(self):
        return self.dev(self.side, self.core, self.z)

    def across(self):
        return self.dev(self.over, self.core, self.z)

    def along(self, k):
        return self.dev(self.chip, self.core, lax.rem(self.z + k, 4))


def greet(at):
    barrier = pltpu.get_barrier_semaphore()
    peers = [at.partner(), at.beside(), at.across()] + [at.along(k) for k in range(1, 4)]
    for peer in peers:
        pl.semaphore_signal(barrier, inc=1, device_id=peer, device_id_type=MESH)
    pl.semaphore_wait(barrier, len(peers))


def wait_for(ref, sem):
    pltpu.make_async_copy(ref, ref, sem).wait()


def send(src, dst, send_sem, recv_sem, device):
    pltpu.make_async_remote_copy(
        src, dst, send_sem, recv_sem, device_id=device, device_id_type=MESH
    ).start()


def when_in(piece, count, action):
    @pl.when(jnp.logical_and(piece >= 0, piece < count))
    def _():
        action(piece)


def gather_kernel(outer, shard, full, own_sem, sent, got_z, got_x, got_y, got_xd, got_yd, got_c):
    at = Place(outer)
    greet(at)
    mine = pltpu.make_async_copy(shard, full.at[:, at.own, at.z], own_sem)
    mine.start()
    x_lane, y_lane, d_lane = at.side * 2 + at.core, at.over * 2 + at.core, at.diag * 2 + at.core

    def first(p):
        src, dst = shard.at[p], full.at[p, at.own, at.z]
        send(src, dst, sent.at[p], got_x.at[p], at.beside())
        send(src, dst, sent.at[p], got_y.at[p], at.across())
        for k in range(1, 4):
            send(src, dst, sent.at[p], got_z.at[p], at.along(k))
        send(src, dst, sent.at[p], got_c.at[p], at.partner())

    def second(p):
        wait_for(full.at[p, at.own, 0:3], got_z.at[p])
        for k in range(1, 4):
            block = full.at[p, at.own, lax.rem(at.z + k, 4)]
            send(block, block, sent.at[p], got_x.at[p], at.beside())
            send(block, block, sent.at[p], got_y.at[p], at.across())
            send(block, block, sent.at[p], got_c.at[p], at.partner())

    def third(p):
        wait_for(full.at[p, x_lane], got_x.at[p])
        block = full.at[p, x_lane, 0:2]
        send(block, block, sent.at[p], got_yd.at[p], at.across())
        block = full.at[p, x_lane]
        send(block, block, sent.at[p], got_c.at[p], at.partner())
        wait_for(full.at[p, y_lane], got_y.at[p])
        block = full.at[p, y_lane, 2:4]
        send(block, block, sent.at[p], got_xd.at[p], at.beside())
        block = full.at[p, y_lane]
        send(block, block, sent.at[p], got_c.at[p], at.partner())

    def fourth(p):
        wait_for(full.at[p, d_lane, 0:2], got_yd.at[p])
        wait_for(full.at[p, d_lane, 2:4], got_xd.at[p])
        block = full.at[p, d_lane]
        send(block, block, sent.at[p], got_c.at[p], at.partner())

    def fifth(p):
        wait_for(full.at[p, 0:4], got_c.at[p])

    first(0)
    first(1)

    def tick(t, carry):
        for action, shift in ((first, 2), (second, 0), (third, -1), (fourth, -2), (fifth, -3)):
            when_in(t + shift, PIECES, action)
        return carry

    lax.fori_loop(0, PIECES + 3, tick, 0)
    mine.wait()

    def drain(p, carry):
        wait_for(full.at[p, 0:7], sent.at[p])
        wait_for(full.at[p, 7, 0:3], sent.at[p])
        return carry

    lax.fori_loop(0, PIECES, drain, 0)


def gather_weights(outer, shard):
    sem = pltpu.SemaphoreType.DMA
    return pl.pallas_call(
        functools.partial(gather_kernel, outer),
        out_shape=jax.ShapeDtypeStruct((PIECES, 8, 4) + shard.shape[1:], BF),
        in_specs=[pl.BlockSpec(memory_space=pl.ANY)],
        out_specs=pl.BlockSpec(memory_space=pl.ANY),
        scratch_shapes=[sem] + [sem((PIECES,))] * 7,
        compiler_params=pltpu.CompilerParams(
            collective_id=1, has_side_effects=True, vmem_limit_bytes=VMEM_LIMIT
        ),
    )(shard)


def scatter_kernel(
    outer, grads, out, part, lane, got_c, got_dx, got_dy, got_x, got_y, got_z,
    load_sem, sent0, sent1, sent2, sent3, sem_c, sem_dx, sem_dy, sem_x, sem_y, sem_z, credit,
):
    at = Place(outer)
    greet(at)

    def load(p):
        return pltpu.make_async_copy(grads.at[p], part.at[lax.rem(p, 2)], load_sem.at[lax.rem(p, 2)])

    def first(p):
        slot = lax.rem(p, 2)
        load(p).wait()

        @pl.when(p >= 2)
        def _():
            pl.semaphore_wait(credit, 1)

        send(part.at[slot, :, 1 - at.core], got_c.at[slot], sent0.at[p], sem_c.at[p], at.partner())

    def second(p):
        slot, row = lax.rem(p, 2), lax.rem(p, LANES)
        wait_for(got_c.at[slot], sem_c.at[p])

        @pl.when(p >= LANES)
        def _():
            wait_for(lane.at[row, 0], sent1.at[p - LANES])
            wait_for(lane.at[row, 0:2], sent2.at[p - LANES])
            wait_for(lane.at[row, 0, 0:3], sent3.at[p - LANES])

        def add(i, carry):
            a, b = lax.div(i, 4), lax.rem(i, 4)
            lane[row, a, b] = part[slot, a, at.core, b] + got_c[slot, a, b]
            return carry

        lax.fori_loop(0, 16, add, 0)

        @pl.when(p < PIECES - 2)
        def _():
            pl.semaphore_signal(credit, inc=1, device_id=at.partner(), device_id_type=MESH)

        wait_for(got_c.at[slot], sent0.at[p])

        @pl.when(p + 2 < PIECES)
        def _():
            load(p + 2).start()

        send(lane.at[row, at.diag, 0:2], got_dy.at[p], sent1.at[p], sem_dy.at[p], at.across())
        send(lane.at[row, at.diag, 2:4], got_dx.at[p], sent1.at[p], sem_dx.at[p], at.beside())

    def third(p):
        row = lax.rem(p, LANES)
        wait_for(got_dy.at[p], sem_dy.at[p])

        def add_y(i, carry):
            lane[row, at.side, i] = lane[row, at.side, i] + got_dy[p, i]
            return carry

        lax.fori_loop(0, 2, add_y, 0)
        send(lane.at[row, at.side], got_x.at[p], sent2.at[p], sem_x.at[p], at.beside())
        wait_for(got_dx.at[p], sem_dx.at[p])

        def add_x(i, carry):
            lane[row, at.over, i + 2] = lane[row, at.over, i + 2] + got_dx[p, i]
            return carry

        lax.fori_loop(0, 2, add_x, 0)
        send(lane.at[row, at.over], got_y.at[p], sent2.at[p], sem_y.at[p], at.across())

    def fourth(p):
        row = lax.rem(p, LANES)
        wait_for(got_x.at[p], sem_x.at[p])
        wait_for(got_y.at[p], sem_y.at[p])

        def add(i, carry):
            total = lane[row, at.chip, i].astype(F32) + got_x[p, i].astype(F32)
            lane[row, at.chip, i] = (total + got_y[p, i].astype(F32)).astype(BF)
            return carry

        lax.fori_loop(0, 4, add, 0)
        for k in range(1, 4):
            block = lane.at[row, at.chip, lax.rem(at.z + k, 4)]
            send(block, got_z.at[p, k - 1], sent3.at[p], sem_z.at[p], at.along(k))

    def fifth(p):
        row = lax.rem(p, LANES)
        wait_for(got_z.at[p], sem_z.at[p])
        total = lane[row, at.chip, at.z].astype(F32)
        for k in range(3):
            total = total + got_z[p, k].astype(F32)
        out[p] = total

    load(0).start()
    load(1).start()

    def tick(t, carry):
        for action, shift in ((first, 0), (second, -1), (third, -2), (fourth, -3), (fifth, -4)):
            when_in(t + shift, PIECES, action)
        return carry

    lax.fori_loop(0, PIECES + 4, tick, 0)
    for p in range(PIECES - LANES, PIECES):
        row = p % LANES
        wait_for(lane.at[row, 0], sent1.at[p])
        wait_for(lane.at[row, 0:2], sent2.at[p])
        wait_for(lane.at[row, 0, 0:3], sent3.at[p])


def scatter_grads(outer, grads):
    sem = pltpu.SemaphoreType.DMA
    rows, cols = grads.shape[-2:]
    return pl.pallas_call(
        functools.partial(scatter_kernel, outer),
        out_shape=jax.ShapeDtypeStruct((PIECES, rows, cols), F32),
        in_specs=[pl.BlockSpec(memory_space=pl.ANY)],
        out_specs=pl.BlockSpec(memory_space=pltpu.VMEM),
        scratch_shapes=[
            pltpu.VMEM((2, 4, 2, 4, rows, cols), BF),
            pltpu.VMEM((LANES, 4, 4, rows, cols), BF),
            pltpu.VMEM((2, 4, 4, rows, cols), BF),
            pltpu.VMEM((PIECES, 2, rows, cols), BF),
            pltpu.VMEM((PIECES, 2, rows, cols), BF),
            pltpu.VMEM((PIECES, 4, rows, cols), BF),
            pltpu.VMEM((PIECES, 4, rows, cols), BF),
            pltpu.VMEM((PIECES, 3, rows, cols), BF),
            sem((2,)),
        ]
        + [sem((PIECES,))] * 10
        + [pltpu.SemaphoreType.REGULAR],
        compiler_params=pltpu.CompilerParams(
            collective_id=2, has_side_effects=True, vmem_limit_bytes=VMEM_LIMIT
        ),
    )(grads)


def layer_norm(values_in, gain, shift):
    average = jnp.mean(values_in, axis=-1, keepdims=True)
    centred = values_in - average
    variance = jnp.mean(centred * centred, axis=-1, keepdims=True)
    return centred * lax.rsqrt(variance + LN_EPS) * gain + shift


def gelu_exact(values_in):
    return jax.nn.gelu(values_in, approximate=False)


def probs_of(record):
    queries, key_rows, values, usable = record
    scores = jnp.einsum("qhd,khd->hqk", queries, key_rows, preferred_element_type=F32)
    scores = scores * (1.0 / math.sqrt(queries.shape[-1]))
    scores = jnp.where(usable[None], scores, MASKED)
    row_max = jnp.max(scores, axis=-1, keepdims=True)
    expo = jnp.exp(scores - row_max)
    return expo / jnp.sum(expo, axis=-1, keepdims=True)


def attend(record):
    probs = probs_of(record)
    mixed = jnp.einsum("hqk,khd->qhd", probs.astype(BF), record[2], preferred_element_type=F32)
    return mixed.astype(BF)


def attend_back(record):
    queries, key_rows, values, usable, grad_out = record
    probs = probs_of(record[:4])
    scale = 1.0 / math.sqrt(queries.shape[-1])
    grad_v = jnp.einsum("hqk,qhd->khd", probs.astype(BF), grad_out, preferred_element_type=F32)
    grad_p = jnp.einsum("qhd,khd->hqk", grad_out, values, preferred_element_type=F32)
    inner = jnp.sum(probs * grad_p, axis=-1, keepdims=True)
    grad_s = (probs * (grad_p - inner)).astype(BF)
    grad_q = jnp.einsum("hqk,khd->qhd", grad_s, key_rows, preferred_element_type=F32) * scale
    grad_k = jnp.einsum("hqk,qhd->khd", grad_s, queries, preferred_element_type=F32) * scale
    return grad_q.astype(BF), grad_k, grad_v


def body(
    outer, tokens, context, timestep, time_weight, time_bias, qkv_weight, qv_bias, out_weight, out_bias,
    gain_one, shift_one, up_weight, up_bias, down_weight, down_bias, gain_two, shift_two, cotangent,
):
    z = lax.axis_index("mp")
    rows, model = tokens.shape
    seqs = context.shape[0]
    seq_len = rows * 4 // seqs
    dp_size = lax.axis_size("dp")
    groups = None
    if outer > 1:
        groups = [[i * outer + j for j in range(outer)] for i in range(8)]
        qkv_weight, out_weight, up_weight, down_weight = (
            lax.all_gather(w, "dp", axis=1, tiled=True, axis_index_groups=groups)
            for w in (qkv_weight, out_weight, up_weight, down_weight)
        )
    shard = jnp.concatenate(
        [
            qkv_weight.reshape(3, -1, 2, 128).transpose(0, 2, 1, 3).reshape(3, 256, 128),
            out_weight.reshape(1, 256, 128),
            up_weight.reshape(4, 256, 128),
            down_weight.reshape(4, 256, 128),
        ]
    )
    full = gather_weights(outer, shard)
    w_qkv = full[0:3].reshape(3, 8, 4, 2, 128, 128).transpose(0, 1, 4, 2, 3, 5).reshape(3, model, model)
    w_out = full[3].transpose(1, 2, 0, 3).reshape(model, model)
    w_up = full[4:8].transpose(2, 0, 3, 1, 4).reshape(4 * model, model)
    w_down = full[8:12].transpose(2, 0, 3, 1, 4).reshape(4 * model, model)
    qv_bias = lax.all_gather(lax.all_gather(qv_bias, "dp", axis=1, tiled=True), "mp", axis=0, tiled=True)
    up_bias_all = lax.all_gather(lax.all_gather(up_bias, "dp", axis=1, tiled=True), "mp", axis=0, tiled=True)
    heads, head = qv_bias.shape[0], qv_bias.shape[1] // 2
    row_ids = z * rows + jnp.arange(rows, dtype=jnp.int32)
    owner = (row_ids // seq_len)[:, None] == jnp.arange(seqs, dtype=jnp.int32)[None, :]
    fraction = jnp.sum(jnp.where(owner, (timestep.astype(F32) / TSTEPS)[None, :], 0.0), axis=1)
    h_zero = tokens.astype(F32) + fraction[:, None] * time_weight + time_bias
    h_low = h_zero.astype(BF)
    h_all = lax.all_gather(h_low, "mp", axis=0, tiled=True)
    h_win = lax.dynamic_slice(h_all, (z * seq_len, 0), (2 * seq_len, model))
    bias_f = qv_bias.astype(F32)
    queries = (jnp.dot(h_low, w_qkv[0], preferred_element_type=F32) + bias_f[:, :head].reshape(-1)).astype(BF)
    keys = jnp.dot(h_win, w_qkv[1], preferred_element_type=F32).astype(BF)
    values = (jnp.dot(h_win, w_qkv[2], preferred_element_type=F32) + bias_f[:, head:].reshape(-1)).astype(BF)
    step = rows // 5
    live = context + BLOCK
    live_two = lax.dynamic_slice(live, (z,), (2,))
    q_blocks = queries.reshape(5, step, heads, head)
    slots = (z + jnp.arange(5)) // 4
    k_two, v_two = keys.reshape(2, seq_len, heads, head), values.reshape(2, seq_len, heads, head)

    def record_of(j):
        slot = slots[j]
        usable = jnp.broadcast_to(jnp.arange(seq_len)[None, :] < live_two[slot], (step, seq_len))
        return q_blocks[j], k_two[slot], v_two[slot], usable

    attn = lax.map(lambda j: attend(record_of(j)), jnp.arange(5)).reshape(rows, model)
    branch_a = jnp.dot(attn, w_out, preferred_element_type=F32) + out_bias
    y_one, ln_one_back = jax.vjp(layer_norm, h_zero + branch_a, gain_one, shift_one)
    y_low = y_one.astype(BF)
    pre = dot_nt(y_low, w_up) + up_bias_all.reshape(-1).astype(F32)
    hidden, gelu_back = jax.vjp(gelu_exact, pre)
    hidden_low = hidden.astype(BF)
    branch_f = jnp.dot(hidden_low, w_down, preferred_element_type=F32) + down_bias
    y_two, ln_two_back = jax.vjp(layer_norm, y_one + branch_f, gain_two, shift_two)
    layer_out = y_two.astype(BF)
    grad_z2, grad_gain_two, grad_shift_two = ln_two_back(cotangent.astype(F32))
    grad_f = grad_z2.astype(BF)
    grad_down_bias = jnp.sum(grad_f.astype(F32), axis=0)
    (grad_pre,) = gelu_back(dot_nt(grad_f, w_down))
    grad_pre = grad_pre.astype(BF)
    grad_up = dot_tn(grad_pre, y_low).astype(BF)
    grad_down = dot_tn(hidden_low, grad_f).astype(BF)
    grad_up_bias = jnp.sum(grad_pre.astype(F32), axis=0).reshape(up_bias_all.shape)
    grad_y1 = grad_z2 + jnp.dot(grad_pre, w_up, preferred_element_type=F32)
    grad_z1, grad_gain_one, grad_shift_one = ln_one_back(grad_y1)
    grad_a = grad_z1.astype(BF)
    grad_out_bias = jnp.sum(grad_a.astype(F32), axis=0)
    grad_attn = dot_nt(grad_a, w_out).astype(BF)
    grad_out_w = dot_tn(attn, grad_a).astype(BF)
    ga = grad_attn.reshape(5, step, heads, head)

    def back(carry, j):
        dk, dv = carry
        slot = slots[j]
        dq, dk_j, dv_j = attend_back(record_of(j) + (ga[j],))
        return (dk.at[slot].add(dk_j), dv.at[slot].add(dv_j)), dq

    zero = jnp.zeros((2, seq_len, heads, head), F32)
    (dk, dv), dq = lax.scan(back, (zero, zero), jnp.arange(5))
    dq = dq.reshape(rows, model)
    dk, dv = dk.astype(BF).reshape(-1, model), dv.astype(BF).reshape(-1, model)
    grad_qkv = jnp.stack([dot_tn(h_low, dq), dot_tn(h_win, dk), dot_tn(h_win, dv)]).astype(BF)
    grad_qv_bias = jnp.concatenate(
        [
            jnp.sum(dq.astype(F32), axis=0).reshape(heads, head),
            jnp.sum(dv.astype(F32), axis=0).reshape(heads, head),
        ],
        axis=1,
    )
    dh_win = dot_nt(dk, w_qkv[1]) + dot_nt(dv, w_qkv[2])
    dh_all = lax.dynamic_update_slice(jnp.zeros((4 * rows, model), F32), dh_win, (z * seq_len, 0))
    grad_tokens = (
        grad_z1
        + dot_nt(dq, w_qkv[0])
        + lax.psum_scatter(dh_all.astype(BF), "mp", scatter_dimension=0, tiled=True).astype(F32)
    )
    grad_time_weight = jnp.sum(fraction[:, None] * grad_tokens, axis=0)
    grad_time_bias = jnp.sum(grad_tokens, axis=0)
    parts = jnp.concatenate(
        [
            grad_qkv.reshape(3, 8, 128, 4, 2, 128).transpose(0, 1, 3, 4, 2, 5).reshape(3, 8, 4, 256, 128),
            grad_out_w.reshape(1, 4, 256, 8, 128).transpose(0, 3, 1, 2, 4),
            grad_up.reshape(4, 4, 256, 8, 128).transpose(1, 3, 0, 2, 4),
            grad_down.reshape(4, 4, 256, 8, 128).transpose(1, 3, 0, 2, 4),
        ]
    )
    done = scatter_grads(outer, parts.reshape(PIECES, 4, 2, 4, 256, 128))
    weight_grads = (
        done[0:3].reshape(3, 2, 128, 128).transpose(0, 2, 1, 3).reshape(3, 128, 256),
        done[3],
        done[4:8].reshape(1024, 128),
        done[8:12].reshape(1024, 128),
    )
    if outer > 1:
        weight_grads = tuple(
            lax.psum_scatter(g, "dp", scatter_dimension=1, tiled=True, axis_index_groups=groups)
            for g in weight_grads
        )
    grad_qkv, grad_out_w, grad_up, grad_down = weight_grads
    small = [
        lax.psum_scatter(v, ("dp", "mp"), scatter_dimension=0, tiled=True)
        for v in (
            grad_out_bias, grad_gain_one, grad_shift_one, grad_gain_two, grad_shift_two, grad_down_bias,
            grad_time_weight, grad_time_bias,
        )
    ]
    grad_qv_bias = lax.psum(grad_qv_bias, ("dp", "mp"))
    grad_up_bias = lax.psum(grad_up_bias, ("dp", "mp"))
    dp = lax.axis_index("dp")
    grad_qv_bias = lax.dynamic_slice(
        grad_qv_bias, (z * (heads // 4), dp * (2 * head // dp_size)), (heads // 4, 2 * head // dp_size)
    )
    n_up, w_upb = up_bias_all.shape
    grad_up_bias = lax.dynamic_slice(
        grad_up_bias, (z * (n_up // 4), dp * (w_upb // dp_size)), (n_up // 4, w_upb // dp_size)
    )
    return (
        layer_out, grad_tokens, small[6], small[7], grad_qkv, grad_qv_bias,
        grad_out_w, small[0], small[1], small[2], grad_up, grad_up_bias,
        grad_down, small[5], small[3], small[4],
    )


def solution(mesh):
    outer = mesh.shape["dp"] // 8
    placed = (
        P(("dp", "mp"), None), P("dp"), P("dp"), P(), P(), P(None, "dp", "mp"), P("mp", "dp"), P("mp", "dp"),
        P(), P(), P(), P("mp", "dp"), P("mp", "dp"), P("mp", "dp"), P(), P(), P(), P(("dp", "mp"), None),
    )
    spread = P(("dp", "mp"))
    wide = P("mp", "dp")
    return jax.shard_map(
        functools.partial(body, outer),
        mesh=mesh,
        in_specs=placed,
        out_specs=(
            P(("dp", "mp"), None), P(("dp", "mp"), None), spread, spread, P(None, "dp", "mp"), wide, wide,
            spread, spread, spread, wide, wide, wide, spread, spread, spread,
        ),
        check_vma=False,
    )
```

```python
import functools

import jax
import jax.numpy as jnp
from jax import lax
from jax.experimental import pallas as pl
from jax.experimental.pallas import tpu as pltpu
from jax.sharding import PartitionSpec as P

BLOCK = 25
TSTEPS = 5000
LN_EPS = 1e-05
MASKED = -1e30
MESH = pl.DeviceIdType.MESH
BF = jnp.bfloat16
F32 = jnp.float32
PIECES = 12
LANES = 4
ROWS = 256
COLS = 128
VMEM_LIMIT = 62 * 2**20


def dot_nn(left, right):
    return lax.dot_general(left, right, (((1,), (0,)), ((), ())), preferred_element_type=F32)


def dot_nt(left, right):
    return lax.dot_general(left, right, (((1,), (1,)), ((), ())), preferred_element_type=F32)


def dot_tn(left, right):
    return lax.dot_general(left, right, (((0,), (0,)), ((), ())), preferred_element_type=F32)


class Place:
    def __init__(self, outer):
        dp = lax.axis_index("dp")
        self.z = lax.axis_index("mp")
        self.outer = outer
        self.own = lax.div(dp, outer)
        self.rest = lax.rem(dp, outer)
        self.core = lax.rem(self.own, 2)
        self.chip = lax.div(self.own, 2)
        col, row = lax.rem(self.chip, 2), lax.div(self.chip, 2)
        self.side = row * 2 + (1 - col)
        self.over = (1 - row) * 2 + col
        self.diag = (1 - row) * 2 + (1 - col)

    def dev(self, chip, core, z):
        return ((chip * 2 + core) * self.outer + self.rest, z)

    def partner(self):
        return self.dev(self.chip, 1 - self.core, self.z)

    def beside(self):
        return self.dev(self.side, self.core, self.z)

    def across(self):
        return self.dev(self.over, self.core, self.z)

    def along(self, k):
        return self.dev(self.chip, self.core, lax.rem(self.z + k, 4))


def greet(at):
    barrier = pltpu.get_barrier_semaphore()
    peers = [at.partner(), at.beside(), at.across()] + [at.along(k) for k in range(1, 4)]
    for peer in peers:
        pl.semaphore_signal(barrier, inc=1, device_id=peer, device_id_type=MESH)
    pl.semaphore_wait(barrier, len(peers))


def wait_for(ref, sem):
    pltpu.make_async_copy(ref, ref, sem).wait()


def send(src, dst, send_sem, recv_sem, device):
    pltpu.make_async_remote_copy(
        src, dst, send_sem, recv_sem, device_id=device, device_id_type=MESH
    ).start()


def when_in(piece, count, action):
    @pl.when(jnp.logical_and(piece >= 0, piece < count))
    def _():
        action(piece)


def cols_of(lane):
    return pl.ds(pl.multiple_of(lane * COLS, COLS), COLS)


def tile_rows(start, size):
    return pl.ds(pl.multiple_of(start, 128), size)


def gather_kernel(
    outer, shard, small, h, full, small_full, h_win,
    own_sem, sent, got_z, got_x, got_y, got_xd, got_yd, got_c, halo_sent, halo_got,
):
    at = Place(outer)
    greet(at)
    z, step = at.z, h.shape[0] // 5
    mine = [
        pltpu.make_async_copy(shard, full.at[:, z, :, cols_of(at.own)], own_sem.at[0]),
        pltpu.make_async_copy(small, small_full.at[pl.ds(z, 1), :, cols_of(at.own)], own_sem.at[1]),
        pltpu.make_async_copy(h, h_win.at[tile_rows(z * step, 5 * step)], own_sem.at[2]),
    ]
    x_lane, y_lane, d_lane = at.side * 2 + at.core, at.over * 2 + at.core, at.diag * 2 + at.core

    def source(p):
        return small if p is None else shard.at[pl.ds(p, 1)]

    def block(p, lane, start, count):
        ref = small_full if p is None else full.at[p]
        return ref.at[pl.ds(start, count), :, cols_of(lane)]

    def index(p):
        return PIECES if p is None else p

    def first(p):
        i, src, dst = index(p), source(p), block(p, at.own, z, 1)
        send(src, dst, sent.at[i], got_x.at[i], at.beside())
        send(src, dst, sent.at[i], got_y.at[i], at.across())
        for k in range(1, 4):
            send(src, dst, sent.at[i], got_z.at[i], at.along(k))
        send(src, dst, sent.at[i], got_c.at[i], at.partner())

    def second(p):
        i = index(p)
        wait_for(block(p, at.own, 0, 3), got_z.at[i])
        for k in range(1, 4):
            ref = block(p, at.own, lax.rem(z + k, 4), 1)
            send(ref, ref, sent.at[i], got_x.at[i], at.beside())
            send(ref, ref, sent.at[i], got_y.at[i], at.across())
            send(ref, ref, sent.at[i], got_c.at[i], at.partner())

    def third(p):
        i = index(p)
        wait_for(block(p, x_lane, 0, 4), got_x.at[i])
        ref = block(p, x_lane, 0, 2)
        send(ref, ref, sent.at[i], got_yd.at[i], at.across())
        ref = block(p, x_lane, 0, 4)
        send(ref, ref, sent.at[i], got_c.at[i], at.partner())
        wait_for(block(p, y_lane, 0, 4), got_y.at[i])
        ref = block(p, y_lane, 2, 2)
        send(ref, ref, sent.at[i], got_xd.at[i], at.beside())
        ref = block(p, y_lane, 0, 4)
        send(ref, ref, sent.at[i], got_c.at[i], at.partner())

    def fourth(p):
        i = index(p)
        wait_for(block(p, d_lane, 0, 2), got_yd.at[i])
        wait_for(block(p, d_lane, 2, 2), got_xd.at[i])
        ref = block(p, d_lane, 0, 4)
        send(ref, ref, sent.at[i], got_c.at[i], at.partner())

    def fifth(p):
        ref = small_full if p is None else full.at[p]
        wait_for(ref.at[:, :, 0 : 4 * COLS], got_c.at[index(p)])

    def drain(p):
        ref = small_full if p is None else full.at[p]
        wait_for(ref.at[:, :, 0 : 7 * COLS], sent.at[index(p)])
        wait_for(ref.at[0:3, :, 0:COLS], sent.at[index(p)])

    def halo():
        for i in range(3):
            @pl.when(jnp.logical_and(z >= 1, z < 4 - i))
            def _():
                dst = h_win.at[tile_rows((4 + z + i) * step, step)]
                send(h.at[tile_rows(i * step, step)], dst, halo_sent, halo_got, at.along(3))

            @pl.when(jnp.logical_and(z <= 2, z >= i))
            def _():
                dst = h_win.at[tile_rows(i * step, step)]
                send(h.at[tile_rows((4 - z + i) * step, step)], dst, halo_sent, halo_got, at.along(1))

    first(None)
    first(0)
    first(1)
    halo()
    for copy in mine:
        copy.start()
    stages = ((second, 0), (third, -1), (fourth, -2), (fifth, -3))

    def tick(t, carry):
        for action, shift in ((first, 2),) + stages:
            when_in(t + shift, PIECES, action)
        for action, shift in stages:
            @pl.when(t == -shift)
            def _():
                action(None)
        return carry

    lax.fori_loop(0, PIECES + 3, tick, 0)
    for copy in mine:
        copy.wait()
    wait_for(h_win.at[0 : 3 * step], halo_got)
    middle = jnp.logical_and(z >= 1, z <= 2)

    @pl.when(middle)
    def _():
        wait_for(h_win.at[0 : 5 * step], halo_sent)

    @pl.when(jnp.logical_not(middle))
    def _():
        wait_for(h_win.at[0:step], halo_sent)

    def drain_one(p, carry):
        drain(p)
        return carry

    lax.fori_loop(0, PIECES, drain_one, 0)
    drain(None)


def gather_weights(outer, shard, small, h):
    sem = pltpu.SemaphoreType.DMA
    step = h.shape[0] // 5
    return pl.pallas_call(
        functools.partial(gather_kernel, outer),
        out_shape=(
            jax.ShapeDtypeStruct((PIECES, 4, ROWS, 8 * COLS), BF),
            jax.ShapeDtypeStruct((4, 16, 8 * COLS), BF),
            jax.ShapeDtypeStruct((8 * step, h.shape[1]), BF),
        ),
        in_specs=[pl.BlockSpec(memory_space=pltpu.VMEM)] * 3,
        out_specs=[pl.BlockSpec(memory_space=pl.ANY)] * 3,
        scratch_shapes=[sem((3,))] + [sem((PIECES + 1,))] * 7 + [sem, sem],
        compiler_params=pltpu.CompilerParams(
            collective_id=1, has_side_effects=True, vmem_limit_bytes=VMEM_LIMIT
        ),
        name="gather",
    )(shard, small, h)


def scatter_kernel(
    outer, g_q, g_k, g_v, g_out, g_up, g_down, small, dh_win, out, small_out, halo_in,
    part, lane, got_c, got_dx, got_dy, got_x, got_y, got_z,
    s_part, s_lane, s_c, s_dx, s_dy, s_x, s_y, s_z,
    load_sem, sent0, sent1, sent2, sent3, sem_c, sem_dx, sem_dy, sem_x, sem_y, sem_z,
    halo_sent, halo_got, credit,
):
    at = Place(outer)
    greet(at)
    z, step = at.z, dh_win.shape[0] // 8
    singles = [(8, g_q), (9, g_k), (10, g_v), (11, g_out)]

    def load(p, action):
        slot = lax.rem(p, 2)

        def go(src):
            copy = pltpu.make_async_copy(src, part.at[slot], load_sem.at[slot])
            copy.start() if action == 0 else copy.wait()

        if action == 1:
            go(g_up.at[0])
            return

        @pl.when(p < 4)
        def _():
            go(g_down.at[p])

        @pl.when(jnp.logical_and(p >= 4, p < 8))
        def _():
            go(g_up.at[lax.rem(p, 4)])

        for i, ref in singles:
            @pl.when(p == i)
            def _():
                go(ref)

    def first(p):
        slot = lax.rem(p, 2)
        load(p, 1)

        @pl.when(p >= 2)
        def _():
            pl.semaphore_wait(credit, 1)

        for a in range(4):
            src = part.at[slot, :, :, cols_of(a * 2 + 1 - at.core)]
            send(src, got_c.at[slot, a], sent0.at[p], sem_c.at[p], at.partner())

    def second(p):
        slot, row = lax.rem(p, 2), lax.rem(p, LANES)
        wait_for(got_c.at[slot], sem_c.at[p])

        @pl.when(p >= LANES)
        def _():
            wait_for(lane.at[row, 0], sent1.at[p - LANES])
            wait_for(lane.at[row, 0:2], sent2.at[p - LANES])
            wait_for(lane.at[row, 0, 0:3], sent3.at[p - LANES])

        def add(i, carry):
            a, b = lax.div(i, 4), lax.rem(i, 4)
            lane[row, a, b] = part[slot, b, :, cols_of(a * 2 + at.core)] + got_c[slot, a, b]
            return carry

        lax.fori_loop(0, 16, add, 0)

        @pl.when(p < PIECES - 2)
        def _():
            pl.semaphore_signal(credit, inc=1, device_id=at.partner(), device_id_type=MESH)

        wait_for(got_c.at[slot], sent0.at[p])

        @pl.when(p + 2 < PIECES)
        def _():
            load(p + 2, 0)

        send(lane.at[row, at.diag, 0:2], got_dy.at[p], sent1.at[p], sem_dy.at[p], at.across())
        send(lane.at[row, at.diag, 2:4], got_dx.at[p], sent1.at[p], sem_dx.at[p], at.beside())

    def third(p):
        row = lax.rem(p, LANES)
        wait_for(got_dy.at[p], sem_dy.at[p])

        def add_y(i, carry):
            lane[row, at.side, i] = lane[row, at.side, i] + got_dy[p, i]
            return carry

        lax.fori_loop(0, 2, add_y, 0)
        send(lane.at[row, at.side], got_x.at[p], sent2.at[p], sem_x.at[p], at.beside())
        wait_for(got_dx.at[p], sem_dx.at[p])

        def add_x(i, carry):
            lane[row, at.over, i + 2] = lane[row, at.over, i + 2] + got_dx[p, i]
            return carry

        lax.fori_loop(0, 2, add_x, 0)
        send(lane.at[row, at.over], got_y.at[p], sent2.at[p], sem_y.at[p], at.across())

    def fourth(p):
        row = lax.rem(p, LANES)
        wait_for(got_x.at[p], sem_x.at[p])
        wait_for(got_y.at[p], sem_y.at[p])

        def add(i, carry):
            total = lane[row, at.chip, i].astype(F32) + got_x[p, i].astype(F32)
            lane[row, at.chip, i] = (total + got_y[p, i].astype(F32)).astype(BF)
            return carry

        lax.fori_loop(0, 4, add, 0)
        for k in range(1, 4):
            block = lane.at[row, at.chip, lax.rem(z + k, 4)]
            send(block, got_z.at[p, k - 1], sent3.at[p], sem_z.at[p], at.along(k))

    def fifth(p):
        row = lax.rem(p, LANES)
        wait_for(got_z.at[p], sem_z.at[p])
        total = lane[row, at.chip, z].astype(F32)
        for k in range(3):
            total = total + got_z[p, k].astype(F32)
        out[p] = total

    n = PIECES

    def small_first():
        pltpu.make_async_copy(small, s_part, load_sem.at[2]).wait()
        for a in range(4):
            src = s_part.at[:, :, cols_of(a * 2 + 1 - at.core)]
            send(src, s_c.at[a], sent0.at[n], sem_c.at[n], at.partner())

    def small_second():
        wait_for(s_c, sem_c.at[n])
        for a in range(4):
            s_lane[a] = s_part[:, :, cols_of(a * 2 + at.core)] + s_c[a]
        send(s_lane.at[at.diag, 0:2], s_dy, sent1.at[n], sem_dy.at[n], at.across())
        send(s_lane.at[at.diag, 2:4], s_dx, sent1.at[n], sem_dx.at[n], at.beside())

    def small_third():
        wait_for(s_dy, sem_dy.at[n])
        s_lane[at.side, 0:2] = s_lane[at.side, 0:2] + s_dy[...]
        send(s_lane.at[at.side], s_x, sent2.at[n], sem_x.at[n], at.beside())
        wait_for(s_dx, sem_dx.at[n])
        s_lane[at.over, 2:4] = s_lane[at.over, 2:4] + s_dx[...]
        send(s_lane.at[at.over], s_y, sent2.at[n], sem_y.at[n], at.across())

    def small_fourth():
        wait_for(s_x, sem_x.at[n])
        wait_for(s_y, sem_y.at[n])
        s_lane[at.chip] = s_lane[at.chip] + s_x[...] + s_y[...]
        for k in range(1, 4):
            block = s_lane.at[at.chip, lax.rem(z + k, 4)]
            send(block, s_z.at[k - 1], sent3.at[n], sem_z.at[n], at.along(k))

    def small_fifth():
        wait_for(s_z, sem_z.at[n])
        small_out[...] = s_lane[at.chip, z] + s_z[0] + s_z[1] + s_z[2]

    def halo():
        for i in range(3):
            @pl.when(z > i)
            def _():
                src = dh_win.at[tile_rows(i * step, step)]
                dst = halo_in.at[tile_rows((5 - z + i) * step, step)]
                send(src, dst, halo_sent, halo_got, at.along(3))

            @pl.when(z < 3 - i)
            def _():
                src = dh_win.at[tile_rows((5 + z + i) * step, step)]
                dst = halo_in.at[tile_rows(i * step, step)]
                send(src, dst, halo_sent, halo_got, at.along(1))

    pltpu.make_async_copy(small, s_part, load_sem.at[2]).start()
    load(0, 0)
    load(1, 0)
    halo()
    stages = ((first, 0), (second, -1), (third, -2), (fourth, -3), (fifth, -4))
    small_stages = (small_first, small_second, small_third, small_fourth, small_fifth)

    def tick(t, carry):
        for action, shift in stages:
            when_in(t + shift, PIECES, action)
        for i, action in enumerate(small_stages):
            @pl.when(t == i + 1)
            def _():
                action()
        return carry

    lax.fori_loop(0, PIECES + 4, tick, 0)
    for p in range(PIECES - LANES, PIECES):
        row = p % LANES
        wait_for(lane.at[row, 0], sent1.at[p])
        wait_for(lane.at[row, 0:2], sent2.at[p])
        wait_for(lane.at[row, 0, 0:3], sent3.at[p])
    wait_for(s_c, sent0.at[n])
    wait_for(s_lane.at[0], sent1.at[n])
    wait_for(s_lane.at[0:2], sent2.at[n])
    wait_for(s_lane.at[0, 0:3], sent3.at[n])
    wait_for(dh_win.at[0 : 3 * step], halo_sent)
    middle = jnp.logical_and(z >= 1, z <= 2)

    @pl.when(middle)
    def _():
        wait_for(halo_in.at[0 : 5 * step], halo_got)

    @pl.when(jnp.logical_not(middle))
    def _():
        wait_for(halo_in.at[0:step], halo_got)


def scatter_grads(outer, grads, small, dh_win):
    sem = pltpu.SemaphoreType.DMA
    half = (4, 4, ROWS, COLS)
    step = dh_win.shape[0] // 8
    anywhere, vmem = pl.BlockSpec(memory_space=pl.ANY), pl.BlockSpec(memory_space=pltpu.VMEM)
    return pl.pallas_call(
        functools.partial(scatter_kernel, outer),
        out_shape=(
            jax.ShapeDtypeStruct((PIECES, ROWS, COLS), F32),
            jax.ShapeDtypeStruct((8, COLS), F32),
            jax.ShapeDtypeStruct((5 * step, dh_win.shape[1]), BF),
        ),
        in_specs=[anywhere] * 8,
        out_specs=[vmem, vmem, anywhere],
        scratch_shapes=[
            pltpu.VMEM((2, 4, ROWS, 8 * COLS), BF),
            pltpu.VMEM((LANES,) + half, BF),
            pltpu.VMEM((2,) + half, BF),
            pltpu.VMEM((PIECES, 2, ROWS, COLS), BF),
            pltpu.VMEM((PIECES, 2, ROWS, COLS), BF),
            pltpu.VMEM((PIECES, 4, ROWS, COLS), BF),
            pltpu.VMEM((PIECES, 4, ROWS, COLS), BF),
            pltpu.VMEM((PIECES, 3, ROWS, COLS), BF),
            pltpu.VMEM((4, 8, 8 * COLS), F32),
            pltpu.VMEM((4, 4, 8, COLS), F32),
            pltpu.VMEM((4, 4, 8, COLS), F32),
            pltpu.VMEM((2, 8, COLS), F32),
            pltpu.VMEM((2, 8, COLS), F32),
            pltpu.VMEM((4, 8, COLS), F32),
            pltpu.VMEM((4, 8, COLS), F32),
            pltpu.VMEM((3, 8, COLS), F32),
            sem((3,)),
        ]
        + [sem((PIECES + 1,))] * 10
        + [sem, sem, pltpu.SemaphoreType.REGULAR],
        compiler_params=pltpu.CompilerParams(
            collective_id=2, has_side_effects=True, vmem_limit_bytes=VMEM_LIMIT
        ),
        name="scatter",
    )(*grads, small, dh_win)


def split_heads(rows):
    low = lax.broadcasted_iota(jnp.int32, rows.shape, 1) < rows.shape[1] // 2
    zero = jnp.zeros_like(rows)
    return jnp.concatenate([jnp.where(low, rows, zero), jnp.where(low, zero, rows)], axis=0)


def join_heads(both):
    half = both.shape[1] // 2
    low = lax.broadcasted_iota(jnp.int32, (both.shape[0], half), 0) < both.shape[0] // 2
    return jnp.where(low, both[:, :half], both[:, half:]).T


def masked_scores(keys, q_two, live):
    scores = dot_nt(keys, q_two)
    return jnp.where(lax.broadcasted_iota(jnp.int32, scores.shape, 0) < live, scores, MASKED)


def attend_kernel(scale, meta, q_ref, k_ref, v_ref, o_ref, lse_ref, v_t):
    seq_len, step = k_ref.shape[0] // 2, q_ref.shape[0] // 5
    v_t[...] = v_ref[...].T
    for j in range(5):
        slot = meta[j]
        keys = tile_rows(slot * seq_len, seq_len)
        rows = slice(j * step, (j + 1) * step)
        q_two = split_heads(q_ref[rows, :] * jnp.asarray(scale, BF))
        scores = masked_scores(k_ref[keys, :], q_two, meta[5 + slot])
        row_max = jnp.max(scores, axis=0, keepdims=True)
        expo = jnp.exp(scores - row_max)
        total = jnp.sum(expo, axis=0, keepdims=True)
        mixed = dot_nn(v_t[:, keys], expo.astype(BF)) / total
        o_ref[rows, :] = join_heads(mixed).astype(BF)
        lse_ref[0, j : j + 1, :] = row_max + jnp.log(total)


def attend(meta, q, k, v, head):
    rows, model = q.shape
    win, step, wide = k.shape[0], rows // 5, 2 * head
    block = lambda n: pl.BlockSpec((n, wide), lambda i, m: (0, i))
    return pl.pallas_call(
        functools.partial(attend_kernel, head**-0.5),
        out_shape=(
            jax.ShapeDtypeStruct((rows, model), BF),
            jax.ShapeDtypeStruct((model // wide, 8, 2 * step), F32),
        ),
        grid_spec=pltpu.PrefetchScalarGridSpec(
            num_scalar_prefetch=1,
            grid=(model // wide,),
            in_specs=[block(rows), block(win), block(win)],
            out_specs=[block(rows), pl.BlockSpec((1, 8, 2 * step), lambda i, m: (i, 0, 0))],
            scratch_shapes=[pltpu.VMEM((wide, win), BF)],
        ),
        compiler_params=pltpu.CompilerParams(vmem_limit_bytes=VMEM_LIMIT // 2),
        name="attend",
    )(meta, q, k, v)


def attend_back_kernel(
    scale, meta, q_ref, k_ref, v_ref, g_ref, lse_ref, dq_ref, dk_ref, dv_ref, k_t, dk_acc, dv_acc
):
    seq_len, step = k_ref.shape[0] // 2, q_ref.shape[0] // 5
    k_t[...] = k_ref[...].T
    dk_acc[...] = jnp.zeros_like(dk_acc)
    dv_acc[...] = jnp.zeros_like(dv_acc)
    for j in range(5):
        slot = meta[j]
        keys = tile_rows(slot * seq_len, seq_len)
        rows = slice(j * step, (j + 1) * step)
        q_two = split_heads(q_ref[rows, :] * jnp.asarray(scale, BF))
        g_two = split_heads(g_ref[rows, :])
        scores = masked_scores(k_ref[keys, :], q_two, meta[5 + slot])
        probs = jnp.exp(scores - lse_ref[0, j : j + 1, :])
        dv_acc[keys, :] += dot_nn(probs.astype(BF), g_two)
        grad_p = dot_nt(v_ref[keys, :], g_two)
        inner = jnp.sum(probs * grad_p, axis=0, keepdims=True)
        grad_s = (probs * (grad_p - inner)).astype(BF)
        dk_acc[keys, :] += dot_nn(grad_s, q_two)
        dq_ref[rows, :] = (join_heads(dot_nn(k_t[:, keys], grad_s)) * scale).astype(BF)
    dk_ref[...] = dk_acc[...].astype(BF)
    dv_ref[...] = dv_acc[...].astype(BF)


def attend_back(meta, q, k, v, g, lse, head):
    rows, model = q.shape
    win, step, wide = k.shape[0], rows // 5, 2 * head
    block = lambda n: pl.BlockSpec((n, wide), lambda i, m: (0, i))
    return pl.pallas_call(
        functools.partial(attend_back_kernel, head**-0.5),
        out_shape=(
            jax.ShapeDtypeStruct((rows, model), BF),
            jax.ShapeDtypeStruct((win, model), BF),
            jax.ShapeDtypeStruct((win, model), BF),
        ),
        grid_spec=pltpu.PrefetchScalarGridSpec(
            num_scalar_prefetch=1,
            grid=(model // wide,),
            in_specs=[
                block(rows), block(win), block(win), block(rows),
                pl.BlockSpec((1, 8, 2 * step), lambda i, m: (i, 0, 0)),
            ],
            out_specs=[block(rows), block(win), block(win)],
            scratch_shapes=[
                pltpu.VMEM((wide, win), BF), pltpu.VMEM((win, wide), F32), pltpu.VMEM((win, wide), F32)
            ],
        ),
        compiler_params=pltpu.CompilerParams(vmem_limit_bytes=VMEM_LIMIT // 2),
        name="attend_back",
    )(meta, q, k, v, g, lse)


def layer_norm(values_in, gain, shift):
    average = jnp.mean(values_in, axis=-1, keepdims=True)
    centred = values_in - average
    variance = jnp.mean(centred * centred, axis=-1, keepdims=True)
    return centred * lax.rsqrt(variance + LN_EPS) * gain + shift


def gelu_exact(values_in):
    return jax.nn.gelu(values_in, approximate=False)


def body(
    outer, tokens, context, timestep, time_weight, time_bias, qkv_weight, qv_bias, out_weight, out_bias,
    gain_one, shift_one, up_weight, up_bias, down_weight, down_bias, gain_two, shift_two, cotangent,
):
    z = lax.axis_index("mp")
    rows, model = tokens.shape
    seqs = context.shape[0]
    seq_len = rows * 4 // seqs
    step = rows // 5
    groups = None
    if outer > 1:
        groups = [[i * outer + j for j in range(outer)] for i in range(8)]
        qkv_weight, out_weight, up_weight, down_weight, qv_bias, up_bias = (
            lax.all_gather(w, "dp", axis=1, tiled=True, axis_index_groups=groups)
            for w in (qkv_weight, out_weight, up_weight, down_weight, qv_bias, up_bias)
        )
    shard = jnp.concatenate(
        [
            qkv_weight.transpose(0, 2, 1),
            out_weight.reshape(1, ROWS, COLS),
            up_weight.reshape(4, ROWS, COLS),
            down_weight.reshape(4, ROWS, COLS),
        ]
    )
    flat = jnp.concatenate([up_bias.reshape(-1), qv_bias.reshape(-1)])
    n_up, n_qv = up_bias.size, qv_bias.size
    small = jnp.pad(flat, (0, 16 * COLS - flat.size)).reshape(1, 16, COLS)
    row_ids = z * rows + jnp.arange(rows, dtype=jnp.int32)
    owner = (row_ids // seq_len)[:, None] == jnp.arange(seqs, dtype=jnp.int32)[None, :]
    portion = timestep.astype(F32) / TSTEPS
    fraction = jnp.sum(jnp.where(owner, portion[None, :], 0.0), axis=1)
    h_zero = tokens.astype(F32) + fraction[:, None] * time_weight + time_bias
    h_low = h_zero.astype(BF)
    full, small_full, h_win = gather_weights(outer, shard, small, h_low)
    w_q, w_k, w_v, w_out = (full[i].reshape(model, model) for i in range(4))
    w_up, w_down = full[4:8].reshape(4 * model, model), full[8:12].reshape(4 * model, model)
    flat = small_full.reshape(4, 16, 8, COLS)[:, :2].transpose(0, 2, 1, 3).reshape(4, 8, 2 * COLS)
    up_all = flat[:, :, :n_up].reshape(4, 8, 4, 2, 16).transpose(2, 0, 3, 1, 4).reshape(-1)
    qv_all = flat[:, :, n_up : n_up + n_qv].reshape(4, 8, 4, 16).transpose(0, 2, 1, 3).reshape(16, 2, -1)
    heads, head = qv_all.shape[0], qv_all.shape[2]
    bias_f = qv_all.astype(F32)
    queries = (dot_nt(h_low, w_q) + bias_f[:, 0].reshape(-1)).astype(BF)
    keys = dot_nt(h_win, w_k).astype(BF)
    values = (dot_nt(h_win, w_v) + bias_f[:, 1].reshape(-1)).astype(BF)
    live = (context + BLOCK).astype(jnp.int32)
    slots = (z + jnp.arange(5, dtype=jnp.int32)) // 4
    meta = jnp.concatenate([slots, lax.dynamic_slice(live, (z,), (2,))])
    attn, lse = attend(meta, queries, keys, values, head)
    branch_a = dot_nn(attn, w_out) + out_bias
    y_one, ln_one_back = jax.vjp(layer_norm, h_zero + branch_a, gain_one, shift_one)
    y_low = y_one.astype(BF)
    pre = dot_nt(y_low, w_up) + up_all.astype(F32)
    hidden, gelu_back = jax.vjp(gelu_exact, pre)
    hidden_low = hidden.astype(BF)
    branch_f = dot_nn(hidden_low, w_down) + down_bias
    y_two, ln_two_back = jax.vjp(layer_norm, y_one + branch_f, gain_two, shift_two)
    layer_out = y_two.astype(BF)
    grad_z2, grad_gain_two, grad_shift_two = ln_two_back(cotangent.astype(F32))
    grad_f = grad_z2.astype(BF)
    grad_down_bias = jnp.sum(grad_f.astype(F32), axis=0)
    (grad_pre,) = gelu_back(dot_nt(grad_f, w_down))
    grad_pre = grad_pre.astype(BF)
    grad_up = dot_tn(grad_pre, y_low).astype(BF)
    grad_down = dot_tn(hidden_low, grad_f).astype(BF)
    grad_up_bias = jnp.sum(grad_pre.astype(F32), axis=0)
    grad_y1 = grad_z2 + dot_nn(grad_pre, w_up)
    grad_z1, grad_gain_one, grad_shift_one = ln_one_back(grad_y1)
    grad_a = grad_z1.astype(BF)
    grad_out_bias = jnp.sum(grad_a.astype(F32), axis=0)
    grad_attn = dot_nt(grad_a, w_out).astype(BF)
    grad_out_w = dot_tn(attn, grad_a).astype(BF)
    dq, dk, dv = attend_back(meta, queries, keys, values, grad_attn, lse, head)
    grad_qv_bias = jnp.stack(
        [
            jnp.sum(dq.astype(F32), axis=0).reshape(heads, head),
            jnp.sum(dv.astype(F32), axis=0).reshape(heads, head),
        ],
        axis=1,
    )
    dh_win = dot_nn(dk, w_k) + dot_nn(dv, w_v)
    dh_own = grad_z1 + dot_nn(dq, w_q)
    portion_two = jnp.repeat(lax.dynamic_slice(portion, (z,), (2,)), seq_len)
    grad_time_weight = jnp.sum(fraction[:, None] * dh_own, axis=0) + jnp.sum(
        portion_two[:, None] * dh_win, axis=0
    )
    grad_time_bias = jnp.sum(dh_own, axis=0) + jnp.sum(dh_win, axis=0)
    dh_own = dh_own + lax.dynamic_slice(dh_win, (z * step, 0), (rows, model))
    spread = model // (32 * outer)
    vectors = jnp.stack(
        [
            grad_time_weight, grad_time_bias, grad_out_bias, grad_gain_one, grad_shift_one,
            grad_down_bias, grad_gain_two, grad_shift_two,
        ]
    )
    packed = jnp.concatenate(
        [
            vectors.reshape(8, 8, outer, 4, spread).transpose(3, 1, 0, 2, 4).reshape(4, 8, -1),
            grad_up_bias.reshape(4, 4, 2, 8, 16).transpose(1, 3, 0, 2, 4).reshape(4, 8, -1),
            grad_qv_bias.reshape(4, 4, 8, 16).transpose(0, 2, 1, 3).reshape(4, 8, -1),
        ],
        axis=2,
    )
    n_vec = 8 * outer * spread
    packed = jnp.pad(packed, ((0, 0), (0, 0), (0, 8 * COLS - packed.shape[2])))
    packed = packed.reshape(4, 8, 8, COLS).transpose(0, 2, 1, 3).reshape(4, 8, 8 * COLS)
    square = (4, ROWS, model)
    tall = (4,) + square
    grads = (
        dot_tn(dq, h_low).astype(BF).reshape(square),
        dot_tn(dk, h_win).astype(BF).reshape(square),
        dot_tn(dv, h_win).astype(BF).reshape(square),
        grad_out_w.reshape(square),
        grad_up.reshape(tall),
        grad_down.reshape(tall),
    )
    done, small_done, halo_in = scatter_grads(outer, grads, packed, dh_win.astype(BF))
    local = jnp.arange(rows, dtype=jnp.int32)
    edge = (4 - z) * step
    reached = jnp.logical_or(
        jnp.logical_and(z <= 2, local >= edge), jnp.logical_and(z >= 1, local < edge)
    )
    grad_tokens = dh_own + jnp.where(reached[:, None], halo_in.astype(F32), 0.0)
    small_done = small_done.reshape(-1)
    results = [
        done[8:11].transpose(0, 2, 1),
        done[11],
        done[4:8].reshape(4 * ROWS, COLS),
        done[0:4].reshape(4 * ROWS, COLS),
        small_done[n_vec : n_vec + n_up].reshape(8, 16),
        small_done[n_vec + n_up : n_vec + n_up + n_qv].reshape(4, 16),
        small_done[:n_vec].reshape(8, outer * spread),
    ]
    if outer > 1:
        results = [
            lax.psum_scatter(g, "dp", scatter_dimension=1, tiled=True, axis_index_groups=groups)
            for g in results
        ]
    grad_qkv, grad_out_w, grad_up, grad_down, grad_up_bias, grad_qv_bias, vectors = results
    return (
        layer_out, grad_tokens, vectors[0], vectors[1], grad_qkv, grad_qv_bias,
        grad_out_w, vectors[2], vectors[3], vectors[4], grad_up, grad_up_bias,
        grad_down, vectors[5], vectors[6], vectors[7],
    )


def solution(mesh):
    outer = mesh.shape["dp"] // 8
    placed = (
        P(("dp", "mp"), None), P("dp"), P("dp"), P(), P(), P(None, "dp", "mp"), P("mp", "dp"), P("mp", "dp"),
        P(), P(), P(), P("mp", "dp"), P("mp", "dp"), P("mp", "dp"), P(), P(), P(), P(("dp", "mp"), None),
    )
    spread = P(("dp", "mp"))
    wide = P("mp", "dp")
    return jax.shard_map(
        functools.partial(body, outer),
        mesh=mesh,
        in_specs=placed,
        out_specs=(
            P(("dp", "mp"), None), P(("dp", "mp"), None), spread, spread, P(None, "dp", "mp"), wide, wide,
            spread, spread, spread, wide, wide, wide, spread, spread, spread,
        ),
        check_vma=False,
    )
```

```python
import functools
import math

import jax
import jax.numpy as jnp
from jax import lax
from jax.experimental import pallas as pl
from jax.experimental.pallas import tpu as pltpu
from jax.sharding import PartitionSpec as P

BLOCK = 25
TSTEPS = 5000
LN_EPS = 1e-05
MASKED = -1e30
MESH = pl.DeviceIdType.MESH
BF = jnp.bfloat16
F32 = jnp.float32
PIECES = 12
LANES = 4
ROWS = 256
COLS = 128
VMEM_LIMIT = 62 * 2**20


def dot_nn(left, right):
    return lax.dot_general(left, right, (((1,), (0,)), ((), ())), preferred_element_type=F32)


def dot_nt(left, right):
    return lax.dot_general(left, right, (((1,), (1,)), ((), ())), preferred_element_type=F32)


def dot_tn(left, right):
    return lax.dot_general(left, right, (((0,), (0,)), ((), ())), preferred_element_type=F32)


class Place:
    def __init__(self, outer):
        dp = lax.axis_index("dp")
        self.z = lax.axis_index("mp")
        self.outer = outer
        self.own = lax.div(dp, outer)
        self.rest = lax.rem(dp, outer)
        self.core = lax.rem(self.own, 2)
        self.chip = lax.div(self.own, 2)
        col, row = lax.rem(self.chip, 2), lax.div(self.chip, 2)
        self.side = row * 2 + (1 - col)
        self.over = (1 - row) * 2 + col
        self.diag = (1 - row) * 2 + (1 - col)

    def dev(self, chip, core, z):
        return ((chip * 2 + core) * self.outer + self.rest, z)

    def partner(self):
        return self.dev(self.chip, 1 - self.core, self.z)

    def beside(self):
        return self.dev(self.side, self.core, self.z)

    def across(self):
        return self.dev(self.over, self.core, self.z)

    def along(self, k):
        return self.dev(self.chip, self.core, lax.rem(self.z + k, 4))


def greet(at):
    barrier = pltpu.get_barrier_semaphore()
    peers = [at.partner(), at.beside(), at.across()] + [at.along(k) for k in range(1, 4)]
    for peer in peers:
        pl.semaphore_signal(barrier, inc=1, device_id=peer, device_id_type=MESH)
    pl.semaphore_wait(barrier, len(peers))


def wait_for(ref, sem):
    pltpu.make_async_copy(ref, ref, sem).wait()


def send(src, dst, send_sem, recv_sem, device):
    pltpu.make_async_remote_copy(
        src, dst, send_sem, recv_sem, device_id=device, device_id_type=MESH
    ).start()


def when_in(piece, count, action):
    @pl.when(jnp.logical_and(piece >= 0, piece < count))
    def _():
        action(piece)


def cols_of(lane):
    return pl.ds(pl.multiple_of(lane * COLS, COLS), COLS)


def tile_rows(start, size):
    return pl.ds(pl.multiple_of(start, 128), size)


def norm_rows(values_in):
    average = jnp.mean(values_in, axis=-1, keepdims=True)
    centred = values_in - average
    rstd = lax.rsqrt(jnp.mean(centred * centred, axis=-1, keepdims=True) + LN_EPS)
    return centred * rstd, rstd


def norm_back(grad, xhat, rstd, gain):
    scaled = grad * gain
    first = jnp.mean(scaled, axis=-1, keepdims=True)
    second = jnp.mean(scaled * xhat, axis=-1, keepdims=True)
    return rstd * (scaled - first - xhat * second)


def fold_rows(values_in):
    rows, model = values_in.shape
    return jnp.sum(values_in.reshape(rows // 8, 8, model), axis=0)


def forward_kernel(
    outer, live, shard, small, h, tokens, cotangent, fraction, vecs,
    w_one, w_up, w_down, small_full, h_win_out, q_out, k_out, v_out, attn_out, y_out, hidden_out, slope_out,
    xhat_out, dz_out, grad_f_out, layer_out, lse, rstd_out, sums,
    h_win, q, k, v, attn, y_low, hidden, slope, xhat, acc, pre, grad_f, out_rows, bias_in, bias, wbuf, v_t,
    own_sem, sent, got_z, got_x, got_y, got_xd, got_yd, got_c, halo_sent, halo_got, load_sem, store_sem, slope_sem,
):
    at = Place(outer)
    greet(at)
    z, rows, model = at.z, h.shape[0], h.shape[1]
    step = rows // 5
    groups = (w_one, w_up, w_down)
    x_lane, y_lane, d_lane = at.side * 2 + at.core, at.over * 2 + at.core, at.diag * 2 + at.core

    def source(p):
        return small if p is None else shard.at[pl.ds(p, 1)]

    def block(ref, lane, start, count):
        return ref.at[pl.ds(start, count), :, cols_of(lane)]

    def index(p):
        return PIECES if p is None else p

    def grouped(action):
        def run(p):
            if p is None:
                action(None, small_full)
                return
            if isinstance(p, int):
                action(p, groups[p // 4].at[p % 4])
                return
            for g, ref in enumerate(groups):
                @pl.when(lax.div(p, 4) == g)
                def _():
                    action(p, ref.at[p - 4 * g])

        return run

    def first(p, ref):
        i, src, dst = index(p), source(p), block(ref, at.own, z, 1)
        send(src, dst, sent.at[i], got_x.at[i], at.beside())
        send(src, dst, sent.at[i], got_y.at[i], at.across())
        for step_z in range(1, 4):
            send(src, dst, sent.at[i], got_z.at[i], at.along(step_z))
        send(src, dst, sent.at[i], got_c.at[i], at.partner())

    def second(p, ref):
        i = index(p)
        wait_for(block(ref, at.own, 0, 3), got_z.at[i])
        for step_z in range(1, 4):
            part = block(ref, at.own, lax.rem(z + step_z, 4), 1)
            send(part, part, sent.at[i], got_x.at[i], at.beside())
            send(part, part, sent.at[i], got_y.at[i], at.across())
            send(part, part, sent.at[i], got_c.at[i], at.partner())

    def third(p, ref):
        i = index(p)
        wait_for(block(ref, x_lane, 0, 4), got_x.at[i])
        part = block(ref, x_lane, 0, 2)
        send(part, part, sent.at[i], got_yd.at[i], at.across())
        part = block(ref, x_lane, 0, 4)
        send(part, part, sent.at[i], got_c.at[i], at.partner())
        wait_for(block(ref, y_lane, 0, 4), got_y.at[i])
        part = block(ref, y_lane, 2, 2)
        send(part, part, sent.at[i], got_xd.at[i], at.beside())
        part = block(ref, y_lane, 0, 4)
        send(part, part, sent.at[i], got_c.at[i], at.partner())

    def fourth(p, ref):
        i = index(p)
        wait_for(block(ref, d_lane, 0, 2), got_yd.at[i])
        wait_for(block(ref, d_lane, 2, 2), got_xd.at[i])
        part = block(ref, d_lane, 0, 4)
        send(part, part, sent.at[i], got_c.at[i], at.partner())

    def load(p, ref):
        slot = lax.rem(p, 3)
        return pltpu.make_async_copy(ref, wbuf.at[slot], load_sem.at[slot])

    def fifth(p, ref):
        wait_for(ref.at[:, :, 0 : 4 * COLS], got_c.at[index(p)])
        if p is None:
            pltpu.make_async_copy(small_full, bias_in, own_sem.at[1]).start()
        else:
            load(p, ref).start()

    def drain(p, ref):
        wait_for(ref.at[:, :, 0 : 7 * COLS], sent.at[index(p)])
        wait_for(ref.at[0:3, :, 0:COLS], sent.at[index(p)])

    first, second, third, fourth, fifth, drain = (
        grouped(action) for action in (first, second, third, fourth, fifth, drain)
    )

    def halo():
        for i in range(3):
            @pl.when(jnp.logical_and(z >= 1, z < 4 - i))
            def _():
                dst = h_win.at[tile_rows((4 + z + i) * step, step)]
                send(h.at[tile_rows(i * step, step)], dst, halo_sent, halo_got, at.along(3))

            @pl.when(jnp.logical_and(z <= 2, z >= i))
            def _():
                dst = h_win.at[tile_rows(i * step, step)]
                send(h.at[tile_rows((4 - z + i) * step, step)], dst, halo_sent, halo_got, at.along(1))

    mine = [
        pltpu.make_async_copy(
            shard.at[4 * g : 4 * g + 4], ref.at[:, z, :, cols_of(at.own)], own_sem.at[2 + g]
        )
        for g, ref in enumerate(groups)
    ] + [pltpu.make_async_copy(small, small_full.at[pl.ds(z, 1), :, cols_of(at.own)], own_sem.at[0])]
    stores = []

    def store(src, dst):
        pltpu.make_async_copy(src, dst, store_sem.at[len(stores)]).start()
        stores.append((src, dst))

    n_tiles = model // ROWS

    def tiles(action):
        def run(n, carry):
            action(n, tile_rows(n * ROWS, ROWS))
            return carry

        lax.fori_loop(0, n_tiles, run, 0)

    def weight(p):
        slot = lax.rem(p, 3)
        pltpu.make_async_copy(w_one.at[0], wbuf.at[slot], load_sem.at[slot]).wait()
        return slot

    def make_bias():
        pltpu.make_async_copy(small_full, bias_in, own_sem.at[1]).wait()
        total = bias_in[:, :, 0:COLS].astype(F32)
        for lane in range(1, 8):
            total = total + bias_in[:, :, lane * COLS : (lane + 1) * COLS].astype(F32)
        bias[...] = total

    def project(p, rows_in, target, bias_row):
        slot = weight(p)

        def one(n, span):
            result = dot_nt(rows_in[...], wbuf[slot, n])
            if bias_row is not None:
                result = result + jnp.concatenate(
                    [bias[n, bias_row : bias_row + 1], bias[n, bias_row + 1 : bias_row + 2]], axis=1
                )
            target[:, span] = result.astype(BF)

        tiles(one)

    def queries():
        make_bias()
        project(0, h, q, 8)
        store(q, q_out)

    def keys():
        wait_for(h_win.at[0 : 3 * step], halo_got)
        h_win[tile_rows(z * step, rows), :] = h[...]
        project(1, h_win, k, None)
        store(k, k_out)
        store(h_win, h_win_out)

    def values():
        project(2, h_win, v, 10)
        store(v, v_out)

    def attend_pairs(start, count):
        def pair(i, carry):
            lanes = cols_of(i)
            v_t[...] = v[:, lanes].T
            for j in range(5):
                slot = lax.div(z + j, 4)
                span = tile_rows(slot * 4 * step, 4 * step)
                here = slice(j * step, (j + 1) * step)
                q_two = split_heads(q[here, lanes] * jnp.asarray(0.125, BF))
                scores = masked_scores(k[span, lanes], q_two, jnp.where(slot == 0, live[0], live[1]))
                row_max = jnp.max(scores, axis=0, keepdims=True)
                expo = jnp.exp(scores - row_max)
                total = jnp.sum(expo, axis=0, keepdims=True)
                mixed = dot_nn(v_t[:, span], expo.astype(BF)) / total
                attn[here, lanes] = join_heads(mixed).astype(BF)
                lse[i, j : j + 1, :] = row_max + jnp.log(total)
            return carry

        lax.fori_loop(start, start + count, pair, 0)

    def row_loop(count, action):
        def run(i, carry):
            action(pl.ds(pl.multiple_of(i * count, count), count))
            return carry

        lax.fori_loop(0, rows // count, run, 0)

    def out_project():
        slot = weight(3)

        def one(n, span):
            wide = wbuf[slot, :, :, span].reshape(model, ROWS)
            acc[:, span] = dot_nn(attn[...], wide)

        tiles(one)
        store(attn, attn_out)

        def norm(here):
            h_zero = tokens[here, :].astype(F32) + fraction[here, 0:1] * vecs[0:1, :] + vecs[1:2, :]
            normal, rstd = norm_rows(h_zero + acc[here, :] + vecs[2:3, :])
            xhat[here, :] = normal
            y_low[here, :] = (normal * vecs[3:4, :] + vecs[4:5, :]).astype(BF)
            rstd_out[here, :] = jnp.broadcast_to(rstd, (rstd.shape[0], COLS))

        row_loop(32, norm)
        acc[...] = jnp.zeros_like(acc)
        store(y_low, y_out)
        store(xhat, xhat_out)

    def slope_store(i):
        slot = lax.rem(i, 2)
        return pltpu.make_async_copy(slope.at[slot], slope_out.at[i], slope_sem.at[slot])

    def hidden_store(i):
        return pltpu.make_async_copy(hidden.at[i], hidden_out.at[i], slope_sem.at[2 + i])

    def up_piece(p):
        i, slot = p - 4, weight(p)
        side = lax.rem(i, 2)

        @pl.when(i >= 2)
        def _():
            slope_store(i - 2).wait()

        def one(n, span):
            offset = jnp.concatenate([bias[n, pl.ds(2 * i, 1)], bias[n, pl.ds(2 * i + 1, 1)]], axis=1)
            pre[...] = dot_nt(y_low[...], wbuf[slot, n]) + offset

            def gelu(here):
                x = pre[here, :]
                cdf = 0.5 + 0.5 * lax.erf(x * math.sqrt(0.5))
                pdf = jnp.exp(x * x * -0.5) * (1.0 / math.sqrt(2.0 * math.pi))
                hidden[i, here, span] = (x * cdf).astype(BF)
                slope[side, here, span] = (cdf + x * pdf).astype(BF)

            row_loop(32, gelu)

        tiles(one)
        slope_store(i).start()
        hidden_store(i).start()

    def down_piece(p):
        i, slot = p - 8, weight(p)

        def one(n, span):
            wide = wbuf[slot, :, :, span].reshape(model, ROWS)
            acc[:, span] += dot_nn(hidden[i], wide)

        tiles(one)

    def finish():
        sums[...] = jnp.zeros_like(sums)

        def norm(here):
            y_one = xhat[here, :] * vecs[3:4, :] + vecs[4:5, :]
            normal, rstd = norm_rows(y_one + acc[here, :] + vecs[5:6, :])
            out_rows[here, :] = (normal * vecs[6:7, :] + vecs[7:8, :]).astype(BF)
            cot = cotangent[here, :].astype(F32)
            grad = norm_back(cot, normal, rstd, vecs[6:7, :])
            acc[here, :] = grad
            low = grad.astype(BF)
            grad_f[here, :] = low
            sums[0] += fold_rows(cot * normal)
            sums[1] += fold_rows(cot)
            sums[2] += fold_rows(low.astype(F32))

        row_loop(32, norm)
        store(acc, dz_out)
        store(grad_f, grad_f_out)
        store(out_rows, layer_out)

    first(None)
    first(0)
    first(1)
    halo()
    for copy in mine:
        copy.start()
    stages = ((second, 0), (third, -1), (fourth, -2), (fifth, -3))
    work = {
        4: (queries,),
        5: (keys,),
        6: (values, lambda: attend_pairs(0, 2)),
        7: (lambda: attend_pairs(2, 4),),
        8: (lambda: attend_pairs(6, 2), out_project),
    }

    def tick(t, carry):
        @pl.when(t == 3)
        def _():
            for copy in mine:
                copy.wait()

        for action, shift in ((first, 2),) + stages:
            when_in(t + shift, PIECES, action)
        for action, shift in stages:
            @pl.when(t == -shift)
            def _():
                action(None)
        for when, actions in work.items():
            @pl.when(t == when)
            def _():
                for action in actions:
                    action()

        @pl.when(jnp.logical_and(t >= 9, t < 13))
        def _():
            up_piece(t - 5)

        @pl.when(t >= 13)
        def _():
            down_piece(t - 5)

        return carry

    lax.fori_loop(0, PIECES + 5, tick, 0)
    finish()
    middle = jnp.logical_and(z >= 1, z <= 2)

    @pl.when(middle)
    def _():
        wait_for(h.at[0 : 5 * step], halo_sent)

    @pl.when(jnp.logical_not(middle))
    def _():
        wait_for(h.at[0:step], halo_sent)

    def drain_one(p, carry):
        drain(p)
        return carry

    lax.fori_loop(0, PIECES, drain_one, 0)
    drain(None)
    slope_store(2).wait()
    slope_store(3).wait()
    for i in range(4):
        hidden_store(i).wait()
    for i, (src, dst) in enumerate(stores):
        pltpu.make_async_copy(src, dst, store_sem.at[i]).wait()


def forward_pass(outer, live, shard, small, h, tokens, cotangent, fraction, vecs):
    sem = pltpu.SemaphoreType.DMA
    rows, model = h.shape
    win = rows // 5 * 8
    weights = jax.ShapeDtypeStruct((4, 4, ROWS, model), BF)
    own = jax.ShapeDtypeStruct((rows, model), BF)
    own_wide = jax.ShapeDtypeStruct((rows, model), F32)
    window = jax.ShapeDtypeStruct((win, model), BF)
    tall = jax.ShapeDtypeStruct((4, rows, model), BF)
    anywhere, vmem = pl.BlockSpec(memory_space=pl.ANY), pl.BlockSpec(memory_space=pltpu.VMEM)
    return pl.pallas_call(
        functools.partial(forward_kernel, outer),
        out_shape=(
            weights, weights, weights, jax.ShapeDtypeStruct((4, 16, model), BF),
            window, own, window, window, own, own, tall, tall, own_wide, own_wide, own, own,
            jax.ShapeDtypeStruct((8, 8, 2 * rows // 5), F32),
            jax.ShapeDtypeStruct((rows, COLS), F32),
            jax.ShapeDtypeStruct((3, 8, model), F32),
        ),
        in_specs=[pl.BlockSpec(memory_space=pltpu.SMEM)] + [vmem] * 7,
        out_specs=[anywhere] * 16 + [vmem] * 3,
        scratch_shapes=[
            pltpu.VMEM((win, model), BF),
            pltpu.VMEM((rows, model), BF),
            pltpu.VMEM((win, model), BF),
            pltpu.VMEM((win, model), BF),
            pltpu.VMEM((rows, model), BF),
            pltpu.VMEM((rows, model), BF),
            pltpu.VMEM((4, rows, model), BF),
            pltpu.VMEM((2, rows, model), BF),
            pltpu.VMEM((rows, model), F32),
            pltpu.VMEM((rows, model), F32),
            pltpu.VMEM((rows, ROWS), F32),
            pltpu.VMEM((rows, model), BF),
            pltpu.VMEM((rows, model), BF),
            pltpu.VMEM((4, 16, model), BF),
            pltpu.VMEM((4, 16, COLS), F32),
            pltpu.VMEM((3, 4, ROWS, model), BF),
            pltpu.VMEM((COLS, win), BF),
            sem((5,)),
        ]
        + [sem((PIECES + 1,))] * 7
        + [sem, sem, sem((3,)), sem((10,)), sem((6,))],
        compiler_params=pltpu.CompilerParams(
            collective_id=1, has_side_effects=True, vmem_limit_bytes=VMEM_LIMIT
        ),
        name="forward",
    )(live, shard, small, h, tokens, cotangent, fraction, vecs)


def scatter_kernel(
    outer, g_q, g_k, g_v, g_out, g_up, g_down, small, dh_win, out, small_out, halo_in,
    part, lane, got_c, got_dx, got_dy, got_x, got_y, got_z,
    s_part, s_lane, s_c, s_dx, s_dy, s_x, s_y, s_z,
    load_sem, sent0, sent1, sent2, sent3, sem_c, sem_dx, sem_dy, sem_x, sem_y, sem_z,
    halo_sent, halo_got, credit,
):
    at = Place(outer)
    greet(at)
    z, step = at.z, dh_win.shape[0] // 8
    singles = [(8, g_q), (9, g_k), (10, g_v), (11, g_out)]

    def load(p, action):
        slot = lax.rem(p, 2)

        def go(src):
            copy = pltpu.make_async_copy(src, part.at[slot], load_sem.at[slot])
            copy.start() if action == 0 else copy.wait()

        if action == 1:
            go(g_up.at[0])
            return

        @pl.when(p < 4)
        def _():
            go(g_down.at[p])

        @pl.when(jnp.logical_and(p >= 4, p < 8))
        def _():
            go(g_up.at[lax.rem(p, 4)])

        for i, ref in singles:
            @pl.when(p == i)
            def _():
                go(ref)

    def first(p):
        slot = lax.rem(p, 2)
        load(p, 1)

        @pl.when(p >= 2)
        def _():
            pl.semaphore_wait(credit, 1)

        for a in range(4):
            src = part.at[slot, :, :, cols_of(a * 2 + 1 - at.core)]
            send(src, got_c.at[slot, a], sent0.at[p], sem_c.at[p], at.partner())

    def second(p):
        slot, row = lax.rem(p, 2), lax.rem(p, LANES)
        wait_for(got_c.at[slot], sem_c.at[p])

        @pl.when(p >= LANES)
        def _():
            wait_for(lane.at[row, 0], sent1.at[p - LANES])
            wait_for(lane.at[row, 0:2], sent2.at[p - LANES])
            wait_for(lane.at[row, 0, 0:3], sent3.at[p - LANES])

        def add(i, carry):
            a, b = lax.div(i, 4), lax.rem(i, 4)
            lane[row, a, b] = part[slot, b, :, cols_of(a * 2 + at.core)] + got_c[slot, a, b]
            return carry

        lax.fori_loop(0, 16, add, 0)

        @pl.when(p < PIECES - 2)
        def _():
            pl.semaphore_signal(credit, inc=1, device_id=at.partner(), device_id_type=MESH)

        wait_for(got_c.at[slot], sent0.at[p])

        @pl.when(p + 2 < PIECES)
        def _():
            load(p + 2, 0)

        send(lane.at[row, at.diag, 0:2], got_dy.at[p], sent1.at[p], sem_dy.at[p], at.across())
        send(lane.at[row, at.diag, 2:4], got_dx.at[p], sent1.at[p], sem_dx.at[p], at.beside())

    def third(p):
        row = lax.rem(p, LANES)
        wait_for(got_dy.at[p], sem_dy.at[p])

        def add_y(i, carry):
            lane[row, at.side, i] = lane[row, at.side, i] + got_dy[p, i]
            return carry

        lax.fori_loop(0, 2, add_y, 0)
        send(lane.at[row, at.side], got_x.at[p], sent2.at[p], sem_x.at[p], at.beside())
        wait_for(got_dx.at[p], sem_dx.at[p])

        def add_x(i, carry):
            lane[row, at.over, i + 2] = lane[row, at.over, i + 2] + got_dx[p, i]
            return carry

        lax.fori_loop(0, 2, add_x, 0)
        send(lane.at[row, at.over], got_y.at[p], sent2.at[p], sem_y.at[p], at.across())

    def fourth(p):
        row = lax.rem(p, LANES)
        wait_for(got_x.at[p], sem_x.at[p])
        wait_for(got_y.at[p], sem_y.at[p])

        def add(i, carry):
            total = lane[row, at.chip, i].astype(F32) + got_x[p, i].astype(F32)
            lane[row, at.chip, i] = (total + got_y[p, i].astype(F32)).astype(BF)
            return carry

        lax.fori_loop(0, 4, add, 0)
        for k in range(1, 4):
            block = lane.at[row, at.chip, lax.rem(z + k, 4)]
            send(block, got_z.at[p, k - 1], sent3.at[p], sem_z.at[p], at.along(k))

    def fifth(p):
        row = lax.rem(p, LANES)
        wait_for(got_z.at[p], sem_z.at[p])
        total = lane[row, at.chip, z].astype(F32)
        for k in range(3):
            total = total + got_z[p, k].astype(F32)
        out[p] = total

    n = PIECES

    def small_first():
        pltpu.make_async_copy(small, s_part, load_sem.at[2]).wait()
        for a in range(4):
            src = s_part.at[:, :, cols_of(a * 2 + 1 - at.core)]
            send(src, s_c.at[a], sent0.at[n], sem_c.at[n], at.partner())

    def small_second():
        wait_for(s_c, sem_c.at[n])
        for a in range(4):
            s_lane[a] = s_part[:, :, cols_of(a * 2 + at.core)] + s_c[a]
        send(s_lane.at[at.diag, 0:2], s_dy, sent1.at[n], sem_dy.at[n], at.across())
        send(s_lane.at[at.diag, 2:4], s_dx, sent1.at[n], sem_dx.at[n], at.beside())

    def small_third():
        wait_for(s_dy, sem_dy.at[n])
        s_lane[at.side, 0:2] = s_lane[at.side, 0:2] + s_dy[...]
        send(s_lane.at[at.side], s_x, sent2.at[n], sem_x.at[n], at.beside())
        wait_for(s_dx, sem_dx.at[n])
        s_lane[at.over, 2:4] = s_lane[at.over, 2:4] + s_dx[...]
        send(s_lane.at[at.over], s_y, sent2.at[n], sem_y.at[n], at.across())

    def small_fourth():
        wait_for(s_x, sem_x.at[n])
        wait_for(s_y, sem_y.at[n])
        s_lane[at.chip] = s_lane[at.chip] + s_x[...] + s_y[...]
        for k in range(1, 4):
            block = s_lane.at[at.chip, lax.rem(z + k, 4)]
            send(block, s_z.at[k - 1], sent3.at[n], sem_z.at[n], at.along(k))

    def small_fifth():
        wait_for(s_z, sem_z.at[n])
        small_out[...] = s_lane[at.chip, z] + s_z[0] + s_z[1] + s_z[2]

    def halo():
        for i in range(3):
            @pl.when(z > i)
            def _():
                src = dh_win.at[tile_rows(i * step, step)]
                dst = halo_in.at[tile_rows((5 - z + i) * step, step)]
                send(src, dst, halo_sent, halo_got, at.along(3))

            @pl.when(z < 3 - i)
            def _():
                src = dh_win.at[tile_rows((5 + z + i) * step, step)]
                dst = halo_in.at[tile_rows(i * step, step)]
                send(src, dst, halo_sent, halo_got, at.along(1))

    pltpu.make_async_copy(small, s_part, load_sem.at[2]).start()
    load(0, 0)
    load(1, 0)
    halo()
    stages = ((first, 0), (second, -1), (third, -2), (fourth, -3), (fifth, -4))
    small_stages = (small_first, small_second, small_third, small_fourth, small_fifth)

    def tick(t, carry):
        for action, shift in stages:
            when_in(t + shift, PIECES, action)
        for i, action in enumerate(small_stages):
            @pl.when(t == i + 1)
            def _():
                action()
        return carry

    lax.fori_loop(0, PIECES + 4, tick, 0)
    for p in range(PIECES - LANES, PIECES):
        row = p % LANES
        wait_for(lane.at[row, 0], sent1.at[p])
        wait_for(lane.at[row, 0:2], sent2.at[p])
        wait_for(lane.at[row, 0, 0:3], sent3.at[p])
    wait_for(s_c, sent0.at[n])
    wait_for(s_lane.at[0], sent1.at[n])
    wait_for(s_lane.at[0:2], sent2.at[n])
    wait_for(s_lane.at[0, 0:3], sent3.at[n])
    wait_for(dh_win.at[0 : 3 * step], halo_sent)
    middle = jnp.logical_and(z >= 1, z <= 2)

    @pl.when(middle)
    def _():
        wait_for(halo_in.at[0 : 5 * step], halo_got)

    @pl.when(jnp.logical_not(middle))
    def _():
        wait_for(halo_in.at[0:step], halo_got)


def scatter_grads(outer, grads, small, dh_win):
    sem = pltpu.SemaphoreType.DMA
    half = (4, 4, ROWS, COLS)
    step = dh_win.shape[0] // 8
    anywhere, vmem = pl.BlockSpec(memory_space=pl.ANY), pl.BlockSpec(memory_space=pltpu.VMEM)
    return pl.pallas_call(
        functools.partial(scatter_kernel, outer),
        out_shape=(
            jax.ShapeDtypeStruct((PIECES, ROWS, COLS), F32),
            jax.ShapeDtypeStruct((8, COLS), F32),
            jax.ShapeDtypeStruct((5 * step, dh_win.shape[1]), BF),
        ),
        in_specs=[anywhere] * 8,
        out_specs=[vmem, vmem, anywhere],
        scratch_shapes=[
            pltpu.VMEM((2, 4, ROWS, 8 * COLS), BF),
            pltpu.VMEM((LANES,) + half, BF),
            pltpu.VMEM((2,) + half, BF),
            pltpu.VMEM((PIECES, 2, ROWS, COLS), BF),
            pltpu.VMEM((PIECES, 2, ROWS, COLS), BF),
            pltpu.VMEM((PIECES, 4, ROWS, COLS), BF),
            pltpu.VMEM((PIECES, 4, ROWS, COLS), BF),
            pltpu.VMEM((PIECES, 3, ROWS, COLS), BF),
            pltpu.VMEM((4, 8, 8 * COLS), F32),
            pltpu.VMEM((4, 4, 8, COLS), F32),
            pltpu.VMEM((4, 4, 8, COLS), F32),
            pltpu.VMEM((2, 8, COLS), F32),
            pltpu.VMEM((2, 8, COLS), F32),
            pltpu.VMEM((4, 8, COLS), F32),
            pltpu.VMEM((4, 8, COLS), F32),
            pltpu.VMEM((3, 8, COLS), F32),
            sem((3,)),
        ]
        + [sem((PIECES + 1,))] * 10
        + [sem, sem, pltpu.SemaphoreType.REGULAR],
        compiler_params=pltpu.CompilerParams(
            collective_id=2, has_side_effects=True, vmem_limit_bytes=VMEM_LIMIT
        ),
        name="scatter",
    )(*grads, small, dh_win)


def split_heads(rows):
    low = lax.broadcasted_iota(jnp.int32, rows.shape, 1) < rows.shape[1] // 2
    zero = jnp.zeros_like(rows)
    return jnp.concatenate([jnp.where(low, rows, zero), jnp.where(low, zero, rows)], axis=0)


def join_heads(both):
    half = both.shape[1] // 2
    low = lax.broadcasted_iota(jnp.int32, (both.shape[0], half), 0) < both.shape[0] // 2
    return jnp.where(low, both[:, :half], both[:, half:]).T


def masked_scores(keys, q_two, live):
    scores = dot_nt(keys, q_two)
    return jnp.where(lax.broadcasted_iota(jnp.int32, scores.shape, 0) < live, scores, MASKED)


def attend_back_kernel(
    scale, meta, q_ref, k_ref, v_ref, g_ref, lse_ref, dq_ref, dk_ref, dv_ref, k_t, dk_acc, dv_acc
):
    seq_len, step = k_ref.shape[0] // 2, q_ref.shape[0] // 5
    k_t[...] = k_ref[...].T
    dk_acc[...] = jnp.zeros_like(dk_acc)
    dv_acc[...] = jnp.zeros_like(dv_acc)
    for j in range(5):
        slot = meta[j]
        keys = tile_rows(slot * seq_len, seq_len)
        rows = slice(j * step, (j + 1) * step)
        q_two = split_heads(q_ref[rows, :] * jnp.asarray(scale, BF))
        g_two = split_heads(g_ref[rows, :])
        scores = masked_scores(k_ref[keys, :], q_two, meta[5 + slot])
        probs = jnp.exp(scores - lse_ref[0, j : j + 1, :])
        dv_acc[keys, :] += dot_nn(probs.astype(BF), g_two)
        grad_p = dot_nt(v_ref[keys, :], g_two)
        inner = jnp.sum(probs * grad_p, axis=0, keepdims=True)
        grad_s = (probs * (grad_p - inner)).astype(BF)
        dk_acc[keys, :] += dot_nn(grad_s, q_two)
        dq_ref[rows, :] = (join_heads(dot_nn(k_t[:, keys], grad_s)) * scale).astype(BF)
    dk_ref[...] = dk_acc[...].astype(BF)
    dv_ref[...] = dv_acc[...].astype(BF)


def attend_back(meta, q, k, v, g, lse, head):
    rows, model = q.shape
    win, step, wide = k.shape[0], rows // 5, 2 * head
    block = lambda n: pl.BlockSpec((n, wide), lambda i, m: (0, i))
    return pl.pallas_call(
        functools.partial(attend_back_kernel, head**-0.5),
        out_shape=(
            jax.ShapeDtypeStruct((rows, model), BF),
            jax.ShapeDtypeStruct((win, model), BF),
            jax.ShapeDtypeStruct((win, model), BF),
        ),
        grid_spec=pltpu.PrefetchScalarGridSpec(
            num_scalar_prefetch=1,
            grid=(model // wide,),
            in_specs=[
                block(rows), block(win), block(win), block(rows),
                pl.BlockSpec((1, 8, 2 * step), lambda i, m: (i, 0, 0)),
            ],
            out_specs=[block(rows), block(win), block(win)],
            scratch_shapes=[
                pltpu.VMEM((wide, win), BF), pltpu.VMEM((win, wide), F32), pltpu.VMEM((win, wide), F32)
            ],
        ),
        compiler_params=pltpu.CompilerParams(vmem_limit_bytes=VMEM_LIMIT // 2),
        name="attend_back",
    )(meta, q, k, v, g, lse)


def body(
    outer, tokens, context, timestep, time_weight, time_bias, qkv_weight, qv_bias, out_weight, out_bias,
    gain_one, shift_one, up_weight, up_bias, down_weight, down_bias, gain_two, shift_two, cotangent,
):
    z = lax.axis_index("mp")
    rows, model = tokens.shape
    seqs = context.shape[0]
    seq_len = rows * 4 // seqs
    step = rows // 5
    groups = None
    if outer > 1:
        groups = [[i * outer + j for j in range(outer)] for i in range(8)]
        qkv_weight, out_weight, up_weight, down_weight, qv_bias, up_bias = (
            lax.all_gather(w, "dp", axis=1, tiled=True, axis_index_groups=groups)
            for w in (qkv_weight, out_weight, up_weight, down_weight, qv_bias, up_bias)
        )
    shard = jnp.concatenate(
        [
            qkv_weight.transpose(0, 2, 1),
            out_weight.reshape(1, ROWS, COLS),
            up_weight.reshape(4, ROWS, COLS),
            down_weight.reshape(4, ROWS, COLS),
        ]
    )
    own = lax.div(lax.axis_index("dp"), outer)
    n_up, n_qv = up_bias.size, qv_bias.size
    part = jnp.arange(COLS) // up_bias.shape[1]
    up_rows = jnp.where(part == own, jnp.tile(up_bias, (1, 8)), 0)
    qv_rows = jnp.where(part[:64] == own % 4, jnp.tile(qv_bias, (1, 4)), 0).reshape(2, COLS)
    none = jnp.zeros_like(qv_rows)
    q_rows, v_rows = jnp.where(own < 4, qv_rows, none), jnp.where(own < 4, none, qv_rows)
    small = jnp.concatenate([up_rows, q_rows, v_rows, none, none]).reshape(1, 16, COLS)
    row_ids = z * rows + jnp.arange(rows, dtype=jnp.int32)
    owner = (row_ids // seq_len)[:, None] == jnp.arange(seqs, dtype=jnp.int32)[None, :]
    portion = timestep.astype(F32) / TSTEPS
    fraction = jnp.sum(jnp.where(owner, portion[None, :], 0.0), axis=1)
    h_low = (tokens.astype(F32) + fraction[:, None] * time_weight + time_bias).astype(BF)
    live = lax.dynamic_slice((context + BLOCK).astype(jnp.int32), (z,), (2,))
    vecs = jnp.stack(
        [time_weight, time_bias, out_bias, gain_one, shift_one, down_bias, gain_two, shift_two]
    )
    (
        w_one, w_up, w_down, _, h_win, queries, keys, values, attn, y_low, hidden, slope, xhat, grad_z2,
        grad_f, layer_out, lse, rstd, sums,
    ) = forward_pass(
        outer, live, shard, small, h_low, tokens, cotangent,
        jnp.broadcast_to(fraction[:, None], (rows, COLS)), vecs,
    )
    w_q, w_k, w_v, w_out = (w_one[i].reshape(model, model) for i in range(4))
    w_up, w_down = (w.reshape(4, model, model) for w in (w_up, w_down))
    heads, head = 4 * qv_bias.shape[0], 64
    slots = (z + jnp.arange(5, dtype=jnp.int32)) // 4
    meta = jnp.concatenate([slots, live])
    grad_gain_two, grad_shift_two, grad_down_bias = jnp.sum(sums, axis=1)
    grad_hidden = jnp.einsum("tm,prm->ptr", grad_f, w_down, preferred_element_type=F32)
    grad_pre = (grad_hidden * slope.astype(F32)).astype(BF)
    grad_up = jnp.einsum("ptr,tm->prm", grad_pre, y_low, preferred_element_type=F32).astype(BF)
    grad_down = jnp.einsum("ptr,tm->prm", hidden, grad_f, preferred_element_type=F32).astype(BF)
    grad_up_bias = jnp.sum(grad_pre.astype(F32), axis=1).reshape(-1)
    grad_y1 = grad_z2 + jnp.einsum("ptr,prm->tm", grad_pre, w_up, preferred_element_type=F32)
    grad_gain_one, grad_shift_one = jnp.sum(grad_y1 * xhat, axis=0), jnp.sum(grad_y1, axis=0)
    grad_z1 = norm_back(grad_y1, xhat, rstd[:, :1], gain_one)
    grad_a = grad_z1.astype(BF)
    grad_out_bias = jnp.sum(grad_a.astype(F32), axis=0)
    grad_attn = dot_nt(grad_a, w_out).astype(BF)
    grad_out_w = dot_tn(attn, grad_a).astype(BF)
    dq, dk, dv = attend_back(meta, queries, keys, values, grad_attn, lse, head)
    grad_qv_bias = jnp.stack(
        [
            jnp.sum(dq.astype(F32), axis=0).reshape(heads, head),
            jnp.sum(dv.astype(F32), axis=0).reshape(heads, head),
        ],
        axis=1,
    )
    dh_win = dot_nn(dk, w_k) + dot_nn(dv, w_v)
    dh_own = grad_z1 + dot_nn(dq, w_q)
    portion_two = jnp.repeat(lax.dynamic_slice(portion, (z,), (2,)), seq_len)
    grad_time_weight = jnp.sum(fraction[:, None] * dh_own, axis=0) + jnp.sum(
        portion_two[:, None] * dh_win, axis=0
    )
    grad_time_bias = jnp.sum(dh_own, axis=0) + jnp.sum(dh_win, axis=0)
    dh_own = dh_own + lax.dynamic_slice(dh_win, (z * step, 0), (rows, model))
    spread = model // (32 * outer)
    vectors = jnp.stack(
        [
            grad_time_weight, grad_time_bias, grad_out_bias, grad_gain_one, grad_shift_one,
            grad_down_bias, grad_gain_two, grad_shift_two,
        ]
    )
    packed = jnp.concatenate(
        [
            vectors.reshape(8, 8, outer, 4, spread).transpose(3, 1, 0, 2, 4).reshape(4, 8, -1),
            grad_up_bias.reshape(4, 4, 2, 8, 16).transpose(1, 3, 0, 2, 4).reshape(4, 8, -1),
            grad_qv_bias.reshape(4, 4, 8, 16).transpose(0, 2, 1, 3).reshape(4, 8, -1),
        ],
        axis=2,
    )
    n_vec = 8 * outer * spread
    packed = jnp.pad(packed, ((0, 0), (0, 0), (0, 8 * COLS - packed.shape[2])))
    packed = packed.reshape(4, 8, 8, COLS).transpose(0, 2, 1, 3).reshape(4, 8, 8 * COLS)
    square = (4, ROWS, model)
    tall = (4,) + square
    grads = (
        dot_tn(dq, h_low).astype(BF).reshape(square),
        dot_tn(dk, h_win).astype(BF).reshape(square),
        dot_tn(dv, h_win).astype(BF).reshape(square),
        grad_out_w.reshape(square),
        grad_up.reshape(tall),
        grad_down.reshape(tall),
    )
    done, small_done, halo_in = scatter_grads(outer, grads, packed, dh_win.astype(BF))
    local = jnp.arange(rows, dtype=jnp.int32)
    edge = (4 - z) * step
    reached = jnp.logical_or(
        jnp.logical_and(z <= 2, local >= edge), jnp.logical_and(z >= 1, local < edge)
    )
    grad_tokens = dh_own + jnp.where(reached[:, None], halo_in.astype(F32), 0.0)
    small_done = small_done.reshape(-1)
    results = [
        done[8:11].transpose(0, 2, 1),
        done[11],
        done[4:8].reshape(4 * ROWS, COLS),
        done[0:4].reshape(4 * ROWS, COLS),
        small_done[n_vec : n_vec + n_up].reshape(8, 16),
        small_done[n_vec + n_up : n_vec + n_up + n_qv].reshape(4, 16),
        small_done[:n_vec].reshape(8, outer * spread),
    ]
    if outer > 1:
        results = [
            lax.psum_scatter(g, "dp", scatter_dimension=1, tiled=True, axis_index_groups=groups)
            for g in results
        ]
    grad_qkv, grad_out_w, grad_up, grad_down, grad_up_bias, grad_qv_bias, vectors = results
    return (
        layer_out, grad_tokens, vectors[0], vectors[1], grad_qkv, grad_qv_bias,
        grad_out_w, vectors[2], vectors[3], vectors[4], grad_up, grad_up_bias,
        grad_down, vectors[5], vectors[6], vectors[7],
    )


def solution(mesh):
    outer = mesh.shape["dp"] // 8
    placed = (
        P(("dp", "mp"), None), P("dp"), P("dp"), P(), P(), P(None, "dp", "mp"), P("mp", "dp"), P("mp", "dp"),
        P(), P(), P(), P("mp", "dp"), P("mp", "dp"), P("mp", "dp"), P(), P(), P(), P(("dp", "mp"), None),
    )
    spread = P(("dp", "mp"))
    wide = P("mp", "dp")
    return jax.shard_map(
        functools.partial(body, outer),
        mesh=mesh,
        in_specs=placed,
        out_specs=(
            P(("dp", "mp"), None), P(("dp", "mp"), None), spread, spread, P(None, "dp", "mp"), wide, wide,
            spread, spread, spread, wide, wide, wide, spread, spread, spread,
        ),
        check_vma=False,
    )
```

```python
import functools
import math

import jax
import jax.numpy as jnp
from jax import lax
from jax.experimental import pallas as pl
from jax.experimental.pallas import tpu as pltpu
from jax.sharding import PartitionSpec as P

BLOCK = 25
TSTEPS = 5000
LN_EPS = 1e-05
MASKED = -1e30
MESH = pl.DeviceIdType.MESH
BF = jnp.bfloat16
F32 = jnp.float32
PIECES = 12
LANES = 4
ROWS = 256
COLS = 128
VMEM_LIMIT = 62 * 2**20


def dot_nn(left, right):
    return lax.dot_general(left, right, (((1,), (0,)), ((), ())), preferred_element_type=F32)


def dot_nt(left, right):
    return lax.dot_general(left, right, (((1,), (1,)), ((), ())), preferred_element_type=F32)


def dot_tn(left, right):
    return lax.dot_general(left, right, (((0,), (0,)), ((), ())), preferred_element_type=F32)


class Place:
    def __init__(self, outer):
        dp = lax.axis_index("dp")
        self.z = lax.axis_index("mp")
        self.outer = outer
        self.own = lax.div(dp, outer)
        self.rest = lax.rem(dp, outer)
        self.core = lax.rem(self.own, 2)
        self.chip = lax.div(self.own, 2)
        col, row = lax.rem(self.chip, 2), lax.div(self.chip, 2)
        self.side = row * 2 + (1 - col)
        self.over = (1 - row) * 2 + col
        self.diag = (1 - row) * 2 + (1 - col)

    def dev(self, chip, core, z):
        return ((chip * 2 + core) * self.outer + self.rest, z)

    def partner(self):
        return self.dev(self.chip, 1 - self.core, self.z)

    def beside(self):
        return self.dev(self.side, self.core, self.z)

    def across(self):
        return self.dev(self.over, self.core, self.z)

    def along(self, k):
        return self.dev(self.chip, self.core, lax.rem(self.z + k, 4))


def greet(at):
    barrier = pltpu.get_barrier_semaphore()
    peers = [at.partner(), at.beside(), at.across()] + [at.along(k) for k in range(1, 4)]
    for peer in peers:
        pl.semaphore_signal(barrier, inc=1, device_id=peer, device_id_type=MESH)
    pl.semaphore_wait(barrier, len(peers))


def wait_for(ref, sem):
    pltpu.make_async_copy(ref, ref, sem).wait()


def send(src, dst, send_sem, recv_sem, device):
    pltpu.make_async_remote_copy(
        src, dst, send_sem, recv_sem, device_id=device, device_id_type=MESH
    ).start()


def when_in(piece, count, action):
    @pl.when(jnp.logical_and(piece >= 0, piece < count))
    def _():
        action(piece)


def cols_of(lane):
    return pl.ds(pl.multiple_of(lane * COLS, COLS), COLS)


def tile_rows(start, size):
    return pl.ds(pl.multiple_of(start, 128), size)


def norm_rows(values_in):
    average = jnp.mean(values_in, axis=-1, keepdims=True)
    centred = values_in - average
    rstd = lax.rsqrt(jnp.mean(centred * centred, axis=-1, keepdims=True) + LN_EPS)
    return centred * rstd, rstd


def norm_back(grad, xhat, rstd, gain):
    scaled = grad * gain
    first = jnp.mean(scaled, axis=-1, keepdims=True)
    second = jnp.mean(scaled * xhat, axis=-1, keepdims=True)
    return rstd * (scaled - first - xhat * second)


def fold_rows(values_in):
    rows, model = values_in.shape
    return jnp.sum(values_in.reshape(rows // 8, 8, model), axis=0)


def forward_kernel(
    outer, live, shard, small, h, tokens, cotangent, fraction, vecs,
    w_one, w_up, w_down, small_full, h_win_out, q_out, k_out, v_out, attn_out, y_out, hidden_out, slope_out,
    xhat_out, dz_out, grad_f_out, layer_out, lse, rstd_out, sums,
    h_win, q, k, v, attn, y_low, hidden, slope, xhat, acc, pre, grad_f, out_rows, bias_in, bias, wbuf, v_t,
    own_sem, sent, got_z, got_x, got_y, got_xd, got_yd, got_c, halo_sent, halo_got, load_sem, store_sem, slope_sem,
):
    at = Place(outer)
    greet(at)
    z, rows, model = at.z, h.shape[0], h.shape[1]
    step = rows // 5
    groups = (w_one, w_up, w_down)
    x_lane, y_lane, d_lane = at.side * 2 + at.core, at.over * 2 + at.core, at.diag * 2 + at.core

    def source(p):
        return small if p is None else shard.at[pl.ds(p, 1)]

    def block(ref, lane, start, count):
        return ref.at[pl.ds(start, count), :, cols_of(lane)]

    def index(p):
        return PIECES if p is None else p

    def grouped(action):
        def run(p):
            if p is None:
                action(None, small_full)
                return
            if isinstance(p, int):
                action(p, groups[p // 4].at[p % 4])
                return
            for g, ref in enumerate(groups):
                @pl.when(lax.div(p, 4) == g)
                def _():
                    action(p, ref.at[p - 4 * g])

        return run

    def first(p, ref):
        i, src, dst = index(p), source(p), block(ref, at.own, z, 1)
        send(src, dst, sent.at[i], got_x.at[i], at.beside())
        send(src, dst, sent.at[i], got_y.at[i], at.across())
        for step_z in range(1, 4):
            send(src, dst, sent.at[i], got_z.at[i], at.along(step_z))
        send(src, dst, sent.at[i], got_c.at[i], at.partner())

    def second(p, ref):
        i = index(p)
        wait_for(block(ref, at.own, 0, 3), got_z.at[i])
        for step_z in range(1, 4):
            part = block(ref, at.own, lax.rem(z + step_z, 4), 1)
            send(part, part, sent.at[i], got_x.at[i], at.beside())
            send(part, part, sent.at[i], got_y.at[i], at.across())
            send(part, part, sent.at[i], got_c.at[i], at.partner())

    def third(p, ref):
        i = index(p)
        wait_for(block(ref, x_lane, 0, 4), got_x.at[i])
        part = block(ref, x_lane, 0, 2)
        send(part, part, sent.at[i], got_yd.at[i], at.across())
        part = block(ref, x_lane, 0, 4)
        send(part, part, sent.at[i], got_c.at[i], at.partner())
        wait_for(block(ref, y_lane, 0, 4), got_y.at[i])
        part = block(ref, y_lane, 2, 2)
        send(part, part, sent.at[i], got_xd.at[i], at.beside())
        part = block(ref, y_lane, 0, 4)
        send(part, part, sent.at[i], got_c.at[i], at.partner())

    def fourth(p, ref):
        i = index(p)
        wait_for(block(ref, d_lane, 0, 2), got_yd.at[i])
        wait_for(block(ref, d_lane, 2, 2), got_xd.at[i])
        part = block(ref, d_lane, 0, 4)
        send(part, part, sent.at[i], got_c.at[i], at.partner())

    def load(p, ref):
        slot = lax.rem(p, 3)
        return pltpu.make_async_copy(ref, wbuf.at[slot], load_sem.at[slot])

    def fifth(p, ref):
        wait_for(ref.at[:, :, 0 : 4 * COLS], got_c.at[index(p)])
        if p is None:
            pltpu.make_async_copy(small_full, bias_in, own_sem.at[1]).start()
        else:
            load(p, ref).start()

    def drain(p, ref):
        wait_for(ref.at[:, :, 0 : 7 * COLS], sent.at[index(p)])
        wait_for(ref.at[0:3, :, 0:COLS], sent.at[index(p)])

    first, second, third, fourth, fifth, drain = (
        grouped(action) for action in (first, second, third, fourth, fifth, drain)
    )

    def halo():
        for i in range(3):
            @pl.when(jnp.logical_and(z >= 1, z < 4 - i))
            def _():
                dst = h_win.at[tile_rows((4 + z + i) * step, step)]
                send(h.at[tile_rows(i * step, step)], dst, halo_sent, halo_got, at.along(3))

            @pl.when(jnp.logical_and(z <= 2, z >= i))
            def _():
                dst = h_win.at[tile_rows(i * step, step)]
                send(h.at[tile_rows((4 - z + i) * step, step)], dst, halo_sent, halo_got, at.along(1))

    mine = [
        pltpu.make_async_copy(
            shard.at[4 * g : 4 * g + 4], ref.at[:, z, :, cols_of(at.own)], own_sem.at[2 + g]
        )
        for g, ref in enumerate(groups)
    ] + [pltpu.make_async_copy(small, small_full.at[pl.ds(z, 1), :, cols_of(at.own)], own_sem.at[0])]
    stores = []

    def store(src, dst):
        pltpu.make_async_copy(src, dst, store_sem.at[len(stores)]).start()
        stores.append((src, dst))

    n_tiles = model // ROWS

    def tiles(action):
        def run(n, carry):
            action(n, tile_rows(n * ROWS, ROWS))
            return carry

        lax.fori_loop(0, n_tiles, run, 0)

    def weight(p):
        slot = lax.rem(p, 3)
        pltpu.make_async_copy(w_one.at[0], wbuf.at[slot], load_sem.at[slot]).wait()
        return slot

    def make_bias():
        pltpu.make_async_copy(small_full, bias_in, own_sem.at[1]).wait()
        total = bias_in[:, :, 0:COLS].astype(F32)
        for lane in range(1, 8):
            total = total + bias_in[:, :, lane * COLS : (lane + 1) * COLS].astype(F32)
        bias[...] = total

    def project(p, rows_in, target, bias_row):
        slot = weight(p)

        def one(n, span):
            result = dot_nt(rows_in[...], wbuf[slot, n])
            if bias_row is not None:
                result = result + jnp.concatenate(
                    [bias[n, bias_row : bias_row + 1], bias[n, bias_row + 1 : bias_row + 2]], axis=1
                )
            target[:, span] = result.astype(BF)

        tiles(one)

    def queries():
        make_bias()
        project(0, h, q, 8)
        store(q, q_out)

    def keys():
        wait_for(h_win.at[0 : 3 * step], halo_got)
        h_win[tile_rows(z * step, rows), :] = h[...]
        project(1, h_win, k, None)
        store(k, k_out)
        store(h_win, h_win_out)

    def values():
        project(2, h_win, v, 10)
        store(v, v_out)

    def attend_pairs(start, count):
        def pair(i, carry):
            lanes = cols_of(i)
            v_t[...] = v[:, lanes].T
            for j in range(5):
                slot = lax.div(z + j, 4)
                span = tile_rows(slot * 4 * step, 4 * step)
                here = slice(j * step, (j + 1) * step)
                q_two = split_heads(q[here, lanes] * jnp.asarray(0.125, BF))
                scores = masked_scores(k[span, lanes], q_two, jnp.where(slot == 0, live[0], live[1]))
                row_max = jnp.max(scores, axis=0, keepdims=True)
                expo = jnp.exp(scores - row_max)
                total = jnp.sum(expo, axis=0, keepdims=True)
                mixed = dot_nn(v_t[:, span], expo.astype(BF)) / total
                attn[here, lanes] = join_heads(mixed).astype(BF)
                lse[i, j : j + 1, :] = row_max + jnp.log(total)
            return carry

        lax.fori_loop(start, start + count, pair, 0)

    def row_loop(count, action):
        def run(i, carry):
            action(pl.ds(pl.multiple_of(i * count, count), count))
            return carry

        lax.fori_loop(0, rows // count, run, 0)

    def out_project():
        slot = weight(3)

        def one(n, span):
            wide = wbuf[slot, :, :, span].reshape(model, ROWS)
            acc[:, span] = dot_nn(attn[...], wide)

        tiles(one)
        store(attn, attn_out)

        def norm(here):
            h_zero = tokens[here, :].astype(F32) + fraction[here, 0:1] * vecs[0:1, :] + vecs[1:2, :]
            normal, rstd = norm_rows(h_zero + acc[here, :] + vecs[2:3, :])
            xhat[here, :] = normal
            y_low[here, :] = (normal * vecs[3:4, :] + vecs[4:5, :]).astype(BF)
            rstd_out[here, :] = jnp.broadcast_to(rstd, (rstd.shape[0], COLS))

        row_loop(32, norm)
        acc[...] = jnp.zeros_like(acc)
        store(y_low, y_out)
        store(xhat, xhat_out)

    def slope_store(i):
        slot = lax.rem(i, 2)
        return pltpu.make_async_copy(slope.at[slot], slope_out.at[i], slope_sem.at[slot])

    def hidden_store(i):
        return pltpu.make_async_copy(hidden.at[i], hidden_out.at[i], slope_sem.at[2 + i])

    def up_piece(p):
        i, slot = p - 4, weight(p)
        side = lax.rem(i, 2)

        @pl.when(i >= 2)
        def _():
            slope_store(i - 2).wait()

        def one(n, span):
            offset = jnp.concatenate([bias[n, pl.ds(2 * i, 1)], bias[n, pl.ds(2 * i + 1, 1)]], axis=1)
            pre[...] = dot_nt(y_low[...], wbuf[slot, n]) + offset

            def gelu(here):
                x = pre[here, :]
                cdf = 0.5 + 0.5 * lax.erf(x * math.sqrt(0.5))
                pdf = jnp.exp(x * x * -0.5) * (1.0 / math.sqrt(2.0 * math.pi))
                hidden[i, here, span] = (x * cdf).astype(BF)
                slope[side, here, span] = (cdf + x * pdf).astype(BF)

            row_loop(32, gelu)

        tiles(one)
        slope_store(i).start()
        hidden_store(i).start()

    def down_piece(p):
        i, slot = p - 8, weight(p)

        def one(n, span):
            wide = wbuf[slot, :, :, span].reshape(model, ROWS)
            acc[:, span] += dot_nn(hidden[i], wide)

        tiles(one)

    def finish():
        sums[...] = jnp.zeros_like(sums)

        def norm(here):
            y_one = xhat[here, :] * vecs[3:4, :] + vecs[4:5, :]
            normal, rstd = norm_rows(y_one + acc[here, :] + vecs[5:6, :])
            out_rows[here, :] = (normal * vecs[6:7, :] + vecs[7:8, :]).astype(BF)
            cot = cotangent[here, :].astype(F32)
            grad = norm_back(cot, normal, rstd, vecs[6:7, :])
            acc[here, :] = grad
            low = grad.astype(BF)
            grad_f[here, :] = low
            sums[0] += fold_rows(cot * normal)
            sums[1] += fold_rows(cot)
            sums[2] += fold_rows(low.astype(F32))

        row_loop(32, norm)
        store(acc, dz_out)
        store(grad_f, grad_f_out)
        store(out_rows, layer_out)

    first(None)
    first(0)
    first(1)
    halo()
    for copy in mine:
        copy.start()
    stages = ((second, 0), (third, -1), (fourth, -2), (fifth, -3))
    work = {
        4: (queries,),
        5: (keys,),
        6: (values, lambda: attend_pairs(0, 2)),
        7: (lambda: attend_pairs(2, 4),),
        8: (lambda: attend_pairs(6, 2), out_project),
    }

    def tick(t, carry):
        @pl.when(t == 3)
        def _():
            for copy in mine:
                copy.wait()

        for action, shift in ((first, 2),) + stages:
            when_in(t + shift, PIECES, action)
        for action, shift in stages:
            @pl.when(t == -shift)
            def _():
                action(None)
        for when, actions in work.items():
            @pl.when(t == when)
            def _():
                for action in actions:
                    action()

        @pl.when(jnp.logical_and(t >= 9, t < 13))
        def _():
            up_piece(t - 5)

        @pl.when(t >= 13)
        def _():
            down_piece(t - 5)

        return carry

    lax.fori_loop(0, PIECES + 5, tick, 0)
    finish()
    middle = jnp.logical_and(z >= 1, z <= 2)

    @pl.when(middle)
    def _():
        wait_for(h.at[0 : 5 * step], halo_sent)

    @pl.when(jnp.logical_not(middle))
    def _():
        wait_for(h.at[0:step], halo_sent)

    def drain_one(p, carry):
        drain(p)
        return carry

    lax.fori_loop(0, PIECES, drain_one, 0)
    drain(None)
    slope_store(2).wait()
    slope_store(3).wait()
    for i in range(4):
        hidden_store(i).wait()
    for i, (src, dst) in enumerate(stores):
        pltpu.make_async_copy(src, dst, store_sem.at[i]).wait()


def forward_pass(outer, live, shard, small, h, tokens, cotangent, fraction, vecs):
    sem = pltpu.SemaphoreType.DMA
    rows, model = h.shape
    win = rows // 5 * 8
    weights = jax.ShapeDtypeStruct((4, 4, ROWS, model), BF)
    own = jax.ShapeDtypeStruct((rows, model), BF)
    own_wide = jax.ShapeDtypeStruct((rows, model), F32)
    window = jax.ShapeDtypeStruct((win, model), BF)
    tall = jax.ShapeDtypeStruct((4, rows, model), BF)
    anywhere, vmem = pl.BlockSpec(memory_space=pl.ANY), pl.BlockSpec(memory_space=pltpu.VMEM)
    return pl.pallas_call(
        functools.partial(forward_kernel, outer),
        out_shape=(
            weights, weights, weights, jax.ShapeDtypeStruct((4, 16, model), BF),
            window, own, window, window, own, own, tall, tall, own_wide, own_wide, own, own,
            jax.ShapeDtypeStruct((8, 8, 2 * rows // 5), F32),
            jax.ShapeDtypeStruct((rows, COLS), F32),
            jax.ShapeDtypeStruct((3, 8, model), F32),
        ),
        in_specs=[pl.BlockSpec(memory_space=pltpu.SMEM)] + [vmem] * 7,
        out_specs=[anywhere] * 16 + [vmem] * 3,
        scratch_shapes=[
            pltpu.VMEM((win, model), BF),
            pltpu.VMEM((rows, model), BF),
            pltpu.VMEM((win, model), BF),
            pltpu.VMEM((win, model), BF),
            pltpu.VMEM((rows, model), BF),
            pltpu.VMEM((rows, model), BF),
            pltpu.VMEM((4, rows, model), BF),
            pltpu.VMEM((2, rows, model), BF),
            pltpu.VMEM((rows, model), F32),
            pltpu.VMEM((rows, model), F32),
            pltpu.VMEM((rows, ROWS), F32),
            pltpu.VMEM((rows, model), BF),
            pltpu.VMEM((rows, model), BF),
            pltpu.VMEM((4, 16, model), BF),
            pltpu.VMEM((4, 16, COLS), F32),
            pltpu.VMEM((3, 4, ROWS, model), BF),
            pltpu.VMEM((COLS, win), BF),
            sem((5,)),
        ]
        + [sem((PIECES + 1,))] * 7
        + [sem, sem, sem((3,)), sem((10,)), sem((6,))],
        compiler_params=pltpu.CompilerParams(
            collective_id=1, has_side_effects=True, vmem_limit_bytes=VMEM_LIMIT
        ),
        name="forward",
    )(live, shard, small, h, tokens, cotangent, fraction, vecs)


def split_heads(rows):
    low = lax.broadcasted_iota(jnp.int32, rows.shape, 1) < rows.shape[1] // 2
    zero = jnp.zeros_like(rows)
    return jnp.concatenate([jnp.where(low, rows, zero), jnp.where(low, zero, rows)], axis=0)


def join_heads(both):
    half = both.shape[1] // 2
    low = lax.broadcasted_iota(jnp.int32, (both.shape[0], half), 0) < both.shape[0] // 2
    return jnp.where(low, both[:, :half], both[:, half:]).T


def masked_scores(keys, q_two, live):
    scores = dot_nt(keys, q_two)
    return jnp.where(lax.broadcasted_iota(jnp.int32, scores.shape, 0) < live, scores, MASKED)


def backward_kernel(
    outer, live, portion, w_one, w_up, w_down, h_win_in, q_in, k_in, v_in, attn_in, y_in, hidden_in, slope_in,
    xhat_in, dz_in, grad_f_in, lse, rstd, vecs, sums_in,
    out, sums_out, tokens_out, pieces,
    part, lane, got_c, got_dx, got_dy, got_x, got_y, got_z,
    wbuf, hidden, slope, y_low, grad_f, acc, xhat, attn, q, k, v, h_win, dk_acc, dv_acc, k_t, dh_low, halo_in,
    dtile, wide_tile, stage, stats, s_sum, s_got,
    part_sem, sent0, sent1, sent2, sent3, sem_c, sem_dx, sem_dy, sem_x, sem_y, sem_z,
    in_sem, hidden_sem, weight_sem, stage_sem, token_sem, halo_sent, halo_got, small_sent, small_got, credit,
):
    at = Place(outer)
    greet(at)
    z, rows, model = at.z, q.shape[0], q.shape[1]
    step = rows // 5
    n_tiles = model // ROWS

    inputs = [
        (grad_f_in, grad_f), (y_in, y_low), (dz_in, acc), (xhat_in, xhat), (attn_in, attn),
        (q_in, q), (k_in, k), (v_in, v), (h_win_in, h_win),
    ]

    def get(i):
        src, dst = inputs[i]
        return pltpu.make_async_copy(src, dst, in_sem.at[i])

    def get_hidden(i):
        slot = lax.rem(i, 2)
        return (
            pltpu.make_async_copy(hidden_in.at[i], hidden.at[slot], hidden_sem.at[slot]),
            pltpu.make_async_copy(slope_in.at[i], slope.at[slot], hidden_sem.at[2 + slot]),
        )

    def get_weight(ref, slot):
        return pltpu.make_async_copy(ref, wbuf.at[slot], weight_sem.at[slot])

    def put_piece(p):
        return pltpu.make_async_copy(stage, pieces.at[p], stage_sem)

    def get_part(p):
        slot = lax.rem(p, 2)
        return pltpu.make_async_copy(pieces.at[p], part.at[slot], part_sem.at[slot])

    def first(p):
        slot = lax.rem(p, 2)
        get_part(p).wait()

        @pl.when(p >= 2)
        def _():
            pl.semaphore_wait(credit, 1)

        for a in range(4):
            src = part.at[slot, :, :, cols_of(a * 2 + 1 - at.core)]
            send(src, got_c.at[slot, a], sent0.at[p], sem_c.at[p], at.partner())

    def second(p):
        slot, row = lax.rem(p, 2), lax.rem(p, LANES)
        wait_for(got_c.at[slot], sem_c.at[p])

        @pl.when(p >= LANES)
        def _():
            wait_for(lane.at[row, 0], sent1.at[p - LANES])
            wait_for(lane.at[row, 0:2], sent2.at[p - LANES])
            wait_for(lane.at[row, 0, 0:3], sent3.at[p - LANES])

        def add(i, carry):
            a, b = lax.div(i, 4), lax.rem(i, 4)
            lane[row, a, b] = part[slot, b, :, cols_of(a * 2 + at.core)] + got_c[slot, a, b]
            return carry

        lax.fori_loop(0, 16, add, 0)

        @pl.when(p < PIECES - 2)
        def _():
            pl.semaphore_signal(credit, inc=1, device_id=at.partner(), device_id_type=MESH)

        wait_for(got_c.at[slot], sent0.at[p])
        send(lane.at[row, at.diag, 0:2], got_dy.at[p], sent1.at[p], sem_dy.at[p], at.across())
        send(lane.at[row, at.diag, 2:4], got_dx.at[p], sent1.at[p], sem_dx.at[p], at.beside())

    def third(p):
        row = lax.rem(p, LANES)
        wait_for(got_dy.at[p], sem_dy.at[p])

        def add_y(i, carry):
            lane[row, at.side, i] = lane[row, at.side, i] + got_dy[p, i]
            return carry

        lax.fori_loop(0, 2, add_y, 0)
        send(lane.at[row, at.side], got_x.at[p], sent2.at[p], sem_x.at[p], at.beside())
        wait_for(got_dx.at[p], sem_dx.at[p])

        def add_x(i, carry):
            lane[row, at.over, i + 2] = lane[row, at.over, i + 2] + got_dx[p, i]
            return carry

        lax.fori_loop(0, 2, add_x, 0)
        send(lane.at[row, at.over], got_y.at[p], sent2.at[p], sem_y.at[p], at.across())

    def fourth(p):
        row = lax.rem(p, LANES)
        wait_for(got_x.at[p], sem_x.at[p])
        wait_for(got_y.at[p], sem_y.at[p])

        def add(i, carry):
            total = lane[row, at.chip, i].astype(F32) + got_x[p, i].astype(F32)
            lane[row, at.chip, i] = (total + got_y[p, i].astype(F32)).astype(BF)
            return carry

        lax.fori_loop(0, 4, add, 0)
        for far in range(1, 4):
            block = lane.at[row, at.chip, lax.rem(z + far, 4)]
            send(block, got_z.at[p, far - 1], sent3.at[p], sem_z.at[p], at.along(far))

    def fifth(p):
        row = lax.rem(p, LANES)
        wait_for(got_z.at[p], sem_z.at[p])
        total = lane[row, at.chip, z].astype(F32)
        for far in range(3):
            total = total + got_z[p, far].astype(F32)

        @pl.when(p < 8)
        def _():
            out[lax.rem(p, 2) * 4 + lax.div(p, 2)] = total

        @pl.when(p == 8)
        def _():
            out[8] = total

        @pl.when(p > 8)
        def _():
            out[20 - p] = total

    def tiles(action):
        def run(n, carry):
            action(n, tile_rows(n * ROWS, ROWS))
            return carry

        lax.fori_loop(0, n_tiles, run, 0)

    def row_loop(count, action):
        def run(i, carry):
            action(pl.ds(pl.multiple_of(i * count, count), count))
            return carry

        lax.fori_loop(0, rows // count, run, 0)

    def produce(p, left, right):
        def one(n, span):
            stage[n] = dot_tn(left[:, span], right()).astype(BF)

        tiles(one)
        put_piece(p).start()

    def grad_down(i):
        @pl.when(i == 0)
        def _():
            get(0).wait()

        for copy in get_hidden(i):
            copy.wait()

        @pl.when(i > 0)
        def _():
            put_piece(2 * i - 1).wait()

        produce(2 * i, hidden.at[lax.rem(i, 2)], lambda: grad_f[...])

    def grad_pre(i):
        slot = lax.rem(i, 2)
        get_weight(w_down.at[i], 0).wait()

        def one(n, span):
            dtile[...] = dot_nt(grad_f[...], wbuf[0, n])
            stats[8 + i, :, span] = jnp.zeros((8, ROWS), F32)

            def scale(here):
                low = (dtile[here, :] * slope[slot, here, span].astype(F32)).astype(BF)
                slope[slot, here, span] = low
                stats[8 + i, :, span] += fold_rows(low.astype(F32))

            row_loop(64, scale)

        tiles(one)

        @pl.when(i < 3)
        def _():
            get_weight(w_down.at[lax.rem(i + 1, 4)], 0).start()

        @pl.when(i == 3)
        def _():
            get_weight(w_one.at[3], 0).start()

    def grad_up(i):
        @pl.when(i == 0)
        def _():
            get(1).wait()

        put_piece(2 * i).wait()
        produce(2 * i + 1, slope.at[lax.rem(i, 2)], lambda: y_low[...])

    def grad_y(i):
        slot = lax.rem(i, 2)
        get_weight(w_up.at[i], 1).wait()

        @pl.when(i == 0)
        def _():
            get(2).wait()

        def one(n, span):
            wide = wbuf[1, :, :, span].reshape(model, ROWS)
            acc[:, span] += dot_nn(slope[slot], wide)

        tiles(one)

        @pl.when(i < 3)
        def _():
            get_weight(w_up.at[lax.rem(i + 1, 4)], 1).start()

        @pl.when(i == 3)
        def _():
            get_weight(w_one.at[1], 1).start()

        @pl.when(i < 2)
        def _():
            for copy in get_hidden(i + 2):
                copy.start()

    def feed_forward(u):
        i, kind = lax.div(u, 4), lax.rem(u, 4)
        for which, action in enumerate((grad_down, grad_pre, grad_up, grad_y)):
            @pl.when(kind == which)
            def _():
                action(i)

    def norm_one():
        get(3).wait()
        get(4).wait()
        stats[2] = jnp.zeros_like(stats[2])
        stats[3] = jnp.zeros_like(stats[2])
        stats[4] = jnp.zeros_like(stats[2])

        def back(here):
            grad, normal = acc[here, :], xhat[here, :]
            stats[3] += fold_rows(grad * normal)
            stats[4] += fold_rows(grad)
            grad = norm_back(grad, normal, rstd[here, 0:1], vecs[3:4, :])
            acc[here, :] = grad
            low = grad.astype(BF)
            grad_f[here, :] = low
            stats[2] += fold_rows(low.astype(F32))

        row_loop(32, back)
        put_piece(7).wait()
        produce(8, attn, lambda: grad_f[...])
        get_weight(w_one.at[3], 0).wait()

        def one(n, span):
            y_low[:, span] = dot_nt(grad_f[...], wbuf[0, n]).astype(BF)

        tiles(one)
        get_weight(w_one.at[2], 0).start()
        put_piece(8).wait()
        for i in range(5, 9):
            get(i).wait()

    def attend_pairs(start, count):
        def pair(i, carry):
            lanes = cols_of(i)
            k_t[...] = k[:, lanes].T
            dk_acc[...] = jnp.zeros_like(dk_acc)
            dv_acc[...] = jnp.zeros_like(dv_acc)
            total = jnp.zeros((8, COLS), F32)
            for j in range(5):
                slot = lax.div(z + j, 4)
                span = tile_rows(slot * 4 * step, 4 * step)
                here = slice(j * step, (j + 1) * step)
                q_two = split_heads(q[here, lanes] * jnp.asarray(0.125, BF))
                g_two = split_heads(y_low[here, lanes])
                scores = masked_scores(k[span, lanes], q_two, jnp.where(slot == 0, live[0], live[1]))
                probs = jnp.exp(scores - lse[i, j : j + 1, :])
                dv_acc[span, :] += dot_nn(probs.astype(BF), g_two)
                grad_p = dot_nt(v[span, lanes], g_two)
                inner = jnp.sum(probs * grad_p, axis=0, keepdims=True)
                grad_s = (probs * (grad_p - inner)).astype(BF)
                dk_acc[span, :] += dot_nn(grad_s, q_two)
                low = (join_heads(dot_nn(k_t[:, span], grad_s)) * 0.125).astype(BF)
                q[here, lanes] = low
                total = total + fold_rows(low.astype(F32))
            stats[12, :, lanes] = total
            low = dv_acc[...].astype(BF)
            v[:, lanes] = low
            stats[13, :, lanes] = fold_rows(low.astype(F32))
            k[:, lanes] = dk_acc[...].astype(BF)
            return carry

        lax.fori_loop(start, start + count, pair, 0)

    def grad_value():
        produce(9, v, lambda: h_win[...])
        put_piece(9).wait()

    def grad_key_query():
        produce(10, k, lambda: h_win[...])
        put_piece(10).wait()
        produce(11, q, lambda: h_win[tile_rows(z * step, rows), :])

    def share(slot):
        return jnp.where(slot == 0, portion[0], portion[1])

    def input_window():
        get_weight(w_one.at[1], 1).wait()
        get_weight(w_one.at[2], 0).wait()

        def one(n, span):
            wide_k = wbuf[1, :, :, span].reshape(model, ROWS)
            wide_v = wbuf[0, :, :, span].reshape(model, ROWS)
            wide_tile[...] = dot_nn(k[...], wide_k) + dot_nn(v[...], wide_v)
            dh_low[:, span] = wide_tile[...].astype(BF)
            low = fold_rows(wide_tile[0 : 4 * step, :])
            high = fold_rows(wide_tile[4 * step : 8 * step, :])
            stats[0, :, span] = low * portion[0] + high * portion[1]
            stats[1, :, span] = low + high

        tiles(one)
        get_weight(w_one.at[0], 1).start()
        put_piece(11).wait()

        for i in range(3):
            @pl.when(z > i)
            def _():
                src = dh_low.at[tile_rows(i * step, step)]
                dst = halo_in.at[tile_rows((5 - z + i) * step, step)]
                send(src, dst, halo_sent, halo_got, at.along(3))

            @pl.when(z < 3 - i)
            def _():
                src = dh_low.at[tile_rows((5 + z + i) * step, step)]
                dst = halo_in.at[tile_rows(i * step, step)]
                send(src, dst, halo_sent, halo_got, at.along(1))

    def input_own():
        get_weight(w_one.at[0], 1).wait()

        def one(n, span):
            acc[:, span] += dot_nn(q[...], wbuf[1, :, :, span].reshape(model, ROWS))
            for j in range(5):
                total = fold_rows(acc[j * step : (j + 1) * step, span])
                stats[0, :, span] += total * share(lax.div(z + j, 4))
                stats[1, :, span] += total

        tiles(one)
        for i, row in ((5, 2), (6, 0), (7, 1)):
            stats[i] = sums_in[row]
        for i in range(14):
            s_sum[0, i : i + 1, :] = jnp.sum(stats[i], axis=0, keepdims=True)
        s_sum[0, 14:16, :] = jnp.zeros((2, model), F32)

    small_peers = (at.partner, at.beside, at.across)

    def small_send(i):
        send(s_sum.at[i], s_got.at[i], small_sent.at[i], small_got.at[i], small_peers[i]())

    def small_add(i):
        wait_for(s_got.at[i], small_got.at[i])
        s_sum[i + 1] = s_sum[i] + s_got[i]

    def small_spread():
        for far in range(1, 4):
            send(s_sum.at[3], s_got.at[2 + far], small_sent.at[3], small_got.at[3], at.along(far))

    middle = jnp.logical_and(z >= 1, z <= 2)

    def put_tokens(j):
        block = slice(j * step, (j + 1) * step)
        return pltpu.make_async_copy(acc.at[block], tokens_out.at[block], token_sem.at[j])

    def finish_tokens():
        @pl.when(middle)
        def _():
            wait_for(halo_in.at[0 : 5 * step], halo_got)

        @pl.when(jnp.logical_not(middle))
        def _():
            wait_for(halo_in.at[0:step], halo_got)

        for j in range(5):
            block = slice(j * step, (j + 1) * step)
            acc[block, :] += dh_low[tile_rows((z + j) * step, step), :].astype(F32)
            upper = jnp.logical_and(z <= 2, j >= 4 - z)
            lower = jnp.logical_and(z >= 1, j < 4 - z)

            @pl.when(jnp.logical_or(upper, lower))
            def _():
                acc[block, :] += halo_in[block, :].astype(F32)

            put_tokens(j).start()

    get(0).start()
    for i in range(2):
        for copy in get_hidden(i):
            copy.start()
    get_weight(w_down.at[0], 0).start()
    for i in range(1, 3):
        get(i).start()
    get_weight(w_up.at[0], 1).start()
    for i in range(3, 9):
        get(i).start()
    work = {
        5: (norm_one,),
        6: (lambda: attend_pairs(0, 2),),
        7: (lambda: attend_pairs(2, 2),),
        8: (lambda: attend_pairs(4, 2),),
        9: (lambda: attend_pairs(6, 2), grad_value),
        10: (grad_key_query,),
        11: (input_window,),
        12: (input_own, lambda: small_send(0)),
        13: (lambda: small_add(0), lambda: small_send(1)),
        14: (lambda: small_add(1), lambda: small_send(2), finish_tokens),
        15: (lambda: small_add(2), small_spread),
    }

    def slot_run(s, carry):
        c = s - 1
        when_in(c, PIECES, lambda p: get_part(p).start())
        for action, shift in ((second, 1), (third, 2), (fourth, 3), (fifth, 4), (first, 0)):
            when_in(c - shift, PIECES, action)

        @pl.when(s < 6)
        def _():
            def sub_step(u, inner):
                when_in(3 * s + u, 16, feed_forward)
                return inner

            lax.fori_loop(0, 3, sub_step, 0)

        for when, actions in work.items():
            @pl.when(s == when)
            def _():
                for action in actions:
                    action()

        return carry

    lax.fori_loop(0, PIECES + 5, slot_run, 0)
    wait_for(s_got.at[3:6], small_got.at[3])
    sums_out[...] = s_sum[3] + s_got[3] + s_got[4] + s_got[5]
    for p in range(PIECES - LANES, PIECES):
        row = p % LANES
        wait_for(lane.at[row, 0], sent1.at[p])
        wait_for(lane.at[row, 0:2], sent2.at[p])
        wait_for(lane.at[row, 0, 0:3], sent3.at[p])
    for i in range(3):
        wait_for(s_sum.at[i], small_sent.at[i])
    wait_for(s_got.at[0:3], small_sent.at[3])
    wait_for(dh_low.at[0 : 3 * step], halo_sent)
    for j in range(5):
        put_tokens(j).wait()


def backward_pass(outer, live, portion, *arrays):
    sem = pltpu.SemaphoreType.DMA
    model = 8 * COLS
    rows = arrays[4].shape[0]
    win = rows // 5 * 8
    half = (4, 4, ROWS, COLS)
    anywhere, vmem = pl.BlockSpec(memory_space=pl.ANY), pl.BlockSpec(memory_space=pltpu.VMEM)
    return pl.pallas_call(
        functools.partial(backward_kernel, outer),
        out_shape=(
            jax.ShapeDtypeStruct((PIECES, ROWS, COLS), F32),
            jax.ShapeDtypeStruct((16, model), F32),
            jax.ShapeDtypeStruct((rows, model), F32),
            jax.ShapeDtypeStruct((PIECES, 4, ROWS, model), BF),
        ),
        in_specs=[pl.BlockSpec(memory_space=pltpu.SMEM)] * 2 + [anywhere] * 14 + [vmem] * 4,
        out_specs=[vmem, vmem, anywhere, anywhere],
        scratch_shapes=[
            pltpu.VMEM((2, 4, ROWS, model), BF),
            pltpu.VMEM((LANES,) + half, BF),
            pltpu.VMEM((2,) + half, BF),
            pltpu.VMEM((PIECES, 2, ROWS, COLS), BF),
            pltpu.VMEM((PIECES, 2, ROWS, COLS), BF),
            pltpu.VMEM((PIECES, 4, ROWS, COLS), BF),
            pltpu.VMEM((PIECES, 4, ROWS, COLS), BF),
            pltpu.VMEM((PIECES, 3, ROWS, COLS), BF),
            pltpu.VMEM((2, 4, ROWS, model), BF),
            pltpu.VMEM((2, rows, model), BF),
            pltpu.VMEM((2, rows, model), BF),
            pltpu.VMEM((rows, model), BF),
            pltpu.VMEM((rows, model), BF),
            pltpu.VMEM((rows, model), F32),
            pltpu.VMEM((rows, model), F32),
            pltpu.VMEM((rows, model), BF),
            pltpu.VMEM((rows, model), BF),
            pltpu.VMEM((win, model), BF),
            pltpu.VMEM((win, model), BF),
            pltpu.VMEM((win, model), BF),
            pltpu.VMEM((win, COLS), F32),
            pltpu.VMEM((win, COLS), F32),
            pltpu.VMEM((COLS, win), BF),
            pltpu.VMEM((win, model), BF),
            pltpu.VMEM((rows, model), BF),
            pltpu.VMEM((rows, ROWS), F32),
            pltpu.VMEM((win, ROWS), F32),
            pltpu.VMEM((4, ROWS, model), BF),
            pltpu.VMEM((14, 8, model), F32),
            pltpu.VMEM((4, 16, model), F32),
            pltpu.VMEM((6, 16, model), F32),
            sem((2,)),
        ]
        + [sem((PIECES,))] * 10
        + [
            sem((9,)), sem((4,)), sem((2,)), sem, sem((5,)), sem, sem, sem((4,)), sem((4,)),
            pltpu.SemaphoreType.REGULAR,
        ],
        compiler_params=pltpu.CompilerParams(
            collective_id=2, has_side_effects=True, vmem_limit_bytes=VMEM_LIMIT
        ),
        name="backward",
    )(live, portion, *arrays)


def body(
    outer, tokens, context, timestep, time_weight, time_bias, qkv_weight, qv_bias, out_weight, out_bias,
    gain_one, shift_one, up_weight, up_bias, down_weight, down_bias, gain_two, shift_two, cotangent,
):
    z = lax.axis_index("mp")
    rows, model = tokens.shape
    seqs = context.shape[0]
    seq_len = rows * 4 // seqs
    step = rows // 5
    groups = None
    if outer > 1:
        groups = [[i * outer + j for j in range(outer)] for i in range(8)]
        qkv_weight, out_weight, up_weight, down_weight, qv_bias, up_bias = (
            lax.all_gather(w, "dp", axis=1, tiled=True, axis_index_groups=groups)
            for w in (qkv_weight, out_weight, up_weight, down_weight, qv_bias, up_bias)
        )
    shard = jnp.concatenate(
        [
            qkv_weight.transpose(0, 2, 1),
            out_weight.reshape(1, ROWS, COLS),
            up_weight.reshape(4, ROWS, COLS),
            down_weight.reshape(4, ROWS, COLS),
        ]
    )
    own = lax.div(lax.axis_index("dp"), outer)
    n_up, n_qv = up_bias.size, qv_bias.size
    part = jnp.arange(COLS) // up_bias.shape[1]
    up_rows = jnp.where(part == own, jnp.tile(up_bias, (1, 8)), 0)
    qv_rows = jnp.where(part[:64] == own % 4, jnp.tile(qv_bias, (1, 4)), 0).reshape(2, COLS)
    none = jnp.zeros_like(qv_rows)
    q_rows, v_rows = jnp.where(own < 4, qv_rows, none), jnp.where(own < 4, none, qv_rows)
    small = jnp.concatenate([up_rows, q_rows, v_rows, none, none]).reshape(1, 16, COLS)
    row_ids = z * rows + jnp.arange(rows, dtype=jnp.int32)
    owner = (row_ids // seq_len)[:, None] == jnp.arange(seqs, dtype=jnp.int32)[None, :]
    portion = timestep.astype(F32) / TSTEPS
    fraction = jnp.sum(jnp.where(owner, portion[None, :], 0.0), axis=1)
    h_low = (tokens.astype(F32) + fraction[:, None] * time_weight + time_bias).astype(BF)
    live = lax.dynamic_slice((context + BLOCK).astype(jnp.int32), (z,), (2,))
    vecs = jnp.stack(
        [time_weight, time_bias, out_bias, gain_one, shift_one, down_bias, gain_two, shift_two]
    )
    (
        w_one, w_up, w_down, _, h_win, queries, keys, values, attn, y_low, hidden, slope, xhat, grad_z2,
        grad_f, layer_out, lse, rstd, sums,
    ) = forward_pass(
        outer, live, shard, small, h_low, tokens, cotangent,
        jnp.broadcast_to(fraction[:, None], (rows, COLS)), vecs,
    )
    done, totals, grad_tokens, _ = backward_pass(
        outer, live, lax.dynamic_slice(portion, (z,), (2,)), w_one, w_up, w_down, h_win, queries, keys,
        values, attn, y_low, hidden, slope, xhat, grad_z2, grad_f, lse, rstd, vecs, sums,
    )
    weight_grads = [
        done[9:12].transpose(0, 2, 1), done[8], done[4:8].reshape(4 * ROWS, COLS),
        done[0:4].reshape(4 * ROWS, COLS),
    ]
    if outer > 1:
        weight_grads = [
            lax.psum_scatter(g, "dp", scatter_dimension=1, tiled=True, axis_index_groups=groups)
            for g in weight_grads
        ]
        totals = lax.psum(totals, "dp", axis_index_groups=groups)
    grad_qkv, grad_out_w, grad_up, grad_down = weight_grads
    dp = lax.axis_index("dp")
    size = lax.axis_size("dp")
    spread = model // (4 * size)
    vectors = lax.dynamic_slice(totals, (0, (dp * 4 + z) * spread), (8, spread))
    grad_up_bias = lax.dynamic_slice(totals, (8, z * ROWS), (4, ROWS)).reshape(8, COLS)
    grad_up_bias = lax.dynamic_slice(grad_up_bias, (0, dp * (COLS // size)), (8, COLS // size))
    grad_qv_bias = totals[12:14].reshape(2, 16, 64).transpose(1, 0, 2).reshape(16, 2 * 64)
    grad_qv_bias = lax.dynamic_slice(grad_qv_bias, (z * 4, dp * (COLS // size)), (4, COLS // size))
    return (
        layer_out, grad_tokens, vectors[0], vectors[1], grad_qkv, grad_qv_bias,
        grad_out_w, vectors[2], vectors[3], vectors[4], grad_up, grad_up_bias,
        grad_down, vectors[5], vectors[6], vectors[7],
    )


def solution(mesh):
    outer = mesh.shape["dp"] // 8
    placed = (
        P(("dp", "mp"), None), P("dp"), P("dp"), P(), P(), P(None, "dp", "mp"), P("mp", "dp"), P("mp", "dp"),
        P(), P(), P(), P("mp", "dp"), P("mp", "dp"), P("mp", "dp"), P(), P(), P(), P(("dp", "mp"), None),
    )
    spread = P(("dp", "mp"))
    wide = P("mp", "dp")
    return jax.shard_map(
        functools.partial(body, outer),
        mesh=mesh,
        in_specs=placed,
        out_specs=(
            P(("dp", "mp"), None), P(("dp", "mp"), None), spread, spread, P(None, "dp", "mp"), wide, wide,
            spread, spread, spread, wide, wide, wide, spread, spread, spread,
        ),
        check_vma=False,
    )
```

```python
import functools
import math

import jax
import jax.numpy as jnp
from jax import lax
from jax.experimental import pallas as pl
from jax.experimental.pallas import tpu as pltpu
from jax.sharding import PartitionSpec as P

BLOCK = 25
TSTEPS = 5000
LN_EPS = 1e-05
MASKED = -1e30
MESH = pl.DeviceIdType.MESH
BF = jnp.bfloat16
F32 = jnp.float32
PIECES = 12
LANES = 4
PARTS = 5
ROWS = 256
COLS = 128
VMEM_LIMIT = 62 * 2**20


def dot_nn(left, right):
    return lax.dot_general(left, right, (((1,), (0,)), ((), ())), preferred_element_type=F32)


def dot_nt(left, right):
    return lax.dot_general(left, right, (((1,), (1,)), ((), ())), preferred_element_type=F32)


def dot_tn(left, right):
    return lax.dot_general(left, right, (((0,), (0,)), ((), ())), preferred_element_type=F32)


class Place:
    def __init__(self, outer):
        dp = lax.axis_index("dp")
        self.z = lax.axis_index("mp")
        self.outer = outer
        self.own = lax.div(dp, outer)
        self.rest = lax.rem(dp, outer)
        self.core = lax.rem(self.own, 2)
        self.chip = lax.div(self.own, 2)
        col, row = lax.rem(self.chip, 2), lax.div(self.chip, 2)
        self.side = row * 2 + (1 - col)
        self.over = (1 - row) * 2 + col
        self.diag = (1 - row) * 2 + (1 - col)

    def dev(self, chip, core, z):
        return ((chip * 2 + core) * self.outer + self.rest, z)

    def partner(self):
        return self.dev(self.chip, 1 - self.core, self.z)

    def beside(self):
        return self.dev(self.side, self.core, self.z)

    def across(self):
        return self.dev(self.over, self.core, self.z)

    def along(self, k):
        return self.dev(self.chip, self.core, lax.rem(self.z + k, 4))


def greet(at):
    barrier = pltpu.get_barrier_semaphore()
    peers = [at.partner(), at.beside(), at.across()] + [at.along(k) for k in range(1, 4)]
    for peer in peers:
        pl.semaphore_signal(barrier, inc=1, device_id=peer, device_id_type=MESH)
    pl.semaphore_wait(barrier, len(peers))


def wait_for(ref, sem):
    pltpu.make_async_copy(ref, ref, sem).wait()


def send(src, dst, send_sem, recv_sem, device):
    pltpu.make_async_remote_copy(
        src, dst, send_sem, recv_sem, device_id=device, device_id_type=MESH
    ).start()


def when_in(piece, count, action):
    @pl.when(jnp.logical_and(piece >= 0, piece < count))
    def _():
        action(piece)


def cols_of(lane):
    return pl.ds(pl.multiple_of(lane * COLS, COLS), COLS)


def load_lanes(src, dst, sem):
    for lane in range(8):
        pltpu.make_async_copy(src.at[lane], dst.at[:, :, lane * COLS : (lane + 1) * COLS], sem).start()


def tile_rows(start, size):
    return pl.ds(pl.multiple_of(start, 128), size)


def norm_rows(values_in):
    average = jnp.mean(values_in, axis=-1, keepdims=True)
    centred = values_in - average
    rstd = lax.rsqrt(jnp.mean(centred * centred, axis=-1, keepdims=True) + LN_EPS)
    return centred * rstd, rstd


def norm_back(grad, xhat, rstd, gain):
    scaled = grad * gain
    first = jnp.mean(scaled, axis=-1, keepdims=True)
    second = jnp.mean(scaled * xhat, axis=-1, keepdims=True)
    return rstd * (scaled - first - xhat * second)


def fold_rows(values_in):
    rows, model = values_in.shape
    return jnp.sum(values_in.reshape(rows // 8, 8, model), axis=0)


def forward_kernel(
    outer, context, timestep, shard_one, shard_up, shard_down, small, h, tokens, cotangent, vecs,
    w_one, w_up, w_down, small_full, h_win_out, q_out, k_out, v_out, attn_out, y_out, hidden_out, slope_out,
    xhat_out, dz_out, grad_f_out, layer_out, lse, rstd_out, sums,
    h_win, q, k, v, attn, y_low, hidden, slope, xhat, acc, pre, grad_f, out_rows, bias_in, bias, wbuf, v_t,
    own_sem, sent, got_z, got_x, got_y, got_xd, got_yd, got_c, halo_sent, halo_got, load_sem, store_sem, slope_sem,
):
    at = Place(outer)
    greet(at)
    z, rows, model = at.z, h.shape[0], h.shape[1]
    step = rows // 5
    groups = (w_one, w_up, w_down)
    x_lane, y_lane, d_lane = at.side * 2 + at.core, at.over * 2 + at.core, at.diag * 2 + at.core

    shards = (shard_one, shard_up, shard_down)

    def block(ref, lane, start, count):
        if ref is small_full:
            return ref.at[pl.ds(start, count), :, cols_of(lane)]
        return ref.at[lane, pl.ds(start, count)]

    def some(ref, lanes):
        return ref.at[:, :, 0 : lanes * COLS] if ref is small_full else ref.at[0:lanes]

    def index(p):
        return PIECES if p is None else p

    def grouped(action):
        def run(p):
            if p is None:
                action(None, small_full, small)
                return
            if isinstance(p, int):
                action(p, groups[p // 4].at[p % 4], shards[p // 4].at[pl.ds(p % 4, 1)])
                return
            for g, ref in enumerate(groups):
                @pl.when(lax.div(p, 4) == g)
                def _():
                    action(p, ref.at[p - 4 * g], shards[g].at[pl.ds(p - 4 * g, 1)])

        return run

    def first(p, ref, src):
        i, dst = index(p), block(ref, at.own, z, 1)
        send(src, dst, sent.at[i], got_x.at[i], at.beside())
        send(src, dst, sent.at[i], got_y.at[i], at.across())
        for step_z in range(1, 4):
            send(src, dst, sent.at[i], got_z.at[i], at.along(step_z))
        send(src, dst, sent.at[i], got_c.at[i], at.partner())

    def second(p, ref, _):
        i = index(p)
        wait_for(block(ref, at.own, 0, 3), got_z.at[i])
        for step_z in range(1, 4):
            part = block(ref, at.own, lax.rem(z + step_z, 4), 1)
            send(part, part, sent.at[i], got_x.at[i], at.beside())
            send(part, part, sent.at[i], got_y.at[i], at.across())
            send(part, part, sent.at[i], got_c.at[i], at.partner())

    def third(p, ref, _):
        i = index(p)
        wait_for(block(ref, x_lane, 0, 4), got_x.at[i])
        part = block(ref, x_lane, 0, 2)
        send(part, part, sent.at[i], got_yd.at[i], at.across())
        part = block(ref, x_lane, 0, 4)
        send(part, part, sent.at[i], got_c.at[i], at.partner())
        wait_for(block(ref, y_lane, 0, 4), got_y.at[i])
        part = block(ref, y_lane, 2, 2)
        send(part, part, sent.at[i], got_xd.at[i], at.beside())
        part = block(ref, y_lane, 0, 4)
        send(part, part, sent.at[i], got_c.at[i], at.partner())

    def fourth(p, ref, _):
        i = index(p)
        wait_for(block(ref, d_lane, 0, 2), got_yd.at[i])
        wait_for(block(ref, d_lane, 2, 2), got_xd.at[i])
        part = block(ref, d_lane, 0, 4)
        send(part, part, sent.at[i], got_c.at[i], at.partner())

    def fifth(p, ref, _):
        wait_for(some(ref, 4), got_c.at[index(p)])
        if p is None:
            pltpu.make_async_copy(small_full, bias_in, own_sem.at[1]).start()
        else:
            load_lanes(ref, wbuf.at[lax.rem(p, 3)], load_sem.at[lax.rem(p, 3)])

    def drain(p, ref, _):
        wait_for(some(ref, 7), sent.at[index(p)])
        wait_for(block(ref, 0, 0, 3), sent.at[index(p)])

    first, second, third, fourth, fifth, drain = (
        grouped(action) for action in (first, second, third, fourth, fifth, drain)
    )

    def halo(part):
        i, small_step = part // 2, step // 2

        def some_rows(start):
            first_row = start * step + part % 2 * small_step
            return pl.ds(pl.multiple_of(first_row, small_step), small_step)

        @pl.when(jnp.logical_and(z >= 1, z < 4 - i))
        def _():
            dst = h_win.at[some_rows(4 + z + i)]
            send(h.at[some_rows(i)], dst, halo_sent, halo_got, at.along(3))

        @pl.when(jnp.logical_and(z <= 2, z >= i))
        def _():
            send(h.at[some_rows(4 - z + i)], h_win.at[some_rows(i)], halo_sent, halo_got, at.along(1))

    mine = [
        pltpu.make_async_copy(shards[g], ref.at[:, at.own, z], own_sem.at[2 + g])
        for g, ref in enumerate(groups)
    ] + [pltpu.make_async_copy(small, small_full.at[pl.ds(z, 1), :, cols_of(at.own)], own_sem.at[0])]
    stores = []

    def store(src, dst):
        pltpu.make_async_copy(src, dst, store_sem.at[len(stores)]).start()
        stores.append((src, dst))

    n_tiles = model // ROWS

    def tiles(action):
        def run(n, carry):
            action(n, tile_rows(n * ROWS, ROWS))
            return carry

        lax.fori_loop(0, n_tiles, run, 0)

    def weight(p):
        slot = lax.rem(p, 3)
        wait_for(wbuf.at[slot], load_sem.at[slot])
        return slot

    def make_bias():
        pltpu.make_async_copy(small_full, bias_in, own_sem.at[1]).wait()
        total = bias_in[:, :, 0:COLS].astype(F32)
        for lane in range(1, 8):
            total = total + bias_in[:, :, lane * COLS : (lane + 1) * COLS].astype(F32)
        bias[...] = total

    def project(p, rows_in, target, bias_row):
        slot = weight(p)

        def one(n, span):
            result = dot_nt(rows_in[...], wbuf[slot, n])
            if bias_row is not None:
                result = result + jnp.concatenate(
                    [bias[n, bias_row : bias_row + 1], bias[n, bias_row + 1 : bias_row + 2]], axis=1
                )
            target[:, span] = result.astype(BF)

        tiles(one)

    def queries():
        make_bias()
        project(0, h, q, 8)
        store(q, q_out)

    def keys():
        wait_for(h_win.at[0 : 3 * step], halo_got)
        h_win[tile_rows(z * step, rows), :] = h[...]
        project(1, h_win, k, None)
        store(k, k_out)
        store(h_win, h_win_out)

    def values():
        project(2, h_win, v, 10)
        store(v, v_out)

    def attend_pairs(start, count):
        def pair(i, carry):
            lanes = cols_of(i)
            v_t[...] = v[:, lanes].T
            for j in range(5):
                slot = lax.div(z + j, 4)
                span = tile_rows(slot * 4 * step, 4 * step)
                here = slice(j * step, (j + 1) * step)
                q_two = split_heads(q[here, lanes] * jnp.asarray(0.125, BF))
                scores = masked_scores(k[span, lanes], q_two, context[z + slot] + BLOCK)
                row_max = jnp.max(scores, axis=0, keepdims=True)
                expo = jnp.exp(scores - row_max)
                total = jnp.sum(expo, axis=0, keepdims=True)
                mixed = dot_nn(v_t[:, span], expo.astype(BF)) / total
                attn[here, lanes] = join_heads(mixed).astype(BF)
                lse[i, j : j + 1, :] = row_max + jnp.log(total)
            return carry

        lax.fori_loop(start, start + count, pair, 0)

    def row_loop(count, action):
        def run(i, carry):
            action(pl.ds(pl.multiple_of(i * count, count), count))
            return carry

        lax.fori_loop(0, rows // count, run, 0)

    def out_project():
        slot = weight(3)

        def one(n, span):
            wide = wbuf[slot, :, :, span].reshape(model, ROWS)
            acc[:, span] = dot_nn(attn[...], wide)

        tiles(one)
        store(attn, attn_out)

        def norm(here, i):
            share = timestep[z + lax.div(z + lax.div(i * 32, step), 4)].astype(F32) * (1.0 / TSTEPS)
            h_zero = tokens[here, :].astype(F32) + share * vecs[0:1, :] + vecs[1:2, :]
            normal, rstd = norm_rows(h_zero + acc[here, :] + vecs[2:3, :])
            xhat[here, :] = normal
            y_low[here, :] = (normal * vecs[3:4, :] + vecs[4:5, :]).astype(BF)
            rstd_out[here, :] = jnp.broadcast_to(rstd, (rstd.shape[0], COLS))

        def run(i, carry):
            norm(pl.ds(pl.multiple_of(i * 32, 32), 32), i)
            return carry

        lax.fori_loop(0, rows // 32, run, 0)
        acc[...] = jnp.zeros_like(acc)
        store(y_low, y_out)
        store(xhat, xhat_out)

    def slope_store(i):
        slot = lax.rem(i, 2)
        return pltpu.make_async_copy(slope.at[slot], slope_out.at[i], slope_sem.at[slot])

    def hidden_store(i):
        return pltpu.make_async_copy(hidden.at[i], hidden_out.at[i], slope_sem.at[2 + i])

    def up_piece(p):
        i, slot = p - 4, weight(p)
        side = lax.rem(i, 2)

        @pl.when(i >= 2)
        def _():
            slope_store(i - 2).wait()

        def one(n, span):
            offset = jnp.concatenate([bias[n, pl.ds(2 * i, 1)], bias[n, pl.ds(2 * i + 1, 1)]], axis=1)
            pre[...] = dot_nt(y_low[...], wbuf[slot, n]) + offset

            def gelu(here):
                x = pre[here, :]
                cdf = 0.5 + 0.5 * lax.erf(x * math.sqrt(0.5))
                pdf = jnp.exp(x * x * -0.5) * (1.0 / math.sqrt(2.0 * math.pi))
                hidden[i, here, span] = (x * cdf).astype(BF)
                slope[side, here, span] = (cdf + x * pdf).astype(BF)

            row_loop(32, gelu)

        tiles(one)
        slope_store(i).start()
        hidden_store(i).start()

    def down_piece(p):
        i, slot = p - 8, weight(p)

        def one(n, span):
            wide = wbuf[slot, :, :, span].reshape(model, ROWS)
            acc[:, span] += dot_nn(hidden[i], wide)

        tiles(one)

    def finish():
        sums[...] = jnp.zeros_like(sums)

        def norm(here):
            y_one = xhat[here, :] * vecs[3:4, :] + vecs[4:5, :]
            normal, rstd = norm_rows(y_one + acc[here, :] + vecs[5:6, :])
            out_rows[here, :] = (normal * vecs[6:7, :] + vecs[7:8, :]).astype(BF)
            cot = cotangent[here, :].astype(F32)
            grad = norm_back(cot, normal, rstd, vecs[6:7, :])
            acc[here, :] = grad
            low = grad.astype(BF)
            grad_f[here, :] = low
            sums[0] += fold_rows(cot * normal)
            sums[1] += fold_rows(cot)
            sums[2] += fold_rows(low.astype(F32))

        row_loop(32, norm)
        store(acc, dz_out)
        store(grad_f, grad_f_out)
        store(out_rows, layer_out)

    first(None)
    first(0)
    first(1)
    for copy in mine:
        copy.start()
    stages = ((second, 0), (third, -1), (fourth, -2), (fifth, -3))
    work = {
        4: (queries,),
        5: (keys,),
        6: (values, lambda: attend_pairs(0, 2)),
        7: (lambda: attend_pairs(2, 4),),
        8: (lambda: attend_pairs(6, 2), out_project),
    }

    def tick(t, carry):
        @pl.when(t == 3)
        def _():
            for copy in mine:
                copy.wait()

        for action, shift in ((first, 2),) + stages:
            when_in(t + shift, PIECES, action)
        for action, shift in stages:
            @pl.when(t == -shift)
            def _():
                action(None)
        for part in range(6):
            @pl.when(t == min(part, 4))
            def _():
                halo(part)
        for when, actions in work.items():
            @pl.when(t == when)
            def _():
                for action in actions:
                    action()

        @pl.when(jnp.logical_and(t >= 9, t < 13))
        def _():
            up_piece(t - 5)

        for i in range(2):
            when_in(2 * (t - 13) + i - 1, 4, lambda n: down_piece(n + 8))
        return carry

    lax.fori_loop(0, PIECES + 4, tick, 0)
    finish()
    middle = jnp.logical_and(z >= 1, z <= 2)

    @pl.when(middle)
    def _():
        wait_for(h.at[0 : 5 * step], halo_sent)

    @pl.when(jnp.logical_not(middle))
    def _():
        wait_for(h.at[0:step], halo_sent)

    def drain_one(p, carry):
        drain(p)
        return carry

    lax.fori_loop(0, PIECES, drain_one, 0)
    drain(None)
    slope_store(2).wait()
    slope_store(3).wait()
    for i in range(4):
        hidden_store(i).wait()
    for i, (src, dst) in enumerate(stores):
        pltpu.make_async_copy(src, dst, store_sem.at[i]).wait()


def forward_pass(outer, context, timestep, *arrays):
    sem = pltpu.SemaphoreType.DMA
    rows, model = arrays[4].shape
    win = rows // 5 * 8
    weights = jax.ShapeDtypeStruct((4, 8, 4, ROWS, COLS), BF)
    own = jax.ShapeDtypeStruct((rows, model), BF)
    own_wide = jax.ShapeDtypeStruct((rows, model), F32)
    window = jax.ShapeDtypeStruct((win, model), BF)
    tall = jax.ShapeDtypeStruct((4, rows, model), BF)
    anywhere, vmem = pl.BlockSpec(memory_space=pl.ANY), pl.BlockSpec(memory_space=pltpu.VMEM)
    return pl.pallas_call(
        functools.partial(forward_kernel, outer),
        out_shape=(
            weights, weights, weights, jax.ShapeDtypeStruct((4, 16, model), BF),
            window, own, window, window, own, own, tall, tall, own_wide, own_wide, own, own,
            jax.ShapeDtypeStruct((8, 8, 2 * rows // 5), F32),
            jax.ShapeDtypeStruct((rows, COLS), F32),
            jax.ShapeDtypeStruct((3, 8, model), F32),
        ),
        in_specs=[pl.BlockSpec(memory_space=pltpu.SMEM)] * 2 + [vmem] * 8,
        out_specs=[anywhere] * 16 + [vmem] * 3,
        scratch_shapes=[
            pltpu.VMEM((win, model), BF),
            pltpu.VMEM((rows, model), BF),
            pltpu.VMEM((win, model), BF),
            pltpu.VMEM((win, model), BF),
            pltpu.VMEM((rows, model), BF),
            pltpu.VMEM((rows, model), BF),
            pltpu.VMEM((4, rows, model), BF),
            pltpu.VMEM((2, rows, model), BF),
            pltpu.VMEM((rows, model), F32),
            pltpu.VMEM((rows, model), F32),
            pltpu.VMEM((rows, ROWS), F32),
            pltpu.VMEM((rows, model), BF),
            pltpu.VMEM((rows, model), BF),
            pltpu.VMEM((4, 16, model), BF),
            pltpu.VMEM((4, 16, COLS), F32),
            pltpu.VMEM((3, 4, ROWS, model), BF),
            pltpu.VMEM((COLS, win), BF),
            sem((5,)),
        ]
        + [sem((PIECES + 1,))] * 7
        + [sem, sem, sem((3,)), sem((10,)), sem((6,))],
        compiler_params=pltpu.CompilerParams(
            collective_id=1, has_side_effects=True, vmem_limit_bytes=VMEM_LIMIT
        ),
        name="forward",
    )(context, timestep, *arrays)


def split_heads(rows):
    low = lax.broadcasted_iota(jnp.int32, rows.shape, 1) < rows.shape[1] // 2
    zero = jnp.zeros_like(rows)
    return jnp.concatenate([jnp.where(low, rows, zero), jnp.where(low, zero, rows)], axis=0)


def join_heads(both):
    half = both.shape[1] // 2
    low = lax.broadcasted_iota(jnp.int32, (both.shape[0], half), 0) < both.shape[0] // 2
    return jnp.where(low, both[:, :half], both[:, half:]).T


def masked_scores(keys, q_two, live):
    scores = dot_nt(keys, q_two)
    return jnp.where(lax.broadcasted_iota(jnp.int32, scores.shape, 0) < live, scores, MASKED)


def backward_kernel(
    outer, context, timestep, w_one, w_up, w_down, h_win_in, q_in, k_in, v_in, attn_in, y_in, hidden_in, slope_in,
    xhat_in, dz_in, grad_f_in, lse, rstd, vecs, sums_in,
    out_down, out_up, out_one, out_qkv, sums_out, tokens_out,
    part, lane, got_c, got_dx, got_dy, got_x, got_y, got_z,
    wbuf, hidden, slope, y_low, grad_f, acc, xhat, attn, q, k, v, h_win, dk_acc, dv_acc, k_t, halo_in,
    dtile, wide_tile, stats, s_sum, s_got,
    sent0, sent1, sent2, sent3, sem_c, sem_dx, sem_dy, sem_x, sem_y, sem_z,
    in_sem, hidden_sem, weight_sem, token_sem, halo_sent, halo_got, small_sent, small_got, credit,
):
    at = Place(outer)
    greet(at)
    z, rows, model = at.z, q.shape[0], q.shape[1]
    step = rows // 5
    n_tiles = model // ROWS

    inputs = [
        (grad_f_in, grad_f), (y_in, y_low), (dz_in, acc), (xhat_in, xhat), (attn_in, attn),
        (q_in, q), (k_in, k), (v_in, v), (h_win_in, h_win),
    ]

    def get(i):
        src, dst = inputs[i]
        return pltpu.make_async_copy(src, dst, in_sem.at[i])

    def get_hidden(i):
        slot = lax.rem(i, 2)
        return (
            pltpu.make_async_copy(hidden_in.at[i], hidden.at[slot], hidden_sem.at[slot]),
            pltpu.make_async_copy(slope_in.at[i], slope.at[slot], hidden_sem.at[2 + slot]),
        )

    def get_weight(ref, slot):
        load_lanes(ref, wbuf.at[slot], weight_sem.at[slot])

    def have_weight(slot):
        wait_for(wbuf.at[slot], weight_sem.at[slot])

    def share(slot):
        return timestep[z + slot].astype(F32) * (1.0 / TSTEPS)

    def first(p):
        slot, src_slot = lax.rem(p, 2), lax.rem(p, PARTS)

        @pl.when(p >= 2)
        def _():
            pl.semaphore_wait(credit, 1)

        for a in range(4):
            src = part.at[src_slot, :, :, cols_of(a * 2 + 1 - at.core)]
            send(src, got_c.at[slot, a], sent0.at[p], sem_c.at[p], at.partner())

    def second(p):
        slot, row, src_slot = lax.rem(p, 2), lax.rem(p, LANES), lax.rem(p, PARTS)
        wait_for(got_c.at[slot], sem_c.at[p])

        @pl.when(p >= LANES)
        def _():
            wait_for(lane.at[row, 0], sent1.at[p - LANES])
            wait_for(lane.at[row, 0:2], sent2.at[p - LANES])
            wait_for(lane.at[row, 0, 0:3], sent3.at[p - LANES])

        def add(i, carry):
            a, b = lax.div(i, 4), lax.rem(i, 4)
            lane[row, a, b] = part[src_slot, b, :, cols_of(a * 2 + at.core)] + got_c[slot, a, b]
            return carry

        lax.fori_loop(0, 16, add, 0)

        @pl.when(p < PIECES - 2)
        def _():
            pl.semaphore_signal(credit, inc=1, device_id=at.partner(), device_id_type=MESH)

        wait_for(got_c.at[slot], sent0.at[p])
        send(lane.at[row, at.diag, 0:2], got_dy.at[p], sent1.at[p], sem_dy.at[p], at.across())
        send(lane.at[row, at.diag, 2:4], got_dx.at[p], sent1.at[p], sem_dx.at[p], at.beside())

    def third(p):
        row = lax.rem(p, LANES)
        wait_for(got_dy.at[p], sem_dy.at[p])

        def add_y(i, carry):
            lane[row, at.side, i] = lane[row, at.side, i] + got_dy[p, i]
            return carry

        lax.fori_loop(0, 2, add_y, 0)
        send(lane.at[row, at.side], got_x.at[p], sent2.at[p], sem_x.at[p], at.beside())
        wait_for(got_dx.at[p], sem_dx.at[p])

        def add_x(i, carry):
            lane[row, at.over, i + 2] = lane[row, at.over, i + 2] + got_dx[p, i]
            return carry

        lax.fori_loop(0, 2, add_x, 0)
        send(lane.at[row, at.over], got_y.at[p], sent2.at[p], sem_y.at[p], at.across())

    def fourth(p):
        row = lax.rem(p, LANES)
        wait_for(got_x.at[p], sem_x.at[p])
        wait_for(got_y.at[p], sem_y.at[p])

        def add(i, carry):
            total = lane[row, at.chip, i].astype(F32) + got_x[p, i].astype(F32)
            lane[row, at.chip, i] = (total + got_y[p, i].astype(F32)).astype(BF)
            return carry

        lax.fori_loop(0, 4, add, 0)
        for far in range(1, 4):
            block = lane.at[row, at.chip, lax.rem(z + far, 4)]
            send(block, got_z.at[p, far - 1], sent3.at[p], sem_z.at[p], at.along(far))

    def fifth(p):
        row = lax.rem(p, LANES)
        wait_for(got_z.at[p], sem_z.at[p])
        total = lane[row, at.chip, z].astype(F32)
        for far in range(3):
            total = total + got_z[p, far].astype(F32)


        @pl.when(jnp.logical_and(p < 8, lax.rem(p, 2) == 0))
        def _():
            out_down[lax.rem(lax.div(p, 2), 4)] = total

        @pl.when(jnp.logical_and(p < 8, lax.rem(p, 2) == 1))
        def _():
            out_up[lax.rem(lax.div(p, 2), 4)] = total

        @pl.when(p == 8)
        def _():
            out_one[...] = total

        @pl.when(p > 8)
        def _():
            out_qkv[11 - p] = total.T

    def tiles(action):
        def run(n, carry):
            action(n, tile_rows(n * ROWS, ROWS))
            return carry

        lax.fori_loop(0, n_tiles, run, 0)

    def row_loop(count, action):
        def run(i, carry):
            action(pl.ds(pl.multiple_of(i * count, count), count))
            return carry

        lax.fori_loop(0, rows // count, run, 0)

    def produce(p, left, right):
        slot = lax.rem(p, PARTS)

        def one(n, span):
            part[slot, n] = dot_tn(left[:, span], right()).astype(BF)

        tiles(one)

    def grad_down(i):
        @pl.when(i == 0)
        def _():
            get(0).wait()

        for copy in get_hidden(i):
            copy.wait()

        produce(2 * i, hidden.at[lax.rem(i, 2)], lambda: grad_f[...])

    def grad_pre(i):
        slot = lax.rem(i, 2)
        have_weight(0)

        def one(n, span):
            dtile[...] = dot_nt(grad_f[...], wbuf[0, n])
            stats[8 + i, :, span] = jnp.zeros((8, ROWS), F32)

            def scale(here):
                low = (dtile[here, :] * slope[slot, here, span].astype(F32)).astype(BF)
                slope[slot, here, span] = low
                stats[8 + i, :, span] += fold_rows(low.astype(F32))

            row_loop(64, scale)

        tiles(one)

        @pl.when(i < 3)
        def _():
            get_weight(w_down.at[lax.rem(i + 1, 4)], 0)

        @pl.when(i == 3)
        def _():
            get_weight(w_one.at[3], 0)

    def grad_up(i):
        @pl.when(i == 0)
        def _():
            get(1).wait()

        produce(2 * i + 1, slope.at[lax.rem(i, 2)], lambda: y_low[...])

    def grad_y(i):
        slot = lax.rem(i, 2)
        have_weight(1)

        @pl.when(i == 0)
        def _():
            get(2).wait()

        def one(n, span):
            wide = wbuf[1, :, :, span].reshape(model, ROWS)
            acc[:, span] += dot_nn(slope[slot], wide)

        tiles(one)

        @pl.when(i < 3)
        def _():
            get_weight(w_up.at[lax.rem(i + 1, 4)], 1)

        @pl.when(i == 3)
        def _():
            get_weight(w_one.at[1], 1)

        @pl.when(i < 2)
        def _():
            for copy in get_hidden(i + 2):
                copy.start()

    def feed_forward(u):
        i, kind = lax.div(u, 4), lax.rem(u, 4)
        for which, action in enumerate((grad_down, grad_pre, grad_up, grad_y)):
            @pl.when(kind == which)
            def _():
                action(i)

    def norm_one():
        get(3).wait()
        get(4).wait()
        stats[2] = jnp.zeros_like(stats[2])
        stats[3] = jnp.zeros_like(stats[2])
        stats[4] = jnp.zeros_like(stats[2])

        def back(here):
            grad, normal = acc[here, :], xhat[here, :]
            stats[3] += fold_rows(grad * normal)
            stats[4] += fold_rows(grad)
            grad = norm_back(grad, normal, rstd[here, 0:1], vecs[3:4, :])
            acc[here, :] = grad
            low = grad.astype(BF)
            grad_f[here, :] = low
            stats[2] += fold_rows(low.astype(F32))

        row_loop(32, back)

    def grad_out():
        produce(8, attn, lambda: grad_f[...])
        have_weight(0)

        def one(n, span):
            y_low[:, span] = dot_nt(grad_f[...], wbuf[0, n]).astype(BF)

        tiles(one)
        get_weight(w_one.at[2], 0)
        for i in range(5, 9):
            get(i).wait()

    def attend_pairs(start, count):
        def pair(i, carry):
            lanes = cols_of(i)
            k_t[...] = k[:, lanes].T
            dk_acc[...] = jnp.zeros_like(dk_acc)
            dv_acc[...] = jnp.zeros_like(dv_acc)
            total = jnp.zeros((8, COLS), F32)
            for j in range(5):
                slot = lax.div(z + j, 4)
                span = tile_rows(slot * 4 * step, 4 * step)
                here = slice(j * step, (j + 1) * step)
                q_two = split_heads(q[here, lanes] * jnp.asarray(0.125, BF))
                g_two = split_heads(y_low[here, lanes])
                scores = masked_scores(k[span, lanes], q_two, context[z + slot] + BLOCK)
                probs = jnp.exp(scores - lse[i, j : j + 1, :])
                dv_acc[span, :] += dot_nn(probs.astype(BF), g_two)
                grad_p = dot_nt(v[span, lanes], g_two)
                inner = jnp.sum(probs * grad_p, axis=0, keepdims=True)
                grad_s = (probs * (grad_p - inner)).astype(BF)
                dk_acc[span, :] += dot_nn(grad_s, q_two)
                low = (join_heads(dot_nn(k_t[:, span], grad_s)) * 0.125).astype(BF)
                q[here, lanes] = low
                total = total + fold_rows(low.astype(F32))
            stats[12, :, lanes] = total
            low = dv_acc[...].astype(BF)
            v[:, lanes] = low
            stats[13, :, lanes] = fold_rows(low.astype(F32))
            k[:, lanes] = dk_acc[...].astype(BF)
            return carry

        lax.fori_loop(start, start + count, pair, 0)

    def grad_value():
        produce(9, v, lambda: h_win[...])

    def grad_key_query():
        produce(10, k, lambda: h_win[...])
        produce(11, q, lambda: h_win[tile_rows(z * step, rows), :])

    def input_window():
        have_weight(1)
        have_weight(0)

        def one(n, span):
            wide_k = wbuf[1, :, :, span].reshape(model, ROWS)
            wide_v = wbuf[0, :, :, span].reshape(model, ROWS)
            wide_tile[...] = dot_nn(k[...], wide_k) + dot_nn(v[...], wide_v)
            h_win[:, span] = wide_tile[...].astype(BF)
            low = fold_rows(wide_tile[0 : 4 * step, :])
            high = fold_rows(wide_tile[4 * step : 8 * step, :])
            stats[0, :, span] = low * share(0) + high * share(1)
            stats[1, :, span] = low + high

        tiles(one)
        get_weight(w_one.at[0], 1)

        for i in range(3):
            @pl.when(z > i)
            def _():
                src = h_win.at[tile_rows(i * step, step)]
                dst = halo_in.at[tile_rows((5 - z + i) * step, step)]
                send(src, dst, halo_sent, halo_got, at.along(3))

            @pl.when(z < 3 - i)
            def _():
                src = h_win.at[tile_rows((5 + z + i) * step, step)]
                dst = halo_in.at[tile_rows(i * step, step)]
                send(src, dst, halo_sent, halo_got, at.along(1))

    def input_own():
        have_weight(1)

        def one(n, span):
            acc[:, span] += dot_nn(q[...], wbuf[1, :, :, span].reshape(model, ROWS))
            for j in range(5):
                total = fold_rows(acc[j * step : (j + 1) * step, span])
                stats[0, :, span] += total * share(lax.div(z + j, 4))
                stats[1, :, span] += total

        tiles(one)
        for i, row in ((5, 2), (6, 0), (7, 1)):
            stats[i] = sums_in[row]
        for i in range(14):
            s_sum[0, i : i + 1, :] = jnp.sum(stats[i], axis=0, keepdims=True)
        s_sum[0, 14:16, :] = jnp.zeros((2, model), F32)

    small_peers = (at.partner, at.beside, at.across)

    def small_send(i):
        send(s_sum.at[i], s_got.at[i], small_sent.at[i], small_got.at[i], small_peers[i]())

    def small_add(i):
        wait_for(s_got.at[i], small_got.at[i])
        s_sum[i + 1] = s_sum[i] + s_got[i]

    def small_spread():
        for far in range(1, 4):
            send(s_sum.at[3], s_got.at[2 + far], small_sent.at[3], small_got.at[3], at.along(far))

    middle = jnp.logical_and(z >= 1, z <= 2)

    def put_tokens(j):
        block = slice(j * step, (j + 1) * step)
        return pltpu.make_async_copy(acc.at[block], tokens_out.at[block], token_sem.at[j])

    def finish_tokens():
        @pl.when(middle)
        def _():
            wait_for(halo_in.at[0 : 5 * step], halo_got)

        @pl.when(jnp.logical_not(middle))
        def _():
            wait_for(halo_in.at[0:step], halo_got)

        for j in range(5):
            block = slice(j * step, (j + 1) * step)
            acc[block, :] += h_win[tile_rows((z + j) * step, step), :].astype(F32)
            upper = jnp.logical_and(z <= 2, j >= 4 - z)
            lower = jnp.logical_and(z >= 1, j < 4 - z)

            @pl.when(jnp.logical_or(upper, lower))
            def _():
                acc[block, :] += halo_in[block, :].astype(F32)

            put_tokens(j).start()

    get(0).start()
    for i in range(2):
        for copy in get_hidden(i):
            copy.start()
    get_weight(w_down.at[0], 0)
    for i in range(1, 3):
        get(i).start()
    get_weight(w_up.at[0], 1)
    for i in range(3, 9):
        get(i).start()
    work = {
        5: (norm_one,),
        6: (grad_out, lambda: attend_pairs(0, 1)),
        7: (lambda: attend_pairs(1, 3),),
        8: (lambda: attend_pairs(4, 3),),
        9: (lambda: attend_pairs(7, 1), grad_value),
        10: (grad_key_query,),
        11: (input_window,),
        12: (input_own, lambda: small_send(0)),
        13: (lambda: small_add(0), lambda: small_send(1)),
        14: (lambda: small_add(1), lambda: small_send(2), finish_tokens),
        15: (lambda: small_add(2), small_spread),
    }

    def slot_run(s, carry):
        c = s - 1
        for action, shift in ((second, 1), (third, 2), (fourth, 3), (fifth, 4), (first, 0)):
            when_in(c - shift, PIECES, action)

        def sub_step(u, inner):
            when_in(3 * s - 2 + u, 16, feed_forward)
            return inner

        lax.fori_loop(0, 3, sub_step, 0)

        for when, actions in work.items():
            @pl.when(s == when)
            def _():
                for action in actions:
                    action()

        return carry

    lax.fori_loop(0, PIECES + 5, slot_run, 0)
    wait_for(s_got.at[3:6], small_got.at[3])
    sums_out[...] = s_sum[3] + s_got[3] + s_got[4] + s_got[5]
    for p in range(PIECES - LANES, PIECES):
        row = p % LANES
        wait_for(lane.at[row, 0], sent1.at[p])
        wait_for(lane.at[row, 0:2], sent2.at[p])
        wait_for(lane.at[row, 0, 0:3], sent3.at[p])
    for i in range(3):
        wait_for(s_sum.at[i], small_sent.at[i])
    wait_for(s_got.at[0:3], small_sent.at[3])
    wait_for(h_win.at[0 : 3 * step], halo_sent)
    for j in range(5):
        put_tokens(j).wait()


def backward_pass(outer, context, timestep, *arrays):
    sem = pltpu.SemaphoreType.DMA
    model = 8 * COLS
    rows = arrays[4].shape[0]
    win = rows // 5 * 8
    half = (4, 4, ROWS, COLS)
    anywhere, vmem = pl.BlockSpec(memory_space=pl.ANY), pl.BlockSpec(memory_space=pltpu.VMEM)
    return pl.pallas_call(
        functools.partial(backward_kernel, outer),
        out_shape=(
            jax.ShapeDtypeStruct((4, ROWS, COLS), F32),
            jax.ShapeDtypeStruct((4, ROWS, COLS), F32),
            jax.ShapeDtypeStruct((ROWS, COLS), F32),
            jax.ShapeDtypeStruct((3, COLS, ROWS), F32),
            jax.ShapeDtypeStruct((16, model), F32),
            jax.ShapeDtypeStruct((rows, model), F32),
        ),
        in_specs=[pl.BlockSpec(memory_space=pltpu.SMEM)] * 2 + [anywhere] * 14 + [vmem] * 4,
        out_specs=[vmem] * 5 + [anywhere],
        scratch_shapes=[
            pltpu.VMEM((PARTS, 4, ROWS, model), BF),
            pltpu.VMEM((LANES,) + half, BF),
            pltpu.VMEM((2,) + half, BF),
            pltpu.VMEM((PIECES, 2, ROWS, COLS), BF),
            pltpu.VMEM((PIECES, 2, ROWS, COLS), BF),
            pltpu.VMEM((PIECES, 4, ROWS, COLS), BF),
            pltpu.VMEM((PIECES, 4, ROWS, COLS), BF),
            pltpu.VMEM((PIECES, 3, ROWS, COLS), BF),
            pltpu.VMEM((2, 4, ROWS, model), BF),
            pltpu.VMEM((2, rows, model), BF),
            pltpu.VMEM((2, rows, model), BF),
            pltpu.VMEM((rows, model), BF),
            pltpu.VMEM((rows, model), BF),
            pltpu.VMEM((rows, model), F32),
            pltpu.VMEM((rows, model), F32),
            pltpu.VMEM((rows, model), BF),
            pltpu.VMEM((rows, model), BF),
            pltpu.VMEM((win, model), BF),
            pltpu.VMEM((win, model), BF),
            pltpu.VMEM((win, model), BF),
            pltpu.VMEM((win, COLS), F32),
            pltpu.VMEM((win, COLS), F32),
            pltpu.VMEM((COLS, win), BF),
            pltpu.VMEM((rows, model), BF),
            pltpu.VMEM((rows, ROWS), F32),
            pltpu.VMEM((win, ROWS), F32),
            pltpu.VMEM((14, 8, model), F32),
            pltpu.VMEM((4, 16, model), F32),
            pltpu.VMEM((6, 16, model), F32),
        ]
        + [sem((PIECES,))] * 10
        + [
            sem((9,)), sem((4,)), sem((2,)), sem((5,)), sem, sem, sem((4,)), sem((4,)),
            pltpu.SemaphoreType.REGULAR,
        ],
        compiler_params=pltpu.CompilerParams(
            collective_id=2, has_side_effects=True, vmem_limit_bytes=VMEM_LIMIT
        ),
        name="backward",
    )(context, timestep, *arrays)


def body(
    outer, tokens, context, timestep, time_weight, time_bias, qkv_weight, qv_bias, out_weight, out_bias,
    gain_one, shift_one, up_weight, up_bias, down_weight, down_bias, gain_two, shift_two, cotangent,
):
    z = lax.axis_index("mp")
    rows, model = tokens.shape
    seqs = context.shape[0]
    seq_len = rows * 4 // seqs
    step = rows // 5
    groups = None
    if outer > 1:
        groups = [[i * outer + j for j in range(outer)] for i in range(8)]
        qkv_weight, out_weight, up_weight, down_weight, qv_bias, up_bias = (
            lax.all_gather(w, "dp", axis=1, tiled=True, axis_index_groups=groups)
            for w in (qkv_weight, out_weight, up_weight, down_weight, qv_bias, up_bias)
        )
    shard_one = jnp.concatenate([qkv_weight.transpose(0, 2, 1), out_weight.reshape(1, ROWS, COLS)])
    shard_up, shard_down = (w.reshape(4, ROWS, COLS) for w in (up_weight, down_weight))
    own = lax.div(lax.axis_index("dp"), outer)
    n_up, n_qv = up_bias.size, qv_bias.size
    part = jnp.arange(COLS) // up_bias.shape[1]
    up_rows = jnp.where(part == own, jnp.tile(up_bias, (1, 8)), 0)
    qv_rows = jnp.where(part[:64] == own % 4, jnp.tile(qv_bias, (1, 4)), 0).reshape(2, COLS)
    none = jnp.zeros_like(qv_rows)
    q_rows, v_rows = jnp.where(own < 4, qv_rows, none), jnp.where(own < 4, none, qv_rows)
    small = jnp.concatenate([up_rows, q_rows, v_rows, none, none]).reshape(1, 16, COLS)
    row_ids = z * rows + jnp.arange(rows, dtype=jnp.int32)
    owner = (row_ids // seq_len)[:, None] == jnp.arange(seqs, dtype=jnp.int32)[None, :]
    portion = timestep.astype(F32) / TSTEPS
    fraction = jnp.sum(jnp.where(owner, portion[None, :], 0.0), axis=1)
    h_low = (tokens.astype(F32) + fraction[:, None] * time_weight + time_bias).astype(BF)
    vecs = jnp.stack(
        [time_weight, time_bias, out_bias, gain_one, shift_one, down_bias, gain_two, shift_two]
    )
    (
        w_one, w_up, w_down, _, h_win, queries, keys, values, attn, y_low, hidden, slope, xhat, grad_z2,
        grad_f, layer_out, lse, rstd, sums,
    ) = forward_pass(
        outer, context, timestep, shard_one, shard_up, shard_down, small, h_low, tokens, cotangent, vecs,
    )
    grad_down, grad_up, grad_out_w, grad_qkv, totals, grad_tokens = backward_pass(
        outer, context, timestep, w_one, w_up, w_down, h_win, queries, keys,
        values, attn, y_low, hidden, slope, xhat, grad_z2, grad_f, lse, rstd, vecs, sums,
    )
    weight_grads = [
        grad_qkv, grad_out_w, grad_up.reshape(4 * ROWS, COLS), grad_down.reshape(4 * ROWS, COLS)
    ]
    if outer > 1:
        weight_grads = [
            lax.psum_scatter(g, "dp", scatter_dimension=1, tiled=True, axis_index_groups=groups)
            for g in weight_grads
        ]
        totals = lax.psum(totals, "dp", axis_index_groups=groups)
    grad_qkv, grad_out_w, grad_up, grad_down = weight_grads
    dp = lax.axis_index("dp")
    size = lax.axis_size("dp")
    spread = model // (4 * size)
    vectors = lax.dynamic_slice(totals, (0, (dp * 4 + z) * spread), (8, spread))
    grad_up_bias = lax.dynamic_slice(totals, (8, z * ROWS), (4, ROWS)).reshape(8, COLS)
    grad_up_bias = lax.dynamic_slice(grad_up_bias, (0, dp * (COLS // size)), (8, COLS // size))
    grad_qv_bias = totals[12:14].reshape(2, 16, 64).transpose(1, 0, 2).reshape(16, 2 * 64)
    grad_qv_bias = lax.dynamic_slice(grad_qv_bias, (z * 4, dp * (COLS // size)), (4, COLS // size))
    return (
        layer_out, grad_tokens, vectors[0], vectors[1], grad_qkv, grad_qv_bias,
        grad_out_w, vectors[2], vectors[3], vectors[4], grad_up, grad_up_bias,
        grad_down, vectors[5], vectors[6], vectors[7],
    )


def solution(mesh):
    outer = mesh.shape["dp"] // 8
    placed = (
        P(("dp", "mp"), None), P("dp"), P("dp"), P(), P(), P(None, "dp", "mp"), P("mp", "dp"), P("mp", "dp"),
        P(), P(), P(), P("mp", "dp"), P("mp", "dp"), P("mp", "dp"), P(), P(), P(), P(("dp", "mp"), None),
    )
    spread = P(("dp", "mp"))
    wide = P("mp", "dp")
    return jax.shard_map(
        functools.partial(body, outer),
        mesh=mesh,
        in_specs=placed,
        out_specs=(
            P(("dp", "mp"), None), P(("dp", "mp"), None), spread, spread, P(None, "dp", "mp"), wide, wide,
            spread, spread, spread, wide, wide, wide, spread, spread, spread,
        ),
        check_vma=False,
    )
```

```python
import functools
import math

import jax
import jax.numpy as jnp
from jax import lax
from jax.experimental import pallas as pl
from jax.experimental.pallas import tpu as pltpu
from jax.sharding import PartitionSpec as P

BLOCK = 25
TSTEPS = 5000
LN_EPS = 1e-05
MASKED = -1e30
MESH = pl.DeviceIdType.MESH
BF = jnp.bfloat16
F32 = jnp.float32
PIECES = 12
LANES = 4
PARTS = 5
ROWS = 256
COLS = 128
VMEM_LIMIT = 62 * 2**20


def dot_nn(left, right):
    return lax.dot_general(left, right, (((1,), (0,)), ((), ())), preferred_element_type=F32)


def dot_nt(left, right):
    return lax.dot_general(left, right, (((1,), (1,)), ((), ())), preferred_element_type=F32)


def dot_tn(left, right):
    return lax.dot_general(left, right, (((0,), (0,)), ((), ())), preferred_element_type=F32)


class Place:
    def __init__(self, outer):
        dp = lax.axis_index("dp")
        self.z = lax.axis_index("mp")
        self.outer = outer
        self.own = lax.div(dp, outer)
        self.rest = lax.rem(dp, outer)
        self.core = lax.rem(self.own, 2)
        self.chip = lax.div(self.own, 2)
        col, row = lax.rem(self.chip, 2), lax.div(self.chip, 2)
        self.side = row * 2 + (1 - col)
        self.over = (1 - row) * 2 + col
        self.diag = (1 - row) * 2 + (1 - col)

    def dev(self, chip, core, z):
        return ((chip * 2 + core) * self.outer + self.rest, z)

    def partner(self):
        return self.dev(self.chip, 1 - self.core, self.z)

    def beside(self):
        return self.dev(self.side, self.core, self.z)

    def across(self):
        return self.dev(self.over, self.core, self.z)

    def along(self, k):
        return self.dev(self.chip, self.core, lax.rem(self.z + k, 4))


def greet(at):
    barrier = pltpu.get_barrier_semaphore()
    peers = [at.partner(), at.beside(), at.across()] + [at.along(k) for k in range(1, 4)]
    for peer in peers:
        pl.semaphore_signal(barrier, inc=1, device_id=peer, device_id_type=MESH)
    pl.semaphore_wait(barrier, len(peers))


def wait_for(ref, sem):
    pltpu.make_async_copy(ref, ref, sem).wait()


def send(src, dst, send_sem, recv_sem, device):
    pltpu.make_async_remote_copy(
        src, dst, send_sem, recv_sem, device_id=device, device_id_type=MESH
    ).start()


def when_in(piece, count, action):
    @pl.when(jnp.logical_and(piece >= 0, piece < count))
    def _():
        action(piece)


def cols_of(lane):
    return pl.ds(pl.multiple_of(lane * COLS, COLS), COLS)


def load_lanes(src, dst, sem):
    for lane in range(8):
        pltpu.make_async_copy(src.at[lane], dst.at[:, :, lane * COLS : (lane + 1) * COLS], sem).start()


def tile_rows(start, size):
    return pl.ds(pl.multiple_of(start, 128), size)


def norm_rows(values_in):
    average = jnp.mean(values_in, axis=-1, keepdims=True)
    centred = values_in - average
    rstd = lax.rsqrt(jnp.mean(centred * centred, axis=-1, keepdims=True) + LN_EPS)
    return centred * rstd, rstd


def norm_back(grad, xhat, rstd, gain):
    scaled = grad * gain
    first = jnp.mean(scaled, axis=-1, keepdims=True)
    second = jnp.mean(scaled * xhat, axis=-1, keepdims=True)
    return rstd * (scaled - first - xhat * second)


def fold_rows(values_in):
    rows, model = values_in.shape
    return jnp.sum(values_in.reshape(rows // 8, 8, model), axis=0)


def forward_kernel(
    outer, context, timestep, shard_one, shard_up, shard_down, small, h, tokens, cotangent, vecs,
    w_one, w_up, w_down, small_full, h_win_out, q_out, k_out, v_out, attn_out, y_out, hidden_out, slope_out,
    xhat_out, dz_out, grad_f_out, layer_out, lse, rstd_out, sums,
    h_win, q, k, v, attn, y_low, hidden, slope, xhat, acc, pre, grad_f, out_rows, bias_in, bias, wbuf, v_t,
    own_sem, sent, got_z, got_x, got_y, got_xd, got_yd, got_c, halo_sent, halo_got, load_sem, store_sem, slope_sem,
):
    at = Place(outer)
    greet(at)
    z, rows, model = at.z, h.shape[0], h.shape[1]
    step = rows // 5
    groups = (w_one, w_up, w_down)
    x_lane, y_lane, d_lane = at.side * 2 + at.core, at.over * 2 + at.core, at.diag * 2 + at.core

    shards = (shard_one, shard_up, shard_down)

    def block(ref, lane, start, count):
        if ref is small_full:
            return ref.at[pl.ds(start, count), :, cols_of(lane)]
        return ref.at[lane, pl.ds(start, count)]

    def some(ref, lanes):
        return ref.at[:, :, 0 : lanes * COLS] if ref is small_full else ref.at[0:lanes]

    def index(p):
        return PIECES if p is None else p

    def grouped(action):
        def run(p):
            if p is None:
                action(None, small_full, small)
                return
            if isinstance(p, int):
                action(p, groups[p // 4].at[p % 4], shards[p // 4].at[pl.ds(p % 4, 1)])
                return
            for g, ref in enumerate(groups):
                @pl.when(lax.div(p, 4) == g)
                def _():
                    action(p, ref.at[p - 4 * g], shards[g].at[pl.ds(p - 4 * g, 1)])

        return run

    def first(p, ref, src):
        i, dst = index(p), block(ref, at.own, z, 1)
        send(src, dst, sent.at[i], got_x.at[i], at.beside())
        send(src, dst, sent.at[i], got_y.at[i], at.across())
        for step_z in range(1, 4):
            send(src, dst, sent.at[i], got_z.at[i], at.along(step_z))
        send(src, dst, sent.at[i], got_c.at[i], at.partner())

    def second(p, ref, _):
        i = index(p)
        wait_for(block(ref, at.own, 0, 3), got_z.at[i])
        for step_z in range(1, 4):
            part = block(ref, at.own, lax.rem(z + step_z, 4), 1)
            send(part, part, sent.at[i], got_x.at[i], at.beside())
            send(part, part, sent.at[i], got_y.at[i], at.across())
            send(part, part, sent.at[i], got_c.at[i], at.partner())

    def third(p, ref, _):
        i = index(p)
        wait_for(block(ref, x_lane, 0, 4), got_x.at[i])
        part = block(ref, x_lane, 0, 2)
        send(part, part, sent.at[i], got_yd.at[i], at.across())
        part = block(ref, x_lane, 0, 4)
        send(part, part, sent.at[i], got_c.at[i], at.partner())
        wait_for(block(ref, y_lane, 0, 4), got_y.at[i])
        part = block(ref, y_lane, 2, 2)
        send(part, part, sent.at[i], got_xd.at[i], at.beside())
        part = block(ref, y_lane, 0, 4)
        send(part, part, sent.at[i], got_c.at[i], at.partner())

    def fourth(p, ref, _):
        i = index(p)
        wait_for(block(ref, d_lane, 0, 2), got_yd.at[i])
        wait_for(block(ref, d_lane, 2, 2), got_xd.at[i])
        part = block(ref, d_lane, 0, 4)
        send(part, part, sent.at[i], got_c.at[i], at.partner())

    def fifth(p, ref, _):
        wait_for(some(ref, 4), got_c.at[index(p)])
        if p is None:
            pltpu.make_async_copy(small_full, bias_in, own_sem.at[1]).start()
        else:
            load_lanes(ref, wbuf.at[lax.rem(p, 3)], load_sem.at[lax.rem(p, 3)])

    def drain(p, ref, _):
        wait_for(some(ref, 7), sent.at[index(p)])
        wait_for(block(ref, 0, 0, 3), sent.at[index(p)])

    first, second, third, fourth, fifth, drain = (
        grouped(action) for action in (first, second, third, fourth, fifth, drain)
    )

    def halo(part):
        i, small_step = part // 2, step // 2

        def some_rows(start):
            first_row = start * step + part % 2 * small_step
            return pl.ds(pl.multiple_of(first_row, small_step), small_step)

        @pl.when(jnp.logical_and(z >= 1, z < 4 - i))
        def _():
            dst = h_win.at[some_rows(4 + z + i)]
            send(h.at[some_rows(i)], dst, halo_sent, halo_got, at.along(3))

        @pl.when(jnp.logical_and(z <= 2, z >= i))
        def _():
            send(h.at[some_rows(4 - z + i)], h_win.at[some_rows(i)], halo_sent, halo_got, at.along(1))

    mine = [
        pltpu.make_async_copy(shards[g], ref.at[:, at.own, z], own_sem.at[2 + g])
        for g, ref in enumerate(groups)
    ] + [pltpu.make_async_copy(small, small_full.at[pl.ds(z, 1), :, cols_of(at.own)], own_sem.at[0])]
    stores = []

    def store(src, dst):
        pltpu.make_async_copy(src, dst, store_sem.at[len(stores)]).start()
        stores.append((src, dst))

    n_tiles = model // ROWS

    def tiles(action):
        def run(n, carry):
            action(n, tile_rows(n * ROWS, ROWS))
            return carry

        lax.fori_loop(0, n_tiles, run, 0)

    def weight(p):
        slot = lax.rem(p, 3)
        wait_for(wbuf.at[slot], load_sem.at[slot])
        return slot

    def make_bias():
        pltpu.make_async_copy(small_full, bias_in, own_sem.at[1]).wait()
        total = bias_in[:, :, 0:COLS].astype(F32)
        for lane in range(1, 8):
            total = total + bias_in[:, :, lane * COLS : (lane + 1) * COLS].astype(F32)
        bias[...] = total

    def project(p, rows_in, target, bias_row):
        slot = weight(p)

        def one(n, span):
            result = dot_nt(rows_in[...], wbuf[slot, n])
            if bias_row is not None:
                result = result + jnp.concatenate(
                    [bias[n, bias_row : bias_row + 1], bias[n, bias_row + 1 : bias_row + 2]], axis=1
                )
            target[:, span] = result.astype(BF)

        tiles(one)

    def queries():
        make_bias()
        project(0, h, q, 8)
        store(q, q_out)

    def keys():
        wait_for(h_win.at[0 : 3 * step], halo_got)
        h_win[tile_rows(z * step, rows), :] = h[...]
        project(1, h_win, k, None)
        store(k, k_out)
        store(h_win, h_win_out)

    def values():
        project(2, h_win, v, 10)
        store(v, v_out)

    def attend_pairs(start, count):
        def pair(i, carry):
            lanes = cols_of(i)
            v_t[...] = v[:, lanes].T
            for j in range(5):
                slot = lax.div(z + j, 4)
                span = tile_rows(slot * 4 * step, 4 * step)
                here = slice(j * step, (j + 1) * step)
                q_two = split_heads(q[here, lanes] * jnp.asarray(0.125, BF))
                scores = masked_scores(k[span, lanes], q_two, context[z + slot] + BLOCK)
                row_max = jnp.max(scores, axis=0, keepdims=True)
                expo = jnp.exp(scores - row_max)
                total = jnp.sum(expo, axis=0, keepdims=True)
                mixed = dot_nn(v_t[:, span], expo.astype(BF)) / total
                attn[here, lanes] = join_heads(mixed).astype(BF)
                lse[i, j : j + 1, :] = row_max + jnp.log(total)
            return carry

        lax.fori_loop(start, start + count, pair, 0)

    def row_loop(count, action):
        def run(i, carry):
            action(pl.ds(pl.multiple_of(i * count, count), count))
            return carry

        lax.fori_loop(0, rows // count, run, 0)

    def out_project():
        slot = weight(3)

        def one(n, span):
            wide = wbuf[slot, :, :, span].reshape(model, ROWS)
            acc[:, span] = dot_nn(attn[...], wide)

        tiles(one)
        store(attn, attn_out)

        def norm(here, i):
            share = timestep[z + lax.div(z + lax.div(i * 32, step), 4)].astype(F32) * (1.0 / TSTEPS)
            h_zero = tokens[here, :].astype(F32) + share * vecs[0:1, :] + vecs[1:2, :]
            normal, rstd = norm_rows(h_zero + acc[here, :] + vecs[2:3, :])
            xhat[here, :] = normal
            y_low[here, :] = (normal * vecs[3:4, :] + vecs[4:5, :]).astype(BF)
            rstd_out[here, :] = jnp.broadcast_to(rstd, (rstd.shape[0], COLS))

        def run(i, carry):
            norm(pl.ds(pl.multiple_of(i * 32, 32), 32), i)
            return carry

        lax.fori_loop(0, rows // 32, run, 0)
        acc[...] = jnp.zeros_like(acc)
        store(y_low, y_out)
        store(xhat, xhat_out)

    def slope_store(i):
        slot = lax.rem(i, 2)
        return pltpu.make_async_copy(slope.at[slot], slope_out.at[i], slope_sem.at[slot])

    def hidden_store(i):
        return pltpu.make_async_copy(hidden.at[i], hidden_out.at[i], slope_sem.at[2 + i])

    def up_piece(p):
        i, slot = p - 4, weight(p)
        side = lax.rem(i, 2)

        @pl.when(i >= 2)
        def _():
            slope_store(i - 2).wait()

        def one(n, span):
            offset = jnp.concatenate([bias[n, pl.ds(2 * i, 1)], bias[n, pl.ds(2 * i + 1, 1)]], axis=1)
            pre[...] = dot_nt(y_low[...], wbuf[slot, n]) + offset

            def gelu(here):
                x = pre[here, :]
                cdf = 0.5 + 0.5 * lax.erf(x * math.sqrt(0.5))
                pdf = jnp.exp(x * x * -0.5) * (1.0 / math.sqrt(2.0 * math.pi))
                hidden[i, here, span] = (x * cdf).astype(BF)
                slope[side, here, span] = (cdf + x * pdf).astype(BF)

            row_loop(32, gelu)

        tiles(one)
        slope_store(i).start()
        hidden_store(i).start()

    def down_piece(p):
        i, slot = p - 8, weight(p)

        def one(n, span):
            wide = wbuf[slot, :, :, span].reshape(model, ROWS)
            acc[:, span] += dot_nn(hidden[i], wide)

        tiles(one)

    def finish():
        sums[...] = jnp.zeros_like(sums)

        def norm(here):
            y_one = xhat[here, :] * vecs[3:4, :] + vecs[4:5, :]
            normal, rstd = norm_rows(y_one + acc[here, :] + vecs[5:6, :])
            out_rows[here, :] = (normal * vecs[6:7, :] + vecs[7:8, :]).astype(BF)
            cot = cotangent[here, :].astype(F32)
            grad = norm_back(cot, normal, rstd, vecs[6:7, :])
            acc[here, :] = grad
            low = grad.astype(BF)
            grad_f[here, :] = low
            sums[0] += fold_rows(cot * normal)
            sums[1] += fold_rows(cot)
            sums[2] += fold_rows(low.astype(F32))

        row_loop(32, norm)
        store(acc, dz_out)
        store(grad_f, grad_f_out)
        store(out_rows, layer_out)

    first(None)
    first(0)
    first(1)
    for copy in mine:
        copy.start()
    stages = ((second, 0), (third, -1), (fourth, -2), (fifth, -3))
    work = {
        4: (queries,),
        5: (keys,),
        6: (values, lambda: attend_pairs(0, 2)),
        7: (lambda: attend_pairs(2, 4),),
        8: (lambda: attend_pairs(6, 2), out_project),
    }

    def tick(t, carry):
        @pl.when(t == 3)
        def _():
            for copy in mine:
                copy.wait()

        for action, shift in ((first, 2),) + stages:
            when_in(t + shift, PIECES, action)
        for action, shift in stages:
            @pl.when(t == -shift)
            def _():
                action(None)
        for part in range(6):
            @pl.when(t == min(part, 4))
            def _():
                halo(part)
        for when, actions in work.items():
            @pl.when(t == when)
            def _():
                for action in actions:
                    action()

        @pl.when(jnp.logical_and(t >= 9, t < 13))
        def _():
            up_piece(t - 5)

        for i in range(2):
            when_in(2 * (t - 13) + i - 1, 4, lambda n: down_piece(n + 8))
        return carry

    lax.fori_loop(0, PIECES + 4, tick, 0)
    finish()
    middle = jnp.logical_and(z >= 1, z <= 2)

    @pl.when(middle)
    def _():
        wait_for(h.at[0 : 5 * step], halo_sent)

    @pl.when(jnp.logical_not(middle))
    def _():
        wait_for(h.at[0:step], halo_sent)

    def drain_one(p, carry):
        drain(p)
        return carry

    lax.fori_loop(0, PIECES, drain_one, 0)
    drain(None)
    slope_store(2).wait()
    slope_store(3).wait()
    for i in range(4):
        hidden_store(i).wait()
    for i, (src, dst) in enumerate(stores):
        pltpu.make_async_copy(src, dst, store_sem.at[i]).wait()


def forward_pass(outer, context, timestep, *arrays):
    sem = pltpu.SemaphoreType.DMA
    rows, model = arrays[4].shape
    win = rows // 5 * 8
    weights = jax.ShapeDtypeStruct((4, 8, 4, ROWS, COLS), BF)
    own = jax.ShapeDtypeStruct((rows, model), BF)
    own_wide = jax.ShapeDtypeStruct((rows, model), F32)
    window = jax.ShapeDtypeStruct((win, model), BF)
    tall = jax.ShapeDtypeStruct((4, rows, model), BF)
    anywhere, vmem = pl.BlockSpec(memory_space=pl.ANY), pl.BlockSpec(memory_space=pltpu.VMEM)
    return pl.pallas_call(
        functools.partial(forward_kernel, outer),
        out_shape=(
            weights, weights, weights, jax.ShapeDtypeStruct((4, 16, model), BF),
            window, own, window, window, own, own, tall, tall, own_wide, own_wide, own, own,
            jax.ShapeDtypeStruct((8, 8, 2 * rows // 5), F32),
            jax.ShapeDtypeStruct((rows, COLS), F32),
            jax.ShapeDtypeStruct((3, 8, model), F32),
        ),
        in_specs=[pl.BlockSpec(memory_space=pltpu.SMEM)] * 2 + [vmem] * 8,
        out_specs=[anywhere] * 16 + [vmem] * 3,
        scratch_shapes=[
            pltpu.VMEM((win, model), BF),
            pltpu.VMEM((rows, model), BF),
            pltpu.VMEM((win, model), BF),
            pltpu.VMEM((win, model), BF),
            pltpu.VMEM((rows, model), BF),
            pltpu.VMEM((rows, model), BF),
            pltpu.VMEM((4, rows, model), BF),
            pltpu.VMEM((2, rows, model), BF),
            pltpu.VMEM((rows, model), F32),
            pltpu.VMEM((rows, model), F32),
            pltpu.VMEM((rows, ROWS), F32),
            pltpu.VMEM((rows, model), BF),
            pltpu.VMEM((rows, model), BF),
            pltpu.VMEM((4, 16, model), BF),
            pltpu.VMEM((4, 16, COLS), F32),
            pltpu.VMEM((3, 4, ROWS, model), BF),
            pltpu.VMEM((COLS, win), BF),
            sem((5,)),
        ]
        + [sem((PIECES + 1,))] * 7
        + [sem, sem, sem((3,)), sem((10,)), sem((6,))],
        compiler_params=pltpu.CompilerParams(
            collective_id=1, has_side_effects=True, vmem_limit_bytes=VMEM_LIMIT
        ),
        name="forward",
    )(context, timestep, *arrays)


def split_heads(rows):
    low = lax.broadcasted_iota(jnp.int32, rows.shape, 1) < rows.shape[1] // 2
    zero = jnp.zeros_like(rows)
    return jnp.concatenate([jnp.where(low, rows, zero), jnp.where(low, zero, rows)], axis=0)


def join_heads(both):
    half = both.shape[1] // 2
    low = lax.broadcasted_iota(jnp.int32, (both.shape[0], half), 0) < both.shape[0] // 2
    return jnp.where(low, both[:, :half], both[:, half:]).T


def masked_scores(keys, q_two, live):
    scores = dot_nt(keys, q_two)
    return jnp.where(lax.broadcasted_iota(jnp.int32, scores.shape, 0) < live, scores, MASKED)


def backward_kernel(
    outer, context, timestep, w_one, w_up, w_down, h_win_in, q_in, k_in, v_in, attn_in, y_in, hidden_in, slope_in,
    xhat_in, dz_in, grad_f_in, lse, rstd, vecs, sums_in,
    out_down, out_up, out_one, out_qkv, sums_out, tokens_out,
    part, lane, got_c, got_dx, got_dy, got_x, got_y, got_z,
    wbuf, hidden, slope, y_low, grad_f, acc, xhat, attn, q, k, v, h_win, dk_acc, dv_acc, k_t, halo_in,
    dtile, wide_tile, stats, s_sum, s_got,
    sent0, sent1, sent2, sent3, sem_c, sem_dx, sem_dy, sem_x, sem_y, sem_z,
    in_sem, hidden_sem, weight_sem, token_sem, halo_sent, halo_got, small_sent, small_got, credit,
):
    at = Place(outer)
    greet(at)
    z, rows, model = at.z, q.shape[0], q.shape[1]
    step = rows // 5
    n_tiles = model // ROWS

    inputs = [
        (grad_f_in, grad_f), (y_in, y_low), (dz_in, acc), (xhat_in, xhat), (attn_in, attn),
        (q_in, q), (k_in, k), (v_in, v), (h_win_in, h_win),
    ]

    def get(i):
        src, dst = inputs[i]
        return pltpu.make_async_copy(src, dst, in_sem.at[i])

    def get_hidden(i):
        slot = lax.rem(i, 2)
        return (
            pltpu.make_async_copy(hidden_in.at[i], hidden.at[slot], hidden_sem.at[slot]),
            pltpu.make_async_copy(slope_in.at[i], slope.at[slot], hidden_sem.at[2 + slot]),
        )

    def get_weight(ref, slot):
        load_lanes(ref, wbuf.at[slot], weight_sem.at[slot])

    def have_weight(slot):
        wait_for(wbuf.at[slot], weight_sem.at[slot])

    def share(slot):
        return timestep[z + slot].astype(F32) * (1.0 / TSTEPS)

    def first(p):
        slot, src_slot = lax.rem(p, 2), lax.rem(p, PARTS)

        @pl.when(p >= 2)
        def _():
            pl.semaphore_wait(credit, 1)

        for a in range(4):
            src = part.at[src_slot, :, :, cols_of(a * 2 + 1 - at.core)]
            send(src, got_c.at[slot, a], sent0.at[p], sem_c.at[p], at.partner())

    def second(p):
        slot, row, src_slot = lax.rem(p, 2), lax.rem(p, LANES), lax.rem(p, PARTS)
        wait_for(got_c.at[slot], sem_c.at[p])

        @pl.when(p >= LANES)
        def _():
            wait_for(lane.at[row, 0], sent1.at[p - LANES])
            wait_for(lane.at[row, 0:2], sent2.at[p - LANES])
            wait_for(lane.at[row, 0, 0:3], sent3.at[p - LANES])

        def add(i, carry):
            a, b = lax.div(i, 4), lax.rem(i, 4)
            lane[row, a, b] = part[src_slot, b, :, cols_of(a * 2 + at.core)] + got_c[slot, a, b]
            return carry

        lax.fori_loop(0, 16, add, 0)

        @pl.when(p < PIECES - 2)
        def _():
            pl.semaphore_signal(credit, inc=1, device_id=at.partner(), device_id_type=MESH)

        wait_for(got_c.at[slot], sent0.at[p])
        send(lane.at[row, at.diag, 0:2], got_dy.at[p], sent1.at[p], sem_dy.at[p], at.across())
        send(lane.at[row, at.diag, 2:4], got_dx.at[p], sent1.at[p], sem_dx.at[p], at.beside())

    def third(p):
        row = lax.rem(p, LANES)
        wait_for(got_dy.at[p], sem_dy.at[p])

        def add_y(i, carry):
            lane[row, at.side, i] = lane[row, at.side, i] + got_dy[p, i]
            return carry

        lax.fori_loop(0, 2, add_y, 0)
        send(lane.at[row, at.side], got_x.at[p], sent2.at[p], sem_x.at[p], at.beside())
        wait_for(got_dx.at[p], sem_dx.at[p])

        def add_x(i, carry):
            lane[row, at.over, i + 2] = lane[row, at.over, i + 2] + got_dx[p, i]
            return carry

        lax.fori_loop(0, 2, add_x, 0)
        send(lane.at[row, at.over], got_y.at[p], sent2.at[p], sem_y.at[p], at.across())

    def fourth(p):
        row = lax.rem(p, LANES)
        wait_for(got_x.at[p], sem_x.at[p])
        wait_for(got_y.at[p], sem_y.at[p])

        def add(i, carry):
            total = lane[row, at.chip, i].astype(F32) + got_x[p, i].astype(F32)
            lane[row, at.chip, i] = (total + got_y[p, i].astype(F32)).astype(BF)
            return carry

        lax.fori_loop(0, 4, add, 0)
        for far in range(1, 4):
            block = lane.at[row, at.chip, lax.rem(z + far, 4)]
            send(block, got_z.at[p, far - 1], sent3.at[p], sem_z.at[p], at.along(far))

    def fifth(p):
        row = lax.rem(p, LANES)
        wait_for(got_z.at[p], sem_z.at[p])
        total = lane[row, at.chip, z].astype(F32)
        for far in range(3):
            total = total + got_z[p, far].astype(F32)


        @pl.when(jnp.logical_and(p < 8, lax.rem(p, 2) == 0))
        def _():
            out_down[lax.rem(lax.div(p, 2), 4)] = total

        @pl.when(jnp.logical_and(p < 8, lax.rem(p, 2) == 1))
        def _():
            out_up[lax.rem(lax.div(p, 2), 4)] = total

        @pl.when(p == 8)
        def _():
            out_one[...] = total

        @pl.when(p > 8)
        def _():
            out_qkv[11 - p] = total.T

    def tiles(action):
        def run(n, carry):
            action(n, tile_rows(n * ROWS, ROWS))
            return carry

        lax.fori_loop(0, n_tiles, run, 0)

    def row_loop(count, action):
        def run(i, carry):
            action(pl.ds(pl.multiple_of(i * count, count), count))
            return carry

        lax.fori_loop(0, rows // count, run, 0)

    def produce(p, left, right):
        slot = lax.rem(p, PARTS)

        def one(n, span):
            part[slot, n] = dot_tn(left[:, span], right()).astype(BF)

        tiles(one)

    def grad_down(i):
        @pl.when(i == 0)
        def _():
            get(0).wait()

        for copy in get_hidden(i):
            copy.wait()

        produce(2 * i, hidden.at[lax.rem(i, 2)], lambda: grad_f[...])

    def grad_pre(i):
        slot = lax.rem(i, 2)
        have_weight(0)

        def one(n, span):
            dtile[...] = dot_nt(grad_f[...], wbuf[0, n])
            stats[8 + i, :, span] = jnp.zeros((8, ROWS), F32)

            def scale(here):
                low = (dtile[here, :] * slope[slot, here, span].astype(F32)).astype(BF)
                slope[slot, here, span] = low
                stats[8 + i, :, span] += fold_rows(low.astype(F32))

            row_loop(64, scale)

        tiles(one)

        @pl.when(i < 3)
        def _():
            get_weight(w_down.at[lax.rem(i + 1, 4)], 0)

        @pl.when(i == 3)
        def _():
            get_weight(w_one.at[3], 0)

    def grad_up(i):
        @pl.when(i == 0)
        def _():
            get(1).wait()

        produce(2 * i + 1, slope.at[lax.rem(i, 2)], lambda: y_low[...])

    def grad_y(i):
        slot = lax.rem(i, 2)
        have_weight(1)

        @pl.when(i == 0)
        def _():
            get(2).wait()

        def one(n, span):
            wide = wbuf[1, :, :, span].reshape(model, ROWS)
            acc[:, span] += dot_nn(slope[slot], wide)

        tiles(one)

        @pl.when(i < 3)
        def _():
            get_weight(w_up.at[lax.rem(i + 1, 4)], 1)

        @pl.when(i == 3)
        def _():
            get_weight(w_one.at[1], 1)

        @pl.when(i < 2)
        def _():
            for copy in get_hidden(i + 2):
                copy.start()

    def feed_forward(u):
        i, kind = lax.div(u, 4), lax.rem(u, 4)
        for which, action in enumerate((grad_down, grad_pre, grad_up, grad_y)):
            @pl.when(kind == which)
            def _():
                action(i)

    def norm_one():
        get(3).wait()
        get(4).wait()
        stats[2] = jnp.zeros_like(stats[2])
        stats[3] = jnp.zeros_like(stats[2])
        stats[4] = jnp.zeros_like(stats[2])

        def back(here):
            grad, normal = acc[here, :], xhat[here, :]
            stats[3] += fold_rows(grad * normal)
            stats[4] += fold_rows(grad)
            grad = norm_back(grad, normal, rstd[here, 0:1], vecs[3:4, :])
            acc[here, :] = grad
            low = grad.astype(BF)
            grad_f[here, :] = low
            stats[2] += fold_rows(low.astype(F32))

        row_loop(32, back)

    def grad_out():
        produce(8, attn, lambda: grad_f[...])
        have_weight(0)

        def one(n, span):
            y_low[:, span] = dot_nt(grad_f[...], wbuf[0, n]).astype(BF)

        tiles(one)
        get_weight(w_one.at[2], 0)
        for i in range(5, 9):
            get(i).wait()

    def attend_pairs(start, count):
        def pair(i, carry):
            lanes = cols_of(i)
            k_t[...] = k[:, lanes].T
            dk_acc[...] = jnp.zeros_like(dk_acc)
            dv_acc[...] = jnp.zeros_like(dv_acc)
            total = jnp.zeros((8, COLS), F32)
            for j in range(5):
                slot = lax.div(z + j, 4)
                span = tile_rows(slot * 4 * step, 4 * step)
                here = slice(j * step, (j + 1) * step)
                q_two = split_heads(q[here, lanes] * jnp.asarray(0.125, BF))
                g_two = split_heads(y_low[here, lanes])
                scores = masked_scores(k[span, lanes], q_two, context[z + slot] + BLOCK)
                probs = jnp.exp(scores - lse[i, j : j + 1, :])
                dv_acc[span, :] += dot_nn(probs.astype(BF), g_two)
                grad_p = dot_nt(v[span, lanes], g_two)
                inner = jnp.sum(probs * grad_p, axis=0, keepdims=True)
                grad_s = (probs * (grad_p - inner)).astype(BF)
                dk_acc[span, :] += dot_nn(grad_s, q_two)
                low = (join_heads(dot_nn(k_t[:, span], grad_s)) * 0.125).astype(BF)
                q[here, lanes] = low
                total = total + fold_rows(low.astype(F32))
            stats[12, :, lanes] = total
            low = dv_acc[...].astype(BF)
            v[:, lanes] = low
            stats[13, :, lanes] = fold_rows(low.astype(F32))
            k[:, lanes] = dk_acc[...].astype(BF)
            return carry

        lax.fori_loop(start, start + count, pair, 0)

    def grad_value():
        produce(9, v, lambda: h_win[...])

    def grad_key_query():
        produce(10, k, lambda: h_win[...])
        produce(11, q, lambda: h_win[tile_rows(z * step, rows), :])

    def input_window():
        have_weight(1)
        have_weight(0)

        def one(n, span):
            wide_k = wbuf[1, :, :, span].reshape(model, ROWS)
            wide_v = wbuf[0, :, :, span].reshape(model, ROWS)
            wide_tile[...] = dot_nn(k[...], wide_k) + dot_nn(v[...], wide_v)
            h_win[:, span] = wide_tile[...].astype(BF)
            low = fold_rows(wide_tile[0 : 4 * step, :])
            high = fold_rows(wide_tile[4 * step : 8 * step, :])
            stats[0, :, span] = low * share(0) + high * share(1)
            stats[1, :, span] = low + high

        tiles(one)
        get_weight(w_one.at[0], 1)

    def halo(part):
        i, half = part // 2, step // 2

        def some_rows(start):
            return pl.ds(pl.multiple_of(start * step + part % 2 * half, half), half)

        @pl.when(z > i)
        def _():
            send(h_win.at[some_rows(i)], halo_in.at[some_rows(5 - z + i)], halo_sent, halo_got, at.along(3))

        @pl.when(z < 3 - i)
        def _():
            send(h_win.at[some_rows(5 + z + i)], halo_in.at[some_rows(i)], halo_sent, halo_got, at.along(1))

    def input_own():
        have_weight(1)

        def one(n, span):
            acc[:, span] += dot_nn(q[...], wbuf[1, :, :, span].reshape(model, ROWS))
            for j in range(5):
                total = fold_rows(acc[j * step : (j + 1) * step, span])
                stats[0, :, span] += total * share(lax.div(z + j, 4))
                stats[1, :, span] += total

        tiles(one)
        for i, row in ((5, 2), (6, 0), (7, 1)):
            stats[i] = sums_in[row]
        for i in range(14):
            s_sum[0, i : i + 1, :] = jnp.sum(stats[i], axis=0, keepdims=True)
        s_sum[0, 14:16, :] = jnp.zeros((2, model), F32)

    small_peers = (at.partner, at.beside, at.across)

    def small_send(i):
        send(s_sum.at[i], s_got.at[i], small_sent.at[i], small_got.at[i], small_peers[i]())

    def small_add(i):
        wait_for(s_got.at[i], small_got.at[i])
        s_sum[i + 1] = s_sum[i] + s_got[i]

    def small_spread():
        for far in range(1, 4):
            send(s_sum.at[3], s_got.at[2 + far], small_sent.at[3], small_got.at[3], at.along(far))

    middle = jnp.logical_and(z >= 1, z <= 2)

    def put_tokens(j):
        block = slice(j * step, (j + 1) * step)
        return pltpu.make_async_copy(acc.at[block], tokens_out.at[block], token_sem.at[j])

    def finish_tokens():
        @pl.when(middle)
        def _():
            wait_for(halo_in.at[0 : 5 * step], halo_got)

        @pl.when(jnp.logical_not(middle))
        def _():
            wait_for(halo_in.at[0:step], halo_got)

        for j in range(5):
            block = slice(j * step, (j + 1) * step)
            acc[block, :] += h_win[tile_rows((z + j) * step, step), :].astype(F32)
            upper = jnp.logical_and(z <= 2, j >= 4 - z)
            lower = jnp.logical_and(z >= 1, j < 4 - z)

            @pl.when(jnp.logical_or(upper, lower))
            def _():
                acc[block, :] += halo_in[block, :].astype(F32)

            put_tokens(j).start()

    get(0).start()
    early = get_hidden(0)
    early[0].start()
    get_weight(w_down.at[0], 0)
    early[1].start()
    get(1).start()
    get_weight(w_up.at[0], 1)
    get(2).start()
    work = {
        5: (norm_one,),
        6: (grad_out, lambda: attend_pairs(0, 1)),
        7: (lambda: attend_pairs(1, 3),),
        8: (lambda: attend_pairs(4, 3),),
        9: (lambda: attend_pairs(7, 1), grad_value),
        10: (grad_key_query,),
        11: (input_window, lambda: halo(0), lambda: halo(1)),
        12: (lambda: halo(2), lambda: halo(3), input_own, lambda: small_send(0)),
        13: (lambda: halo(4), lambda: halo(5), lambda: small_add(0), lambda: small_send(1)),
        14: (lambda: small_add(1), lambda: small_send(2)),
        15: (lambda: small_add(2), small_spread, finish_tokens),
    }

    def slot_run(s, carry):
        c = s - 1
        for action, shift in ((second, 1), (third, 2), (fourth, 3), (fifth, 4), (first, 0)):
            when_in(c - shift, PIECES, action)

        def sub_step(u, inner):
            when_in(3 * s - 2 + u, 16, feed_forward)
            return inner

        @pl.when(s == 1)
        def _():
            for copy in get_hidden(1):
                copy.start()

        @pl.when(s == 2)
        def _():
            for i in range(3, 5):
                get(i).start()

        @pl.when(s == 3)
        def _():
            for i in range(5, 9):
                get(i).start()

        lax.fori_loop(0, 3, sub_step, 0)

        for when, actions in work.items():
            @pl.when(s == when)
            def _():
                for action in actions:
                    action()

        return carry

    lax.fori_loop(0, PIECES + 5, slot_run, 0)
    wait_for(s_got.at[3:6], small_got.at[3])
    sums_out[...] = s_sum[3] + s_got[3] + s_got[4] + s_got[5]
    for p in range(PIECES - LANES, PIECES):
        row = p % LANES
        wait_for(lane.at[row, 0], sent1.at[p])
        wait_for(lane.at[row, 0:2], sent2.at[p])
        wait_for(lane.at[row, 0, 0:3], sent3.at[p])
    for i in range(3):
        wait_for(s_sum.at[i], small_sent.at[i])
    wait_for(s_got.at[0:3], small_sent.at[3])
    wait_for(h_win.at[0 : 3 * step], halo_sent)
    for j in range(5):
        put_tokens(j).wait()


def backward_pass(outer, context, timestep, *arrays):
    sem = pltpu.SemaphoreType.DMA
    model = 8 * COLS
    rows = arrays[4].shape[0]
    win = rows // 5 * 8
    half = (4, 4, ROWS, COLS)
    anywhere, vmem = pl.BlockSpec(memory_space=pl.ANY), pl.BlockSpec(memory_space=pltpu.VMEM)
    return pl.pallas_call(
        functools.partial(backward_kernel, outer),
        out_shape=(
            jax.ShapeDtypeStruct((4, ROWS, COLS), F32),
            jax.ShapeDtypeStruct((4, ROWS, COLS), F32),
            jax.ShapeDtypeStruct((ROWS, COLS), F32),
            jax.ShapeDtypeStruct((3, COLS, ROWS), F32),
            jax.ShapeDtypeStruct((16, model), F32),
            jax.ShapeDtypeStruct((rows, model), F32),
        ),
        in_specs=[pl.BlockSpec(memory_space=pltpu.SMEM)] * 2 + [anywhere] * 14 + [vmem] * 4,
        out_specs=[vmem] * 5 + [anywhere],
        scratch_shapes=[
            pltpu.VMEM((PARTS, 4, ROWS, model), BF),
            pltpu.VMEM((LANES,) + half, BF),
            pltpu.VMEM((2,) + half, BF),
            pltpu.VMEM((PIECES, 2, ROWS, COLS), BF),
            pltpu.VMEM((PIECES, 2, ROWS, COLS), BF),
            pltpu.VMEM((PIECES, 4, ROWS, COLS), BF),
            pltpu.VMEM((PIECES, 4, ROWS, COLS), BF),
            pltpu.VMEM((PIECES, 3, ROWS, COLS), BF),
            pltpu.VMEM((2, 4, ROWS, model), BF),
            pltpu.VMEM((2, rows, model), BF),
            pltpu.VMEM((2, rows, model), BF),
            pltpu.VMEM((rows, model), BF),
            pltpu.VMEM((rows, model), BF),
            pltpu.VMEM((rows, model), F32),
            pltpu.VMEM((rows, model), F32),
            pltpu.VMEM((rows, model), BF),
            pltpu.VMEM((rows, model), BF),
            pltpu.VMEM((win, model), BF),
            pltpu.VMEM((win, model), BF),
            pltpu.VMEM((win, model), BF),
            pltpu.VMEM((win, COLS), F32),
            pltpu.VMEM((win, COLS), F32),
            pltpu.VMEM((COLS, win), BF),
            pltpu.VMEM((rows, model), BF),
            pltpu.VMEM((rows, ROWS), F32),
            pltpu.VMEM((win, ROWS), F32),
            pltpu.VMEM((14, 8, model), F32),
            pltpu.VMEM((4, 16, model), F32),
            pltpu.VMEM((6, 16, model), F32),
        ]
        + [sem((PIECES,))] * 10
        + [
            sem((9,)), sem((4,)), sem((2,)), sem((5,)), sem, sem, sem((4,)), sem((4,)),
            pltpu.SemaphoreType.REGULAR,
        ],
        compiler_params=pltpu.CompilerParams(
            collective_id=2, has_side_effects=True, vmem_limit_bytes=VMEM_LIMIT
        ),
        name="backward",
    )(context, timestep, *arrays)


def body(
    outer, tokens, context, timestep, time_weight, time_bias, qkv_weight, qv_bias, out_weight, out_bias,
    gain_one, shift_one, up_weight, up_bias, down_weight, down_bias, gain_two, shift_two, cotangent,
):
    z = lax.axis_index("mp")
    rows, model = tokens.shape
    seqs = context.shape[0]
    seq_len = rows * 4 // seqs
    step = rows // 5
    groups = None
    if outer > 1:
        groups = [[i * outer + j for j in range(outer)] for i in range(8)]
        qkv_weight, out_weight, up_weight, down_weight, qv_bias, up_bias = (
            lax.all_gather(w, "dp", axis=1, tiled=True, axis_index_groups=groups)
            for w in (qkv_weight, out_weight, up_weight, down_weight, qv_bias, up_bias)
        )
    shard_one = jnp.concatenate([qkv_weight.transpose(0, 2, 1), out_weight.reshape(1, ROWS, COLS)])
    shard_up, shard_down = (w.reshape(4, ROWS, COLS) for w in (up_weight, down_weight))
    own = lax.div(lax.axis_index("dp"), outer)
    n_up, n_qv = up_bias.size, qv_bias.size
    part = jnp.arange(COLS) // up_bias.shape[1]
    up_rows = jnp.where(part == own, jnp.tile(up_bias, (1, 8)), 0)
    qv_rows = jnp.where(part[:64] == own % 4, jnp.tile(qv_bias, (1, 4)), 0).reshape(2, COLS)
    none = jnp.zeros_like(qv_rows)
    q_rows, v_rows = jnp.where(own < 4, qv_rows, none), jnp.where(own < 4, none, qv_rows)
    small = jnp.concatenate([up_rows, q_rows, v_rows, none, none]).reshape(1, 16, COLS)
    row_ids = z * rows + jnp.arange(rows, dtype=jnp.int32)
    owner = (row_ids // seq_len)[:, None] == jnp.arange(seqs, dtype=jnp.int32)[None, :]
    portion = timestep.astype(F32) / TSTEPS
    fraction = jnp.sum(jnp.where(owner, portion[None, :], 0.0), axis=1)
    h_low = (tokens.astype(F32) + fraction[:, None] * time_weight + time_bias).astype(BF)
    vecs = jnp.stack(
        [time_weight, time_bias, out_bias, gain_one, shift_one, down_bias, gain_two, shift_two]
    )
    (
        w_one, w_up, w_down, _, h_win, queries, keys, values, attn, y_low, hidden, slope, xhat, grad_z2,
        grad_f, layer_out, lse, rstd, sums,
    ) = forward_pass(
        outer, context, timestep, shard_one, shard_up, shard_down, small, h_low, tokens, cotangent, vecs,
    )
    grad_down, grad_up, grad_out_w, grad_qkv, totals, grad_tokens = backward_pass(
        outer, context, timestep, w_one, w_up, w_down, h_win, queries, keys,
        values, attn, y_low, hidden, slope, xhat, grad_z2, grad_f, lse, rstd, vecs, sums,
    )
    weight_grads = [
        grad_qkv, grad_out_w, grad_up.reshape(4 * ROWS, COLS), grad_down.reshape(4 * ROWS, COLS)
    ]
    if outer > 1:
        weight_grads = [
            lax.psum_scatter(g, "dp", scatter_dimension=1, tiled=True, axis_index_groups=groups)
            for g in weight_grads
        ]
        totals = lax.psum(totals, "dp", axis_index_groups=groups)
    grad_qkv, grad_out_w, grad_up, grad_down = weight_grads
    dp = lax.axis_index("dp")
    size = lax.axis_size("dp")
    spread = model // (4 * size)
    vectors = lax.dynamic_slice(totals, (0, (dp * 4 + z) * spread), (8, spread))
    grad_up_bias = lax.dynamic_slice(totals, (8, z * ROWS), (4, ROWS)).reshape(8, COLS)
    grad_up_bias = lax.dynamic_slice(grad_up_bias, (0, dp * (COLS // size)), (8, COLS // size))
    grad_qv_bias = totals[12:14].reshape(2, 16, 64).transpose(1, 0, 2).reshape(16, 2 * 64)
    grad_qv_bias = lax.dynamic_slice(grad_qv_bias, (z * 4, dp * (COLS // size)), (4, COLS // size))
    return (
        layer_out, grad_tokens, vectors[0], vectors[1], grad_qkv, grad_qv_bias,
        grad_out_w, vectors[2], vectors[3], vectors[4], grad_up, grad_up_bias,
        grad_down, vectors[5], vectors[6], vectors[7],
    )


def solution(mesh):
    outer = mesh.shape["dp"] // 8
    placed = (
        P(("dp", "mp"), None), P("dp"), P("dp"), P(), P(), P(None, "dp", "mp"), P("mp", "dp"), P("mp", "dp"),
        P(), P(), P(), P("mp", "dp"), P("mp", "dp"), P("mp", "dp"), P(), P(), P(), P(("dp", "mp"), None),
    )
    spread = P(("dp", "mp"))
    wide = P("mp", "dp")
    return jax.shard_map(
        functools.partial(body, outer),
        mesh=mesh,
        in_specs=placed,
        out_specs=(
            P(("dp", "mp"), None), P(("dp", "mp"), None), spread, spread, P(None, "dp", "mp"), wide, wide,
            spread, spread, spread, wide, wide, wide, spread, spread, spread,
        ),
        check_vma=False,
    )
```

```python
import functools
import math

import jax
import jax.numpy as jnp
from jax import lax
from jax.experimental import pallas as pl
from jax.experimental.pallas import tpu as pltpu
from jax.sharding import PartitionSpec as P

BLOCK = 25
TSTEPS = 5000
LN_EPS = 1e-05
MASKED = -1e30
MESH = pl.DeviceIdType.MESH
BF = jnp.bfloat16
F32 = jnp.float32
PIECES = 12
LANES = 4
PARTS = 5
ROWS = 256
COLS = 128
VMEM_LIMIT = 62 * 2**20


def dot_nn(left, right):
    return lax.dot_general(left, right, (((1,), (0,)), ((), ())), preferred_element_type=F32)


def dot_nt(left, right):
    return lax.dot_general(left, right, (((1,), (1,)), ((), ())), preferred_element_type=F32)


def dot_tn(left, right):
    return lax.dot_general(left, right, (((0,), (0,)), ((), ())), preferred_element_type=F32)


class Place:
    def __init__(self, outer):
        dp = lax.axis_index("dp")
        self.z = lax.axis_index("mp")
        self.outer = outer
        self.own = lax.div(dp, outer)
        self.rest = lax.rem(dp, outer)
        self.core = lax.rem(self.own, 2)
        self.chip = lax.div(self.own, 2)
        col, row = lax.rem(self.chip, 2), lax.div(self.chip, 2)
        self.side = row * 2 + (1 - col)
        self.over = (1 - row) * 2 + col
        self.diag = (1 - row) * 2 + (1 - col)

    def dev(self, chip, core, z):
        return ((chip * 2 + core) * self.outer + self.rest, z)

    def partner(self):
        return self.dev(self.chip, 1 - self.core, self.z)

    def beside(self):
        return self.dev(self.side, self.core, self.z)

    def across(self):
        return self.dev(self.over, self.core, self.z)

    def along(self, k):
        return self.dev(self.chip, self.core, lax.rem(self.z + k, 4))


def greet(at):
    barrier = pltpu.get_barrier_semaphore()
    peers = [at.partner(), at.beside(), at.across()] + [at.along(k) for k in range(1, 4)]
    for peer in peers:
        pl.semaphore_signal(barrier, inc=1, device_id=peer, device_id_type=MESH)
    pl.semaphore_wait(barrier, len(peers))


def wait_for(ref, sem):
    pltpu.make_async_copy(ref, ref, sem).wait()


def send(src, dst, send_sem, recv_sem, device):
    pltpu.make_async_remote_copy(
        src, dst, send_sem, recv_sem, device_id=device, device_id_type=MESH
    ).start()


def when_in(piece, count, action):
    @pl.when(jnp.logical_and(piece >= 0, piece < count))
    def _():
        action(piece)


def cols_of(lane):
    return pl.ds(pl.multiple_of(lane * COLS, COLS), COLS)


def load_lanes(src, dst, sem):
    for lane in range(8):
        pltpu.make_async_copy(src.at[lane], dst.at[:, :, lane * COLS : (lane + 1) * COLS], sem).start()


def tile_rows(start, size):
    return pl.ds(pl.multiple_of(start, 128), size)


def norm_rows(values_in):
    average = jnp.mean(values_in, axis=-1, keepdims=True)
    centred = values_in - average
    rstd = lax.rsqrt(jnp.mean(centred * centred, axis=-1, keepdims=True) + LN_EPS)
    return centred * rstd, rstd


def norm_back(grad, xhat, rstd, gain):
    scaled = grad * gain
    first = jnp.mean(scaled, axis=-1, keepdims=True)
    second = jnp.mean(scaled * xhat, axis=-1, keepdims=True)
    return rstd * (scaled - first - xhat * second)


def fold_rows(values_in):
    rows, model = values_in.shape
    return jnp.sum(values_in.reshape(rows // 8, 8, model), axis=0)


def forward_kernel(
    outer, context, timestep, shard_one, shard_up, shard_down, small, h, tokens, cotangent, vecs,
    w_one, w_up, w_down, small_full, h_win_out, q_out, k_out, v_out, attn_out, y_out, hidden_out, slope_out,
    xhat_out, dz_out, grad_f_out, layer_out, lse, rstd_out, sums,
    h_win, q, k, v, attn, y_low, hidden, slope, xhat, acc, pre, grad_f, out_rows, bias_in, bias, wbuf, v_t,
    own_sem, sent, got_z, got_x, got_y, got_xd, got_yd, got_c, halo_sent, halo_got, load_sem, store_sem, slope_sem,
):
    at = Place(outer)
    greet(at)
    z, rows, model = at.z, h.shape[0], h.shape[1]
    step = rows // 5
    groups = (w_one, w_up, w_down)
    x_lane, y_lane, d_lane = at.side * 2 + at.core, at.over * 2 + at.core, at.diag * 2 + at.core

    shards = (shard_one, shard_up, shard_down)

    def block(ref, lane, start, count):
        if ref is small_full:
            return ref.at[pl.ds(start, count), :, cols_of(lane)]
        return ref.at[lane, pl.ds(start, count)]

    def some(ref, lanes):
        return ref.at[:, :, 0 : lanes * COLS] if ref is small_full else ref.at[0:lanes]

    def index(p):
        return PIECES if p is None else p

    def grouped(action):
        def run(p):
            if p is None:
                action(None, small_full, small)
                return
            if isinstance(p, int):
                action(p, groups[p // 4].at[p % 4], shards[p // 4].at[pl.ds(p % 4, 1)])
                return
            for g, ref in enumerate(groups):
                @pl.when(lax.div(p, 4) == g)
                def _():
                    action(p, ref.at[p - 4 * g], shards[g].at[pl.ds(p - 4 * g, 1)])

        return run

    def first(p, ref, src):
        i, dst = index(p), block(ref, at.own, z, 1)
        send(src, dst, sent.at[i], got_x.at[i], at.beside())
        send(src, dst, sent.at[i], got_y.at[i], at.across())
        for step_z in range(1, 4):
            send(src, dst, sent.at[i], got_z.at[i], at.along(step_z))
        send(src, dst, sent.at[i], got_c.at[i], at.partner())

    def second(p, ref, _):
        i = index(p)
        wait_for(block(ref, at.own, 0, 3), got_z.at[i])
        for step_z in range(1, 4):
            part = block(ref, at.own, lax.rem(z + step_z, 4), 1)
            send(part, part, sent.at[i], got_x.at[i], at.beside())
            send(part, part, sent.at[i], got_y.at[i], at.across())
            send(part, part, sent.at[i], got_c.at[i], at.partner())

    def third(p, ref, _):
        i = index(p)
        wait_for(block(ref, x_lane, 0, 4), got_x.at[i])
        part = block(ref, x_lane, 0, 2)
        send(part, part, sent.at[i], got_yd.at[i], at.across())
        part = block(ref, x_lane, 0, 4)
        send(part, part, sent.at[i], got_c.at[i], at.partner())
        wait_for(block(ref, y_lane, 0, 4), got_y.at[i])
        part = block(ref, y_lane, 2, 2)
        send(part, part, sent.at[i], got_xd.at[i], at.beside())
        part = block(ref, y_lane, 0, 4)
        send(part, part, sent.at[i], got_c.at[i], at.partner())

    def fourth(p, ref, _):
        i = index(p)
        wait_for(block(ref, d_lane, 0, 2), got_yd.at[i])
        wait_for(block(ref, d_lane, 2, 2), got_xd.at[i])
        part = block(ref, d_lane, 0, 4)
        send(part, part, sent.at[i], got_c.at[i], at.partner())

    def fifth(p, ref, _):
        wait_for(some(ref, 4), got_c.at[index(p)])
        if p is None:
            pltpu.make_async_copy(small_full, bias_in, own_sem.at[1]).start()
        else:
            load_lanes(ref, wbuf.at[lax.rem(p, 3)], load_sem.at[lax.rem(p, 3)])

    def drain(p, ref, _):
        wait_for(some(ref, 7), sent.at[index(p)])
        wait_for(block(ref, 0, 0, 3), sent.at[index(p)])

    first, second, third, fourth, fifth, drain = (
        grouped(action) for action in (first, second, third, fourth, fifth, drain)
    )

    def halo(part):
        i, small_step = part // 2, step // 2

        def some_rows(start):
            first_row = start * step + part % 2 * small_step
            return pl.ds(pl.multiple_of(first_row, small_step), small_step)

        @pl.when(jnp.logical_and(z >= 1, z < 4 - i))
        def _():
            dst = h_win.at[some_rows(4 + z + i)]
            send(h.at[some_rows(i)], dst, halo_sent, halo_got, at.along(3))

        @pl.when(jnp.logical_and(z <= 2, z >= i))
        def _():
            send(h.at[some_rows(4 - z + i)], h_win.at[some_rows(i)], halo_sent, halo_got, at.along(1))

    mine = [
        pltpu.make_async_copy(shards[g], ref.at[:, at.own, z], own_sem.at[2 + g])
        for g, ref in enumerate(groups)
    ] + [pltpu.make_async_copy(small, small_full.at[pl.ds(z, 1), :, cols_of(at.own)], own_sem.at[0])]
    stores = []

    def store(src, dst):
        pltpu.make_async_copy(src, dst, store_sem.at[len(stores)]).start()
        stores.append((src, dst))

    n_tiles = model // ROWS

    def tiles(action):
        def run(n, carry):
            action(n, tile_rows(n * ROWS, ROWS))
            return carry

        lax.fori_loop(0, n_tiles, run, 0)

    def weight(p):
        slot = lax.rem(p, 3)
        wait_for(wbuf.at[slot], load_sem.at[slot])
        return slot

    def make_bias():
        pltpu.make_async_copy(small_full, bias_in, own_sem.at[1]).wait()
        total = bias_in[:, :, 0:COLS].astype(F32)
        for lane in range(1, 8):
            total = total + bias_in[:, :, lane * COLS : (lane + 1) * COLS].astype(F32)
        bias[...] = total

    def project(p, rows_in, target, bias_row):
        slot = weight(p)

        def one(n, span):
            result = dot_nt(rows_in[...], wbuf[slot, n])
            if bias_row is not None:
                result = result + jnp.concatenate(
                    [bias[n, bias_row : bias_row + 1], bias[n, bias_row + 1 : bias_row + 2]], axis=1
                )
            target[:, span] = result.astype(BF)

        tiles(one)

    def queries():
        make_bias()
        project(0, h, q, 8)
        store(q, q_out)

    def keys():
        wait_for(h_win.at[0 : 3 * step], halo_got)
        h_win[tile_rows(z * step, rows), :] = h[...]
        project(1, h_win, k, None)
        store(k, k_out)
        store(h_win, h_win_out)

    def values():
        project(2, h_win, v, 10)
        store(v, v_out)

    def attend_pairs(start, count):
        def pair(i, carry):
            lanes = cols_of(i)
            v_t[...] = v[:, lanes].T
            for j in range(5):
                slot = lax.div(z + j, 4)
                span = tile_rows(slot * 4 * step, 4 * step)
                here = slice(j * step, (j + 1) * step)
                q_two = split_heads(q[here, lanes] * jnp.asarray(0.125, BF))
                scores = masked_scores(k[span, lanes], q_two, context[z + slot] + BLOCK)
                row_max = jnp.max(scores, axis=0, keepdims=True)
                expo = jnp.exp(scores - row_max)
                total = jnp.sum(expo, axis=0, keepdims=True)
                mixed = dot_nn(v_t[:, span], expo.astype(BF)) / total
                attn[here, lanes] = join_heads(mixed).astype(BF)
                lse[i, j : j + 1, :] = row_max + jnp.log(total)
            return carry

        lax.fori_loop(start, start + count, pair, 0)

    def row_loop(count, action):
        def run(i, carry):
            action(pl.ds(pl.multiple_of(i * count, count), count))
            return carry

        lax.fori_loop(0, rows // count, run, 0)

    def out_project():
        slot = weight(3)

        def one(n, span):
            wide = wbuf[slot, :, :, span].reshape(model, ROWS)
            acc[:, span] = dot_nn(attn[...], wide)

        tiles(one)
        store(attn, attn_out)

        def norm(here, i):
            share = timestep[z + lax.div(z + lax.div(i * 64, step), 4)].astype(F32) * (1.0 / TSTEPS)
            h_zero = tokens[here, :].astype(F32) + share * vecs[0:1, :] + vecs[1:2, :]
            normal, rstd = norm_rows(h_zero + acc[here, :] + vecs[2:3, :])
            xhat[here, :] = normal
            y_low[here, :] = (normal * vecs[3:4, :] + vecs[4:5, :]).astype(BF)
            rstd_out[here, :] = jnp.broadcast_to(rstd, (rstd.shape[0], COLS))

        def run(i, carry):
            norm(pl.ds(pl.multiple_of(i * 64, 64), 64), i)
            return carry

        lax.fori_loop(0, rows // 64, run, 0)
        acc[...] = jnp.zeros_like(acc)
        store(y_low, y_out)
        store(xhat, xhat_out)

    def slope_store(i):
        slot = lax.rem(i, 2)
        return pltpu.make_async_copy(slope.at[slot], slope_out.at[i], slope_sem.at[slot])

    def hidden_store(i):
        return pltpu.make_async_copy(hidden.at[i], hidden_out.at[i], slope_sem.at[2 + i])

    def up_piece(p):
        i, slot = p - 4, weight(p)
        side = lax.rem(i, 2)

        @pl.when(i >= 2)
        def _():
            slope_store(i - 2).wait()

        def one(n, span):
            offset = jnp.concatenate([bias[n, pl.ds(2 * i, 1)], bias[n, pl.ds(2 * i + 1, 1)]], axis=1)
            pre[...] = dot_nt(y_low[...], wbuf[slot, n]) + offset

            def gelu(here):
                x = pre[here, :]
                cdf = 0.5 + 0.5 * lax.erf(x * math.sqrt(0.5))
                pdf = jnp.exp(x * x * -0.5) * (1.0 / math.sqrt(2.0 * math.pi))
                hidden[i, here, span] = (x * cdf).astype(BF)
                slope[side, here, span] = (cdf + x * pdf).astype(BF)

            row_loop(64, gelu)

        tiles(one)
        slope_store(i).start()
        hidden_store(i).start()

    def down_piece(p):
        i, slot = p - 8, weight(p)

        def one(n, span):
            wide = wbuf[slot, :, :, span].reshape(model, ROWS)
            acc[:, span] += dot_nn(hidden[i], wide)

        tiles(one)

    def finish():
        sums[...] = jnp.zeros_like(sums)

        def norm(here):
            y_one = xhat[here, :] * vecs[3:4, :] + vecs[4:5, :]
            normal, rstd = norm_rows(y_one + acc[here, :] + vecs[5:6, :])
            out_rows[here, :] = (normal * vecs[6:7, :] + vecs[7:8, :]).astype(BF)
            cot = cotangent[here, :].astype(F32)
            grad = norm_back(cot, normal, rstd, vecs[6:7, :])
            acc[here, :] = grad
            low = grad.astype(BF)
            grad_f[here, :] = low
            sums[0] += fold_rows(cot * normal)
            sums[1] += fold_rows(cot)
            sums[2] += fold_rows(low.astype(F32))

        row_loop(128, norm)
        store(acc, dz_out)
        store(grad_f, grad_f_out)
        store(out_rows, layer_out)

    first(None)
    first(0)
    first(1)
    for copy in mine:
        copy.start()
    stages = ((second, 0), (third, -1), (fourth, -2), (fifth, -3))
    work = {
        4: (queries,),
        5: (keys,),
        6: (values, lambda: attend_pairs(0, 2)),
        7: (lambda: attend_pairs(2, 4),),
        8: (lambda: attend_pairs(6, 2), out_project),
    }

    def tick(t, carry):
        @pl.when(t == 3)
        def _():
            for copy in mine:
                copy.wait()

        for action, shift in ((first, 2),) + stages:
            when_in(t + shift, PIECES, action)
        for action, shift in stages:
            @pl.when(t == -shift)
            def _():
                action(None)
        for part in range(6):
            @pl.when(t == min(part, 4))
            def _():
                halo(part)
        for when, actions in work.items():
            @pl.when(t == when)
            def _():
                for action in actions:
                    action()

        @pl.when(jnp.logical_and(t >= 9, t < 13))
        def _():
            up_piece(t - 5)

        for i in range(2):
            when_in(2 * (t - 13) + i - 1, 4, lambda n: down_piece(n + 8))
        return carry

    lax.fori_loop(0, PIECES + 4, tick, 0)
    finish()
    middle = jnp.logical_and(z >= 1, z <= 2)

    @pl.when(middle)
    def _():
        wait_for(h.at[0 : 5 * step], halo_sent)

    @pl.when(jnp.logical_not(middle))
    def _():
        wait_for(h.at[0:step], halo_sent)

    def drain_one(p, carry):
        drain(p)
        return carry

    lax.fori_loop(0, PIECES, drain_one, 0)
    drain(None)
    slope_store(2).wait()
    slope_store(3).wait()
    for i in range(4):
        hidden_store(i).wait()
    for i, (src, dst) in enumerate(stores):
        pltpu.make_async_copy(src, dst, store_sem.at[i]).wait()


def forward_pass(outer, context, timestep, *arrays):
    sem = pltpu.SemaphoreType.DMA
    rows, model = arrays[4].shape
    win = rows // 5 * 8
    weights = jax.ShapeDtypeStruct((4, 8, 4, ROWS, COLS), BF)
    own = jax.ShapeDtypeStruct((rows, model), BF)
    own_wide = jax.ShapeDtypeStruct((rows, model), F32)
    window = jax.ShapeDtypeStruct((win, model), BF)
    tall = jax.ShapeDtypeStruct((4, rows, model), BF)
    anywhere, vmem = pl.BlockSpec(memory_space=pl.ANY), pl.BlockSpec(memory_space=pltpu.VMEM)
    return pl.pallas_call(
        functools.partial(forward_kernel, outer),
        out_shape=(
            weights, weights, weights, jax.ShapeDtypeStruct((4, 16, model), BF),
            window, own, window, window, own, own, tall, tall, own_wide, own_wide, own, own,
            jax.ShapeDtypeStruct((8, 8, 2 * rows // 5), F32),
            jax.ShapeDtypeStruct((rows, COLS), F32),
            jax.ShapeDtypeStruct((3, 8, model), F32),
        ),
        in_specs=[pl.BlockSpec(memory_space=pltpu.SMEM)] * 2 + [vmem] * 8,
        out_specs=[anywhere] * 16 + [vmem] * 3,
        scratch_shapes=[
            pltpu.VMEM((win, model), BF),
            pltpu.VMEM((rows, model), BF),
            pltpu.VMEM((win, model), BF),
            pltpu.VMEM((win, model), BF),
            pltpu.VMEM((rows, model), BF),
            pltpu.VMEM((rows, model), BF),
            pltpu.VMEM((4, rows, model), BF),
            pltpu.VMEM((2, rows, model), BF),
            pltpu.VMEM((rows, model), F32),
            pltpu.VMEM((rows, model), F32),
            pltpu.VMEM((rows, ROWS), F32),
            pltpu.VMEM((rows, model), BF),
            pltpu.VMEM((rows, model), BF),
            pltpu.VMEM((4, 16, model), BF),
            pltpu.VMEM((4, 16, COLS), F32),
            pltpu.VMEM((3, 4, ROWS, model), BF),
            pltpu.VMEM((COLS, win), BF),
            sem((5,)),
        ]
        + [sem((PIECES + 1,))] * 7
        + [sem, sem, sem((3,)), sem((10,)), sem((6,))],
        compiler_params=pltpu.CompilerParams(
            collective_id=1, has_side_effects=True, vmem_limit_bytes=VMEM_LIMIT
        ),
        name="forward",
    )(context, timestep, *arrays)


def split_heads(rows):
    low = lax.broadcasted_iota(jnp.int32, rows.shape, 1) < rows.shape[1] // 2
    zero = jnp.zeros_like(rows)
    return jnp.concatenate([jnp.where(low, rows, zero), jnp.where(low, zero, rows)], axis=0)


def join_heads(both):
    half = both.shape[1] // 2
    low = lax.broadcasted_iota(jnp.int32, (both.shape[0], half), 0) < both.shape[0] // 2
    return jnp.where(low, both[:, :half], both[:, half:]).T


def masked_scores(keys, q_two, live):
    scores = dot_nt(keys, q_two)
    return jnp.where(lax.broadcasted_iota(jnp.int32, scores.shape, 0) < live, scores, MASKED)


def backward_kernel(
    outer, context, timestep, w_one, w_up, w_down, h_win_in, q_in, k_in, v_in, attn_in, y_in, hidden_in, slope_in,
    xhat_in, dz_in, grad_f_in, lse, rstd, vecs, sums_in,
    out_down, out_up, out_one, out_qkv, sums_out, tokens_out,
    part, lane, got_c, got_dx, got_dy, got_x, got_y, got_z,
    wbuf, hidden, slope, y_low, grad_f, acc, xhat, attn, q, k, v, h_win, dk_acc, dv_acc, k_t, halo_in,
    dtile, wide_tile, stats, s_sum, s_got,
    sent0, sent1, sent2, sent3, sem_c, sem_dx, sem_dy, sem_x, sem_y, sem_z,
    in_sem, hidden_sem, weight_sem, token_sem, halo_sent, halo_got, small_sent, small_got, credit,
):
    at = Place(outer)
    greet(at)
    z, rows, model = at.z, q.shape[0], q.shape[1]
    step = rows // 5
    n_tiles = model // ROWS

    inputs = [
        (grad_f_in, grad_f), (y_in, y_low), (dz_in, acc), (xhat_in, xhat), (attn_in, attn),
        (q_in, q), (k_in, k), (v_in, v), (h_win_in, h_win),
    ]

    def get(i):
        src, dst = inputs[i]
        return pltpu.make_async_copy(src, dst, in_sem.at[i])

    def get_hidden(i):
        slot = lax.rem(i, 2)
        return (
            pltpu.make_async_copy(hidden_in.at[i], hidden.at[slot], hidden_sem.at[slot]),
            pltpu.make_async_copy(slope_in.at[i], slope.at[slot], hidden_sem.at[2 + slot]),
        )

    def get_weight(ref, slot):
        load_lanes(ref, wbuf.at[slot], weight_sem.at[slot])

    def have_weight(slot):
        wait_for(wbuf.at[slot], weight_sem.at[slot])

    def share(slot):
        return timestep[z + slot].astype(F32) * (1.0 / TSTEPS)

    def first(p):
        slot, src_slot = lax.rem(p, 2), lax.rem(p, PARTS)

        @pl.when(p >= 2)
        def _():
            pl.semaphore_wait(credit, 1)

        for a in range(4):
            src = part.at[src_slot, :, :, cols_of(a * 2 + 1 - at.core)]
            send(src, got_c.at[slot, a], sent0.at[p], sem_c.at[p], at.partner())

    def second(p):
        slot, row, src_slot = lax.rem(p, 2), lax.rem(p, LANES), lax.rem(p, PARTS)
        wait_for(got_c.at[slot], sem_c.at[p])

        @pl.when(p >= LANES)
        def _():
            wait_for(lane.at[row, 0], sent1.at[p - LANES])
            wait_for(lane.at[row, 0:2], sent2.at[p - LANES])
            wait_for(lane.at[row, 0, 0:3], sent3.at[p - LANES])

        def add(i, carry):
            a, b = lax.div(i, 4), lax.rem(i, 4)
            lane[row, a, b] = part[src_slot, b, :, cols_of(a * 2 + at.core)] + got_c[slot, a, b]
            return carry

        lax.fori_loop(0, 16, add, 0)

        @pl.when(p < PIECES - 2)
        def _():
            pl.semaphore_signal(credit, inc=1, device_id=at.partner(), device_id_type=MESH)

        wait_for(got_c.at[slot], sent0.at[p])
        send(lane.at[row, at.diag, 0:2], got_dy.at[p], sent1.at[p], sem_dy.at[p], at.across())
        send(lane.at[row, at.diag, 2:4], got_dx.at[p], sent1.at[p], sem_dx.at[p], at.beside())

    def third(p):
        row = lax.rem(p, LANES)
        wait_for(got_dy.at[p], sem_dy.at[p])

        def add_y(i, carry):
            lane[row, at.side, i] = lane[row, at.side, i] + got_dy[p, i]
            return carry

        lax.fori_loop(0, 2, add_y, 0)
        send(lane.at[row, at.side], got_x.at[p], sent2.at[p], sem_x.at[p], at.beside())
        wait_for(got_dx.at[p], sem_dx.at[p])

        def add_x(i, carry):
            lane[row, at.over, i + 2] = lane[row, at.over, i + 2] + got_dx[p, i]
            return carry

        lax.fori_loop(0, 2, add_x, 0)
        send(lane.at[row, at.over], got_y.at[p], sent2.at[p], sem_y.at[p], at.across())

    def fourth(p):
        row = lax.rem(p, LANES)
        wait_for(got_x.at[p], sem_x.at[p])
        wait_for(got_y.at[p], sem_y.at[p])

        def add(i, carry):
            total = lane[row, at.chip, i].astype(F32) + got_x[p, i].astype(F32)
            lane[row, at.chip, i] = (total + got_y[p, i].astype(F32)).astype(BF)
            return carry

        lax.fori_loop(0, 4, add, 0)
        for far in range(1, 4):
            block = lane.at[row, at.chip, lax.rem(z + far, 4)]
            send(block, got_z.at[p, far - 1], sent3.at[p], sem_z.at[p], at.along(far))

    def fifth(p):
        row = lax.rem(p, LANES)
        wait_for(got_z.at[p], sem_z.at[p])
        total = lane[row, at.chip, z].astype(F32)
        for far in range(3):
            total = total + got_z[p, far].astype(F32)


        @pl.when(jnp.logical_and(p < 8, lax.rem(p, 2) == 0))
        def _():
            out_down[lax.rem(lax.div(p, 2), 4)] = total

        @pl.when(jnp.logical_and(p < 8, lax.rem(p, 2) == 1))
        def _():
            out_up[lax.rem(lax.div(p, 2), 4)] = total

        @pl.when(p == 8)
        def _():
            out_one[...] = total

        @pl.when(p > 8)
        def _():
            out_qkv[11 - p] = total.T

    def tiles(action):
        def run(n, carry):
            action(n, tile_rows(n * ROWS, ROWS))
            return carry

        lax.fori_loop(0, n_tiles, run, 0)

    def row_loop(count, action):
        def run(i, carry):
            action(pl.ds(pl.multiple_of(i * count, count), count))
            return carry

        lax.fori_loop(0, rows // count, run, 0)

    def produce(p, left, right):
        slot = lax.rem(p, PARTS)

        def one(n, span):
            part[slot, n] = dot_tn(left[:, span], right()).astype(BF)

        tiles(one)

    def grad_down(i):
        @pl.when(i == 0)
        def _():
            get(0).wait()

        for copy in get_hidden(i):
            copy.wait()

        produce(2 * i, hidden.at[lax.rem(i, 2)], lambda: grad_f[...])

    def grad_pre(i):
        slot = lax.rem(i, 2)
        have_weight(0)

        def one(n, span):
            dtile[...] = dot_nt(grad_f[...], wbuf[0, n])
            stats[8 + i, :, span] = jnp.zeros((8, ROWS), F32)

            def scale(here):
                low = (dtile[here, :] * slope[slot, here, span].astype(F32)).astype(BF)
                slope[slot, here, span] = low
                stats[8 + i, :, span] += fold_rows(low.astype(F32))

            row_loop(64, scale)

        tiles(one)

        @pl.when(i < 3)
        def _():
            get_weight(w_down.at[lax.rem(i + 1, 4)], 0)

        @pl.when(i == 3)
        def _():
            get_weight(w_one.at[3], 0)

    def grad_up(i):
        @pl.when(i == 0)
        def _():
            get(1).wait()

        produce(2 * i + 1, slope.at[lax.rem(i, 2)], lambda: y_low[...])

    def grad_y(i):
        slot = lax.rem(i, 2)
        have_weight(1)

        @pl.when(i == 0)
        def _():
            get(2).wait()

        def one(n, span):
            wide = wbuf[1, :, :, span].reshape(model, ROWS)
            acc[:, span] += dot_nn(slope[slot], wide)

        tiles(one)

        @pl.when(i < 3)
        def _():
            get_weight(w_up.at[lax.rem(i + 1, 4)], 1)

        @pl.when(i == 3)
        def _():
            get_weight(w_one.at[1], 1)

        @pl.when(i < 2)
        def _():
            for copy in get_hidden(i + 2):
                copy.start()

    def feed_forward(u):
        i, kind = lax.div(u, 4), lax.rem(u, 4)
        for which, action in enumerate((grad_down, grad_pre, grad_up, grad_y)):
            @pl.when(kind == which)
            def _():
                action(i)

    def norm_one():
        get(3).wait()
        get(4).wait()
        stats[2] = jnp.zeros_like(stats[2])
        stats[3] = jnp.zeros_like(stats[2])
        stats[4] = jnp.zeros_like(stats[2])

        def back(here):
            grad, normal = acc[here, :], xhat[here, :]
            stats[3] += fold_rows(grad * normal)
            stats[4] += fold_rows(grad)
            grad = norm_back(grad, normal, rstd[here, 0:1], vecs[3:4, :])
            acc[here, :] = grad
            low = grad.astype(BF)
            grad_f[here, :] = low
            stats[2] += fold_rows(low.astype(F32))

        row_loop(64, back)

    def grad_out():
        produce(8, attn, lambda: grad_f[...])
        have_weight(0)

        def one(n, span):
            y_low[:, span] = dot_nt(grad_f[...], wbuf[0, n]).astype(BF)

        tiles(one)
        get_weight(w_one.at[2], 0)
        for i in range(5, 9):
            get(i).wait()

    def attend_pairs(start, count):
        def pair(i, carry):
            lanes = cols_of(i)
            k_t[...] = k[:, lanes].T
            dk_acc[...] = jnp.zeros_like(dk_acc)
            dv_acc[...] = jnp.zeros_like(dv_acc)
            total = jnp.zeros((8, COLS), F32)
            for j in range(5):
                slot = lax.div(z + j, 4)
                span = tile_rows(slot * 4 * step, 4 * step)
                here = slice(j * step, (j + 1) * step)
                q_two = split_heads(q[here, lanes] * jnp.asarray(0.125, BF))
                g_two = split_heads(y_low[here, lanes])
                scores = masked_scores(k[span, lanes], q_two, context[z + slot] + BLOCK)
                probs = jnp.exp(scores - lse[i, j : j + 1, :])
                dv_acc[span, :] += dot_nn(probs.astype(BF), g_two)
                grad_p = dot_nt(v[span, lanes], g_two)
                inner = jnp.sum(probs * grad_p, axis=0, keepdims=True)
                grad_s = (probs * (grad_p - inner)).astype(BF)
                dk_acc[span, :] += dot_nn(grad_s, q_two)
                low = (join_heads(dot_nn(k_t[:, span], grad_s)) * 0.125).astype(BF)
                q[here, lanes] = low
                total = total + fold_rows(low.astype(F32))
            stats[12, :, lanes] = total
            low = dv_acc[...].astype(BF)
            v[:, lanes] = low
            stats[13, :, lanes] = fold_rows(low.astype(F32))
            k[:, lanes] = dk_acc[...].astype(BF)
            return carry

        lax.fori_loop(start, start + count, pair, 0)

    def grad_value():
        produce(9, v, lambda: h_win[...])

    def grad_key_query():
        produce(10, k, lambda: h_win[...])
        produce(11, q, lambda: h_win[tile_rows(z * step, rows), :])

    def input_window():
        have_weight(1)
        have_weight(0)

        def one(n, span):
            wide_k = wbuf[1, :, :, span].reshape(model, ROWS)
            wide_v = wbuf[0, :, :, span].reshape(model, ROWS)
            wide_tile[...] = dot_nn(k[...], wide_k) + dot_nn(v[...], wide_v)
            h_win[:, span] = wide_tile[...].astype(BF)
            low = fold_rows(wide_tile[0 : 4 * step, :])
            high = fold_rows(wide_tile[4 * step : 8 * step, :])
            stats[0, :, span] = low * share(0) + high * share(1)
            stats[1, :, span] = low + high

        tiles(one)
        get_weight(w_one.at[0], 1)

    def halo(part):
        i, half = part // 2, step // 2

        def some_rows(start):
            return pl.ds(pl.multiple_of(start * step + part % 2 * half, half), half)

        @pl.when(z > i)
        def _():
            send(h_win.at[some_rows(i)], halo_in.at[some_rows(5 - z + i)], halo_sent, halo_got, at.along(3))

        @pl.when(z < 3 - i)
        def _():
            send(h_win.at[some_rows(5 + z + i)], halo_in.at[some_rows(i)], halo_sent, halo_got, at.along(1))

    def input_own():
        have_weight(1)

        def one(n, span):
            acc[:, span] += dot_nn(q[...], wbuf[1, :, :, span].reshape(model, ROWS))
            for j in range(5):
                total = fold_rows(acc[j * step : (j + 1) * step, span])
                stats[0, :, span] += total * share(lax.div(z + j, 4))
                stats[1, :, span] += total

        tiles(one)
        for i, row in ((5, 2), (6, 0), (7, 1)):
            stats[i] = sums_in[row]
        for i in range(14):
            s_sum[0, i : i + 1, :] = jnp.sum(stats[i], axis=0, keepdims=True)
        s_sum[0, 14:16, :] = jnp.zeros((2, model), F32)

    small_peers = (at.partner, at.beside, at.across)

    def small_send(i):
        send(s_sum.at[i], s_got.at[i], small_sent.at[i], small_got.at[i], small_peers[i]())

    def small_add(i):
        wait_for(s_got.at[i], small_got.at[i])
        s_sum[i + 1] = s_sum[i] + s_got[i]

    def small_spread():
        for far in range(1, 4):
            send(s_sum.at[3], s_got.at[2 + far], small_sent.at[3], small_got.at[3], at.along(far))

    middle = jnp.logical_and(z >= 1, z <= 2)

    def put_tokens(j):
        block = slice(j * step, (j + 1) * step)
        return pltpu.make_async_copy(acc.at[block], tokens_out.at[block], token_sem.at[j])

    def finish_tokens():
        @pl.when(middle)
        def _():
            wait_for(halo_in.at[0 : 5 * step], halo_got)

        @pl.when(jnp.logical_not(middle))
        def _():
            wait_for(halo_in.at[0:step], halo_got)

        for j in range(5):
            block = slice(j * step, (j + 1) * step)
            acc[block, :] += h_win[tile_rows((z + j) * step, step), :].astype(F32)
            upper = jnp.logical_and(z <= 2, j >= 4 - z)
            lower = jnp.logical_and(z >= 1, j < 4 - z)

            @pl.when(jnp.logical_or(upper, lower))
            def _():
                acc[block, :] += halo_in[block, :].astype(F32)

            put_tokens(j).start()

    get(0).start()
    early = get_hidden(0)
    early[0].start()
    get_weight(w_down.at[0], 0)
    early[1].start()
    get(1).start()
    get_weight(w_up.at[0], 1)
    get(2).start()
    work = {
        5: (norm_one,),
        6: (grad_out, lambda: attend_pairs(0, 1)),
        7: (lambda: attend_pairs(1, 3),),
        8: (lambda: attend_pairs(4, 3),),
        9: (lambda: attend_pairs(7, 1), grad_value),
        10: (grad_key_query,),
        11: (input_window, lambda: halo(0), lambda: halo(1)),
        12: (lambda: halo(2), lambda: halo(3), input_own, lambda: small_send(0)),
        13: (lambda: halo(4), lambda: halo(5), lambda: small_add(0), lambda: small_send(1)),
        14: (lambda: small_add(1), lambda: small_send(2)),
        15: (lambda: small_add(2), small_spread, finish_tokens),
    }

    def slot_run(s, carry):
        c = s - 1
        for action, shift in ((second, 1), (third, 2), (fourth, 3), (fifth, 4), (first, 0)):
            when_in(c - shift, PIECES, action)

        def sub_step(u, inner):
            when_in(3 * s - 2 + u, 16, feed_forward)
            return inner

        @pl.when(s == 1)
        def _():
            for copy in get_hidden(1):
                copy.start()

        @pl.when(s == 2)
        def _():
            for i in range(3, 5):
                get(i).start()

        @pl.when(s == 3)
        def _():
            for i in range(5, 9):
                get(i).start()

        lax.fori_loop(0, 3, sub_step, 0)

        for when, actions in work.items():
            @pl.when(s == when)
            def _():
                for action in actions:
                    action()

        return carry

    lax.fori_loop(0, PIECES + 5, slot_run, 0)
    wait_for(s_got.at[3:6], small_got.at[3])
    sums_out[...] = s_sum[3] + s_got[3] + s_got[4] + s_got[5]
    for p in range(PIECES - LANES, PIECES):
        row = p % LANES
        wait_for(lane.at[row, 0], sent1.at[p])
        wait_for(lane.at[row, 0:2], sent2.at[p])
        wait_for(lane.at[row, 0, 0:3], sent3.at[p])
    for i in range(3):
        wait_for(s_sum.at[i], small_sent.at[i])
    wait_for(s_got.at[0:3], small_sent.at[3])
    wait_for(h_win.at[0 : 3 * step], halo_sent)
    for j in range(5):
        put_tokens(j).wait()


def backward_pass(outer, context, timestep, *arrays):
    sem = pltpu.SemaphoreType.DMA
    model = 8 * COLS
    rows = arrays[4].shape[0]
    win = rows // 5 * 8
    half = (4, 4, ROWS, COLS)
    anywhere, vmem = pl.BlockSpec(memory_space=pl.ANY), pl.BlockSpec(memory_space=pltpu.VMEM)
    return pl.pallas_call(
        functools.partial(backward_kernel, outer),
        out_shape=(
            jax.ShapeDtypeStruct((4, ROWS, COLS), F32),
            jax.ShapeDtypeStruct((4, ROWS, COLS), F32),
            jax.ShapeDtypeStruct((ROWS, COLS), F32),
            jax.ShapeDtypeStruct((3, COLS, ROWS), F32),
            jax.ShapeDtypeStruct((16, model), F32),
            jax.ShapeDtypeStruct((rows, model), F32),
        ),
        in_specs=[pl.BlockSpec(memory_space=pltpu.SMEM)] * 2 + [anywhere] * 14 + [vmem] * 4,
        out_specs=[vmem] * 5 + [anywhere],
        scratch_shapes=[
            pltpu.VMEM((PARTS, 4, ROWS, model), BF),
            pltpu.VMEM((LANES,) + half, BF),
            pltpu.VMEM((2,) + half, BF),
            pltpu.VMEM((PIECES, 2, ROWS, COLS), BF),
            pltpu.VMEM((PIECES, 2, ROWS, COLS), BF),
            pltpu.VMEM((PIECES, 4, ROWS, COLS), BF),
            pltpu.VMEM((PIECES, 4, ROWS, COLS), BF),
            pltpu.VMEM((PIECES, 3, ROWS, COLS), BF),
            pltpu.VMEM((2, 4, ROWS, model), BF),
            pltpu.VMEM((2, rows, model), BF),
            pltpu.VMEM((2, rows, model), BF),
            pltpu.VMEM((rows, model), BF),
            pltpu.VMEM((rows, model), BF),
            pltpu.VMEM((rows, model), F32),
            pltpu.VMEM((rows, model), F32),
            pltpu.VMEM((rows, model), BF),
            pltpu.VMEM((rows, model), BF),
            pltpu.VMEM((win, model), BF),
            pltpu.VMEM((win, model), BF),
            pltpu.VMEM((win, model), BF),
            pltpu.VMEM((win, COLS), F32),
            pltpu.VMEM((win, COLS), F32),
            pltpu.VMEM((COLS, win), BF),
            pltpu.VMEM((rows, model), BF),
            pltpu.VMEM((rows, ROWS), F32),
            pltpu.VMEM((win, ROWS), F32),
            pltpu.VMEM((14, 8, model), F32),
            pltpu.VMEM((4, 16, model), F32),
            pltpu.VMEM((6, 16, model), F32),
        ]
        + [sem((PIECES,))] * 10
        + [
            sem((9,)), sem((4,)), sem((2,)), sem((5,)), sem, sem, sem((4,)), sem((4,)),
            pltpu.SemaphoreType.REGULAR,
        ],
        compiler_params=pltpu.CompilerParams(
            collective_id=2, has_side_effects=True, vmem_limit_bytes=VMEM_LIMIT
        ),
        name="backward",
    )(context, timestep, *arrays)


def body(
    outer, tokens, context, timestep, time_weight, time_bias, qkv_weight, qv_bias, out_weight, out_bias,
    gain_one, shift_one, up_weight, up_bias, down_weight, down_bias, gain_two, shift_two, cotangent,
):
    z = lax.axis_index("mp")
    rows, model = tokens.shape
    seqs = context.shape[0]
    seq_len = rows * 4 // seqs
    step = rows // 5
    groups = None
    if outer > 1:
        groups = [[i * outer + j for j in range(outer)] for i in range(8)]
        qkv_weight, out_weight, up_weight, down_weight, qv_bias, up_bias = (
            lax.all_gather(w, "dp", axis=1, tiled=True, axis_index_groups=groups)
            for w in (qkv_weight, out_weight, up_weight, down_weight, qv_bias, up_bias)
        )
    shard_one = jnp.concatenate([qkv_weight.transpose(0, 2, 1), out_weight.reshape(1, ROWS, COLS)])
    shard_up, shard_down = (w.reshape(4, ROWS, COLS) for w in (up_weight, down_weight))
    own = lax.div(lax.axis_index("dp"), outer)
    n_up, n_qv = up_bias.size, qv_bias.size
    part = jnp.arange(COLS) // up_bias.shape[1]
    up_rows = jnp.where(part == own, jnp.tile(up_bias, (1, 8)), 0)
    qv_rows = jnp.where(part[:64] == own % 4, jnp.tile(qv_bias, (1, 4)), 0).reshape(2, COLS)
    none = jnp.zeros_like(qv_rows)
    q_rows, v_rows = jnp.where(own < 4, qv_rows, none), jnp.where(own < 4, none, qv_rows)
    small = jnp.concatenate([up_rows, q_rows, v_rows, none, none]).reshape(1, 16, COLS)
    row_ids = z * rows + jnp.arange(rows, dtype=jnp.int32)
    owner = (row_ids // seq_len)[:, None] == jnp.arange(seqs, dtype=jnp.int32)[None, :]
    portion = timestep.astype(F32) / TSTEPS
    fraction = jnp.sum(jnp.where(owner, portion[None, :], 0.0), axis=1)
    h_low = (tokens.astype(F32) + fraction[:, None] * time_weight + time_bias).astype(BF)
    vecs = jnp.stack(
        [time_weight, time_bias, out_bias, gain_one, shift_one, down_bias, gain_two, shift_two]
    )
    (
        w_one, w_up, w_down, _, h_win, queries, keys, values, attn, y_low, hidden, slope, xhat, grad_z2,
        grad_f, layer_out, lse, rstd, sums,
    ) = forward_pass(
        outer, context, timestep, shard_one, shard_up, shard_down, small, h_low, tokens, cotangent, vecs,
    )
    grad_down, grad_up, grad_out_w, grad_qkv, totals, grad_tokens = backward_pass(
        outer, context, timestep, w_one, w_up, w_down, h_win, queries, keys,
        values, attn, y_low, hidden, slope, xhat, grad_z2, grad_f, lse, rstd, vecs, sums,
    )
    weight_grads = [
        grad_qkv, grad_out_w, grad_up.reshape(4 * ROWS, COLS), grad_down.reshape(4 * ROWS, COLS)
    ]
    if outer > 1:
        weight_grads = [
            lax.psum_scatter(g, "dp", scatter_dimension=1, tiled=True, axis_index_groups=groups)
            for g in weight_grads
        ]
        totals = lax.psum(totals, "dp", axis_index_groups=groups)
    grad_qkv, grad_out_w, grad_up, grad_down = weight_grads
    dp = lax.axis_index("dp")
    size = lax.axis_size("dp")
    spread = model // (4 * size)
    vectors = lax.dynamic_slice(totals, (0, (dp * 4 + z) * spread), (8, spread))
    grad_up_bias = lax.dynamic_slice(totals, (8, z * ROWS), (4, ROWS)).reshape(8, COLS)
    grad_up_bias = lax.dynamic_slice(grad_up_bias, (0, dp * (COLS // size)), (8, COLS // size))
    grad_qv_bias = totals[12:14].reshape(2, 16, 64).transpose(1, 0, 2).reshape(16, 2 * 64)
    grad_qv_bias = lax.dynamic_slice(grad_qv_bias, (z * 4, dp * (COLS // size)), (4, COLS // size))
    return (
        layer_out, grad_tokens, vectors[0], vectors[1], grad_qkv, grad_qv_bias,
        grad_out_w, vectors[2], vectors[3], vectors[4], grad_up, grad_up_bias,
        grad_down, vectors[5], vectors[6], vectors[7],
    )


def solution(mesh):
    outer = mesh.shape["dp"] // 8
    placed = (
        P(("dp", "mp"), None), P("dp"), P("dp"), P(), P(), P(None, "dp", "mp"), P("mp", "dp"), P("mp", "dp"),
        P(), P(), P(), P("mp", "dp"), P("mp", "dp"), P("mp", "dp"), P(), P(), P(), P(("dp", "mp"), None),
    )
    spread = P(("dp", "mp"))
    wide = P("mp", "dp")
    return jax.shard_map(
        functools.partial(body, outer),
        mesh=mesh,
        in_specs=placed,
        out_specs=(
            P(("dp", "mp"), None), P(("dp", "mp"), None), spread, spread, P(None, "dp", "mp"), wide, wide,
            spread, spread, spread, wide, wide, wide, spread, spread, spread,
        ),
        check_vma=False,
    )
```
